32 devices in a mesh: dp: 16 (over z, x, core), branch: 2 (over y).
Axes of the slice: x: 2, y: 2, z: 4, core: 2. Of those that a mesh axis runs over, the one named last changes fastest.
Arguments:
- tokens: bfloat16 [32768, 768], P('dp'), may hold values from -6 to 6
- lengths: int32 [64], P('dp'), may hold values from 40 to 512, as said below
- w_query: bfloat16 [768, 384], replicated, may hold values from -0.21875 to 0.21875
- branch_proj: bfloat16 [2, 2, 768, 384], P('branch'), may hold values from -0.21875 to 0.21875
- depth_kernel: bfloat16 [9, 768], replicated, may hold values from -2 to 2
- kernel_gen: bfloat16 [384, 54], replicated, may hold values from -0.3125 to 0.3125
- w_out: bfloat16 [768, 768], replicated, may hold values from -0.875 to 0.875
- gain_one: float32 [768], replicated, may hold values from 0.5 to 1.5
- bias_one: float32 [768], replicated, may hold values from -1.5 to 1.5
- w_inner: bfloat16 [2, 384, 1536], P(None, None, ('dp', 'branch')), may hold values from -0.3125 to 0.3125
- w_outer: bfloat16 [2, 384, 1536], P(None, None, ('dp', 'branch')), may hold values from -0.15625 to 0.15625
- gain_two: float32 [768], replicated, may hold values from 0.5 to 1.5
- bias_two: float32 [768], replicated, may hold values from -1.5 to 1.5
- cotangent: bfloat16 [32768, 768], P(('dp', 'branch')), may hold values from -6 to 6
Outputs:
- layer_out: bfloat16 [32768, 768], P(('dp', 'branch'))
- input_grad: float32 [32768, 768], P(('dp', 'branch'))
- query_grad: float32 [768, 384], replicated
- branch_grad: float32 [2, 2, 768, 384], P('branch')
- depth_grad: float32 [9, 768], replicated
- kernel_gen_grad: float32 [384, 54], replicated
- out_weight_grad: float32 [768, 768], replicated
- gain_one_grad: float32 [768], replicated
- bias_one_grad: float32 [768], replicated
- inner_grad: float32 [2, 384, 1536], P(None, None, ('dp', 'branch'))
- outer_grad: float32 [2, 384, 1536], P(None, None, ('dp', 'branch'))
- gain_two_grad: float32 [768], replicated
- bias_two_grad: float32 [768], replicated
The draws below stay inside these ranges and needn't reach their ends.
Inputs may be any that keep to these rules, and one draw needn't show every extreme that they name: Row r holds lengths[r] real tokens at its first slots and padding after them; in every draw some row is completely real (512 tokens).
All inputs are finite; a program needn't handle non-finite values.
Results may differ from the reference program's by a relative error of at most 0.02.
Values may be sent and summed in bfloat16 or wider, within the bound.
No kernel may reach another device: no remote copies, remote signals or barrier semaphores. Data moves between devices by JAX's collectives and lax.ppermute only.
A program may use at most 256 MiB of HBM per device.

```python
import math
import jax
import jax.numpy as jnp
from jax import lax

D = 768
HEADS = 6
HSIZE = 64
KERN = 9
FF = 3072
GROUPS = 2
SEQ = 512
MIN_LEN = 40
HB = 384
ROWS = 64
TOKENS = 32768


def draw_lengths(key, part):
    first_key, second_key = jax.random.split(jax.random.fold_in(key, 17))
    drawn = jax.random.randint(first_key, (ROWS,), MIN_LEN, SEQ + 1)
    full_row = jax.random.randint(second_key, (), 0, ROWS)
    places = jnp.arange(ROWS)
    return jnp.where(places == full_row, SEQ, drawn).astype(jnp.int32)


def levels(own_key, extent, cuts, low, largest):
    def one(dim, parts):
        draws = jax.random.uniform(jax.random.fold_in(jax.random.fold_in(own_key, 6), dim), (parts,), jnp.float32, low / len(cuts), largest / len(cuts))
        return jnp.repeat(jnp.exp(draws), extent[dim] // parts).reshape((-1,) + (1,) * (len(extent) - dim - 1))

    level = one(*cuts[0])
    for cut in cuts[1:]:
        level = level * one(*cut)
    return level


def normal_values(own_key, shape, width, limit, shards=(), dtype=jnp.bfloat16):
    values = jax.random.normal(own_key, shape, jnp.float32) * width
    if len(shards) > 0:
        values = levels(own_key, shape, shards, -0.22, 0.18) * values
    return jnp.clip(values, min=-limit, max=limit).astype(dtype)


def setup_inputs(seed: int = 0) -> dict:
    key_of = jax.random.split(jax.random.key(seed), 15)
    tokens = normal_values(key_of[0], (TOKENS, D), 1.0, 6.0, ((0, 16),))
    lengths = draw_lengths(jax.random.fold_in(key_of[14], 71), 0)
    w_query = normal_values(key_of[2], (D, HB), D ** -0.5, 0.21875)
    branch_proj = normal_values(key_of[3], (2, 2, D, HB), D ** -0.5, 0.21875, ((0, 2),))
    depth_kernel = normal_values(key_of[4], (KERN, D), KERN ** -0.5, 2.0)
    kernel_gen = normal_values(key_of[5], (HB, HEADS * KERN), HB ** -0.5, 0.3125)
    w_out = normal_values(key_of[6], (D, D), (D // 16) ** -0.5, 0.875)
    gain_one = jnp.clip(1.0 + 0.1 * jax.random.normal(key_of[7], (D,), jnp.float32), 0.5, 1.5)
    bias_one = normal_values(key_of[8], (D,), 0.3, 1.5, (), jnp.float32)
    w_inner = normal_values(key_of[9], (GROUPS, D // GROUPS, FF // GROUPS), (D // GROUPS) ** -0.5, 0.3125, ((2, 32),))
    w_outer = normal_values(key_of[10], (GROUPS, D // GROUPS, FF // GROUPS), (FF // GROUPS) ** -0.5, 0.15625, ((2, 32),))
    gain_two = jnp.clip(1.0 + 0.1 * jax.random.normal(key_of[11], (D,), jnp.float32), 0.5, 1.5)
    bias_two = normal_values(key_of[12], (D,), 0.3, 1.5, (), jnp.float32)
    cotangent = normal_values(key_of[13], (TOKENS, D), 1.0, 6.0, ((0, 32),))
    return {"tokens": tokens, "lengths": lengths, "w_query": w_query, "branch_proj": branch_proj, "depth_kernel": depth_kernel, "kernel_gen": kernel_gen, "w_out": w_out, "gain_one": gain_one, "bias_one": bias_one, "w_inner": w_inner, "w_outer": w_outer, "gain_two": gain_two, "bias_two": bias_two, "cotangent": cotangent}


EPS = 1e-12
MASKED = -1000000000.0
HIGH = lax.Precision.HIGHEST

@jax.custom_vjp
def low(v):
    return lax.optimization_barrier(v.astype(jnp.bfloat16)).astype(jnp.float32)

@jax.custom_vjp
def low_back(v):
    return v

def low_keep(v):
    return (low(v), None)

def low_pass(kept, grad):
    return (grad,)

def back_keep(v):
    return (v, None)

def back_low(kept, grad):
    return (low(grad),)
low.defvjp(low_keep, low_pass)
low_back.defvjp(back_keep, back_low)

def layer_norm(field, gain_vec, bias_vec):
    centre = lax.optimization_barrier(jnp.mean(field, -1, keepdims=True))
    centred = field - centre
    spread_sq = lax.optimization_barrier(jnp.mean(centred * centred, -1, keepdims=True))
    return centred * lax.rsqrt(spread_sq + EPS) * gain_vec + bias_vec

def gelu_exact(field):
    return jax.nn.gelu(field, approximate=False)

def depthwise(field, kernel):
    taps = kernel.shape[0]
    margin = (taps - 1) // 2
    length = field.shape[1]
    padded = jnp.pad(field, ((0, 0), (margin, margin), (0, 0)))
    summed = jnp.zeros_like(field)
    for offset in range(taps):
        summed = summed + kernel[offset] * padded[:, offset:offset + length]
    return summed

def mix_window(row_count, logits, values):
    tok_count = logits.shape[0]
    length = tok_count // row_count
    kern_w = logits.reshape(row_count, length, HEADS, KERN)
    kern_w = jnp.exp(kern_w - lax.optimization_barrier(jnp.max(kern_w, -1, keepdims=True)))
    kern_w = kern_w / lax.optimization_barrier(jnp.sum(kern_w, -1, keepdims=True))
    margin = (KERN - 1) // 2
    grid = values.reshape(row_count, length, HEADS, HSIZE)
    padded = jnp.pad(grid, ((0, 0), (margin, margin), (0, 0), (0, 0)))
    summed = jnp.zeros_like(grid)
    for offset in range(KERN):
        summed = summed + kern_w[..., offset:offset + 1] * padded[:, offset:offset + length]
    return summed.reshape(tok_count, HEADS * HSIZE)

def attend_row(pieces):
    query_rows, key_rows, value_rows, is_valid = pieces
    scale = 1.0 / math.sqrt(query_rows.shape[-1])
    scores = low_back(jnp.einsum('qhe,khe->hqk', query_rows, key_rows, precision=HIGH) * scale)
    scores = jnp.where(is_valid[None, None, :], scores, MASKED)
    expo = jnp.exp(scores - lax.optimization_barrier(jnp.max(scores, -1, keepdims=True)))
    probs = expo / lax.optimization_barrier(jnp.sum(expo, -1, keepdims=True))
    return jnp.einsum('hqk,khe->qhe', low(probs), value_rows, precision=HIGH)

def matmul(left, right):
    return jnp.dot(left, right, precision=HIGH)

def reference(tokens, lengths, w_query, branch_proj, depth_kernel, kernel_gen, w_out, gain_one, bias_one, w_inner, w_outer, gain_two, bias_two, cotangent):
    row_count = lengths.shape[0]
    tok_count = row_count * SEQ
    positions = lax.broadcasted_iota(jnp.int32, (row_count, SEQ), 1)
    is_valid = positions < lengths.astype(jnp.int32)[:, None]
    tok_mask = is_valid.astype(jnp.float32).reshape(tok_count, 1)

    def forward(tok_f, wq_f, bp_f, dk_f, kg_f, wo_f, g_one, b_one, wi_f, wu_f, g_two, b_two):
        model_width = tok_f.shape[1]
        inputs = tok_f * tok_mask
        query = low_back(low(matmul(inputs, wq_f)))
        key_all = low_back(low(matmul(inputs, bp_f[0, 0])))
        value_all = low_back(low(matmul(inputs, bp_f[0, 1])))
        shape_heads = (row_count, SEQ, HEADS, HSIZE)
        att_out = lax.map(jax.checkpoint(attend_row), (query.reshape(shape_heads), key_all.reshape(shape_heads), value_all.reshape(shape_heads), is_valid))
        att_out = low_back(low(att_out.reshape(tok_count, HEADS * HSIZE)))
        spread = low(depthwise(inputs.reshape(row_count, SEQ, model_width), dk_f).reshape(tok_count, model_width))
        span_key = low_back(matmul(spread, bp_f[1, 0]))
        mixed_key = low(span_key * query)
        logits = low_back(matmul(mixed_key, kg_f))
        conv_value = low_back(low(matmul(inputs, bp_f[1, 1])))
        conv_out = low_back(low(mix_window(row_count, logits, conv_value)))
        mixed = jnp.concatenate([att_out, conv_out], 1)
        pre_one = inputs + low_back(matmul(mixed, wo_f))
        normed = layer_norm(pre_one, g_one, b_one)
        normed_r = low(normed)
        grouped = normed_r.reshape(tok_count, GROUPS, model_width // GROUPS)
        inner_pre = low_back(jnp.einsum('tgi,gif->tgf', grouped, wi_f, precision=HIGH))
        activ = low(gelu_exact(inner_pre))
        ffn_out = low_back(jnp.einsum('tgf,gof->tgo', activ, wu_f, precision=HIGH).reshape(tok_count, model_width))
        final = layer_norm(normed + ffn_out, g_two, b_two)
        return final * tok_mask
    floats = (tokens.astype(jnp.float32), w_query.astype(jnp.float32), branch_proj.astype(jnp.float32), depth_kernel.astype(jnp.float32), kernel_gen.astype(jnp.float32), w_out.astype(jnp.float32), gain_one.astype(jnp.float32), bias_one.astype(jnp.float32), w_inner.astype(jnp.float32), w_outer.astype(jnp.float32), gain_two.astype(jnp.float32), bias_two.astype(jnp.float32))
    result, backward = jax.vjp(forward, *floats)
    grads = backward(cotangent.astype(jnp.float32))
    return (result.astype(jnp.bfloat16), grads[0], grads[1], grads[2], grads[3], grads[4], grads[5], grads[6], grads[7], grads[8], grads[9], grads[10], grads[11])
```

```python
from functools import partial
import math

import jax
import jax.numpy as jnp
from jax import lax
from jax.sharding import PartitionSpec as P

HEADS = 6
HSIZE = 64
KERN = 9
EPS = 1e-12
MASKED = -1000000000.0
AXES = ("dp", "branch")
BF = jnp.bfloat16
F32 = jnp.float32


class Links:
    def __init__(self, mesh):
        self.dp = mesh.shape["dp"]
        self.count = self.dp * 2
        bits = self.count.bit_length() - 1
        assert mesh.shape["branch"] == 2 and self.count == 1 << bits and bits >= 3
        self.far = [list(range(low, min(low + 2, bits))) for low in range(3, bits, 2)]

    def send(self, value, partner):
        return lax.ppermute(value, AXES, [(d, partner(d)) for d in range(self.count)])

    def core(self, value):
        return self.send(value, lambda d: d ^ 2)

    def first(self, value):
        return self.send(value, lambda d: d ^ 1 if d & 2 else d ^ 4)

    def second(self, value):
        return self.send(value, lambda d: d ^ 4 if d & 2 else d ^ 1)

    def masks(self, group):
        return [i << group[0] for i in range(1, 1 << len(group))]

    def far_send(self, value, mask):
        return self.send(value, lambda d: d ^ mask)

    def place(self):
        me = lax.axis_index("dp") * 2 + lax.axis_index("branch")
        core = (me >> 1) & 1
        branch = me & 1
        side = (me >> 2) & 1
        return me, core, jnp.where(core == 1, branch, side), jnp.where(core == 1, side, branch)

    def gather_slots(self, piece, axis):
        for group in reversed(self.far):
            piece = jnp.concatenate(
                [piece] + [self.far_send(piece, m) for m in self.masks(group)], axis
            )
        for step in (self.second, self.first, self.core):
            piece = jnp.concatenate([piece, step(piece)], axis)
        return piece

    def scatter_slots(self, total, axis):
        for step in (self.core, self.first, self.second):
            keep, give = jnp.split(total, 2, axis)
            total = keep + step(give.astype(BF)).astype(F32)
        for group in self.far:
            masks = self.masks(group)
            parts = jnp.split(total, len(masks) + 1, axis)
            total = parts[0]
            for mask, part in zip(masks, parts[1:]):
                total = total + self.far_send(part.astype(BF), mask).astype(F32)
        return total

    def scatter_far(self, total):
        me = self.place()[0]
        for group in self.far:
            masks = self.masks(group)
            count = len(masks) + 1
            own = (me >> group[0]) & (count - 1)
            parts = total.reshape((count, -1) + total.shape[1:])
            total = lax.dynamic_index_in_dim(parts, own, 0, False)
            for i, mask in enumerate(masks):
                part = lax.dynamic_index_in_dim(parts, own ^ (i + 1), 0, False)
                total = total + self.far_send(part.astype(BF), mask).astype(F32)
        return total

    def gather_far(self, piece):
        me = self.place()[0]
        for group in reversed(self.far):
            masks = self.masks(group)
            own = (me >> group[0]) & len(masks)
            parts = jnp.stack([piece] + [self.far_send(piece, m) for m in masks])
            piece = jnp.concatenate(
                [lax.dynamic_index_in_dim(parts, own ^ i, 0, False) for i in range(len(masks) + 1)]
            )
        return piece

    @staticmethod
    def halve(total, own, step):
        parts = total.reshape((2, -1) + total.shape[1:])
        keep = lax.dynamic_index_in_dim(parts, own, 0, False)
        give = lax.dynamic_index_in_dim(parts, 1 - own, 0, False)
        return keep + step(give.astype(BF)).astype(F32)

    @staticmethod
    def double(piece, own, step):
        other = step(piece)
        return jnp.where(
            own == 0, jnp.concatenate([piece, other]), jnp.concatenate([other, piece])
        )

    def sum_all(self, total):
        _, core, one, two = self.place()
        total = self.halve(total, core, self.core)
        total = self.halve(total, one, self.first)
        total = self.halve(total, two, self.second)
        piece = self.gather_far(self.scatter_far(total).astype(BF))
        piece = self.double(piece, two, self.second)
        piece = self.double(piece, one, self.first)
        return self.double(piece, core, self.core).astype(F32)

    def sum_branch(self, total):
        _, core, one, two = self.place()
        rows, width = total.shape[1:]
        side = (self.place()[0] >> 2) & 1
        grid = total.reshape(2, 2, 2, rows // 4, width)
        keep = lax.dynamic_index_in_dim(grid, core, 1, False)
        give = lax.dynamic_index_in_dim(grid, 1 - core, 1, False)
        part = keep + self.core(give.astype(BF)).astype(F32)
        part = jnp.where(core == 0, jnp.swapaxes(part, 0, 1), part)
        part = self.halve(part.reshape(4, rows // 4, width), one, self.first)
        part = self.halve(part, two, self.second)
        piece = self.gather_far(self.scatter_far(part.reshape(-1, width)).astype(BF))
        piece = self.double(piece, side, lambda v: self.far_send(v, 4))
        return self.double(piece, core, self.core).astype(F32)


def layer_norm(field, gain_vec, bias_vec):
    centre = jnp.mean(field, -1, keepdims=True)
    centred = field - centre
    spread_sq = jnp.mean(centred * centred, -1, keepdims=True)
    return centred * lax.rsqrt(spread_sq + EPS) * gain_vec + bias_vec


def gelu_exact(field):
    return jax.nn.gelu(field, approximate=False)


def depthwise(field, kernel):
    taps = kernel.shape[0]
    margin = (taps - 1) // 2
    length = field.shape[1]
    padded = jnp.pad(field, ((0, 0), (margin, margin), (0, 0)))
    summed = jnp.zeros_like(field)
    for offset in range(taps):
        summed = summed + kernel[offset] * padded[:, offset : offset + length]
    return summed


def mix_window(row_count, logits, values):
    tok_count = logits.shape[0]
    length = tok_count // row_count
    kern_w = logits.reshape(row_count, length, HEADS, KERN)
    kern_w = jnp.exp(kern_w - jnp.max(kern_w, -1, keepdims=True))
    kern_w = kern_w / jnp.sum(kern_w, -1, keepdims=True)
    margin = (KERN - 1) // 2
    grid = values.reshape(row_count, length, HEADS, HSIZE)
    padded = jnp.pad(grid, ((0, 0), (margin, margin), (0, 0), (0, 0)))
    summed = jnp.zeros_like(grid)
    for offset in range(KERN):
        summed = summed + kern_w[..., offset : offset + 1] * padded[:, offset : offset + length]
    return summed.reshape(tok_count, HEADS * HSIZE)


def dot(left, right):
    return jnp.dot(left, right, preferred_element_type=F32)


def over_rows(left, right):
    return lax.dot_general(left, right, (((0,), (0,)), ((), ())), preferred_element_type=F32)


def by_transpose(left, right):
    return lax.dot_general(left, right, (((1,), (1,)), ((), ())), preferred_element_type=F32)


def row_scores(query_rows, key_rows, is_valid):
    scale = 1.0 / math.sqrt(query_rows.shape[-1])
    scores = (
        jnp.einsum("qhe,khe->hqk", query_rows, key_rows, preferred_element_type=F32) * scale
    )
    return jnp.where(is_valid[None, None, :], scores, MASKED)


def attend_row(query_rows, key_rows, value_rows, valid_row):
    scores = row_scores(query_rows, key_rows, valid_row)
    top_score = jnp.max(scores, -1, keepdims=True)
    expo = jnp.exp(scores - top_score)
    row_total = jnp.sum(expo, -1, keepdims=True)
    probs = (expo / row_total).astype(BF)
    result = jnp.einsum("hqk,khe->qhe", probs, value_rows, preferred_element_type=F32)
    return result.astype(BF), (top_score + jnp.log(row_total))[..., 0]


def attend_row_back(query_rows, key_rows, value_rows, valid_row, lse_row, grad_rows):
    scale = 1.0 / math.sqrt(query_rows.shape[-1])
    scores = row_scores(query_rows, key_rows, valid_row)
    probs = jnp.exp(scores - lse_row[..., None])
    grad_probs = jnp.einsum("qhe,khe->hqk", grad_rows, value_rows, preferred_element_type=F32)
    grad_scores = (
        probs * (grad_probs - jnp.sum(probs * grad_probs, -1, keepdims=True))
    ).astype(BF)
    grad_query = (
        jnp.einsum("hqk,khe->qhe", grad_scores, key_rows, preferred_element_type=F32) * scale
    )
    grad_key = (
        jnp.einsum("hqk,qhe->khe", grad_scores, query_rows, preferred_element_type=F32) * scale
    )
    grad_value = jnp.einsum(
        "hqk,qhe->khe", probs.astype(BF), grad_rows, preferred_element_type=F32
    )
    return grad_query, grad_key.astype(BF), grad_value.astype(BF)


def per_device(
    links,
    tokens,
    lengths,
    w_query,
    branch_proj,
    depth_kernel,
    kernel_gen,
    w_out,
    gain_one,
    bias_one,
    w_inner,
    w_outer,
    gain_two,
    bias_two,
    cotangent,
):
    me, core_bit, _, _ = links.place()
    side = lax.axis_index("branch")
    row_count = lengths.shape[0] // 2
    seq_len = tokens.shape[0] // lengths.shape[0]
    tok_count = row_count * seq_len
    width = tokens.shape[1]
    half = w_query.shape[1]
    groups = w_inner.shape[0]

    own_w = branch_proj[0]
    far_w = links.send(
        lax.dynamic_index_in_dim(own_w, core_bit, 0, False), lambda d: d ^ 1
    )
    next_w = links.core(far_w)
    other_w = jnp.where(core_bit == 0, jnp.stack([far_w, next_w]), jnp.stack([next_w, far_w]))
    att_w = jnp.where(side == 0, own_w, other_w)
    conv_w = jnp.where(side == 0, other_w, own_w)

    piece = jnp.stack([w_inner, w_outer]).swapaxes(2, 3)
    all_w = links.gather_slots(piece, 2)
    inner_w, outer_w = all_w[0], all_w[1]

    my_tokens = lax.dynamic_slice_in_dim(tokens, side * tok_count, tok_count, 0)
    my_lengths = lax.dynamic_slice_in_dim(lengths, side * row_count, row_count, 0)
    is_valid = lax.broadcasted_iota(jnp.int32, (row_count, seq_len), 1) < my_lengths[:, None]
    tok_mask = is_valid.astype(F32).reshape(tok_count, 1)
    x_in = my_tokens * tok_mask.astype(BF)
    x_f = x_in.astype(F32)
    depth_f = depth_kernel.astype(F32)
    x_grid = x_f.reshape(row_count, seq_len, width)
    heads = (seq_len, HEADS, HSIZE)
    window_mix = partial(mix_window, row_count)

    query = dot(x_in, w_query).astype(BF)
    query_f = query.astype(F32)
    key = dot(x_in, att_w[0]).astype(BF)
    value = dot(x_in, att_w[1]).astype(BF)

    def row_of(field, r):
        return field[r * seq_len : (r + 1) * seq_len].reshape(heads)

    att_rows = [
        attend_row(row_of(query, r), row_of(key, r), row_of(value, r), is_valid[r])
        for r in range(row_count)
    ]
    att_out = jnp.concatenate([a.reshape(seq_len, half) for a, _ in att_rows])
    spread = depthwise(x_grid, depth_f).reshape(tok_count, width).astype(BF)
    span_key = dot(spread, conv_w[0])
    mixed_key = (span_key * query_f).astype(BF)
    logits = dot(mixed_key, kernel_gen)
    conv_value = dot(x_in, conv_w[1]).astype(BF)
    conv_value_f = conv_value.astype(F32)
    conv_out = window_mix(logits, conv_value_f).astype(BF)
    mixed = jnp.concatenate([att_out, conv_out], 1)

    pre_one = x_f + dot(mixed, w_out)
    normed, norm_one_back = jax.vjp(layer_norm, pre_one, gain_one, bias_one)
    normed_r = normed.astype(BF)
    grouped_in = normed_r.reshape(tok_count, groups, width // groups)
    inner_pre = jnp.einsum("tgi,gfi->tgf", grouped_in, inner_w, preferred_element_type=F32)
    activ, gelu_back = jax.vjp(gelu_exact, inner_pre)
    activ_r = activ.astype(BF)
    ffn = jnp.einsum("tgf,gfo->tgo", activ_r, outer_w, preferred_element_type=F32)
    final, norm_two_back = jax.vjp(
        layer_norm, normed + ffn.reshape(tok_count, width), gain_two, bias_two
    )
    layer_out = (final * tok_mask).astype(BF)
    grad_final = cotangent.astype(F32) * tok_mask
    grad_pre_two, grad_gain_two, grad_bias_two = norm_two_back(grad_final)
    grad_ffn = grad_pre_two.astype(BF).reshape(tok_count, groups, width // groups)
    grad_outer = jnp.einsum("tgf,tgo->gfo", activ_r, grad_ffn, preferred_element_type=F32)
    grad_activ = jnp.einsum("tgo,gfo->tgf", grad_ffn, outer_w, preferred_element_type=F32)
    grad_pre = gelu_back(grad_activ)[0].astype(BF)
    grad_inner = jnp.einsum("tgf,tgi->gfi", grad_pre, grouped_in, preferred_element_type=F32)
    grad_in = jnp.einsum("tgf,gfi->tgi", grad_pre, inner_w, preferred_element_type=F32)
    ffn_grads = links.scatter_slots(jnp.stack([grad_inner, grad_outer]), 2).swapaxes(2, 3)
    grad_pre_one, grad_gain_one, grad_bias_one = norm_one_back(
        grad_pre_two + grad_in.reshape(tok_count, width)
    )
    grad_mix = grad_pre_one.astype(BF)
    grad_w_out = over_rows(mixed, grad_mix)
    out_sum = links.sum_all(grad_w_out.reshape(-1, half)).reshape(grad_w_out.shape)
    grad_mixed = by_transpose(grad_mix, w_out).astype(BF)
    grad_att, grad_conv = grad_mixed[:, :half], grad_mixed[:, half:]

    _, window_back = jax.vjp(window_mix, logits, conv_value_f)
    grad_logits, grad_cv = window_back(grad_conv.astype(F32))
    grad_logits = grad_logits.astype(BF)
    grad_cv = grad_cv.astype(BF)
    grad_gen = over_rows(mixed_key, grad_logits)
    grad_key_mix = by_transpose(grad_logits, kernel_gen)
    grad_span = (grad_key_mix * query_f).astype(BF)
    q_conv = grad_key_mix * span_key
    grad_span_w = over_rows(spread, grad_span)
    grad_spread = by_transpose(grad_span, conv_w[0])
    _, depth_back = jax.vjp(depthwise, x_grid, depth_f)
    grad_field, grad_depth = depth_back(grad_spread.reshape(row_count, seq_len, width))
    grad_cv_w = over_rows(x_in, grad_cv)
    x_conv = grad_field.reshape(tok_count, width) + by_transpose(grad_cv, conv_w[1])

    back_rows = [
        attend_row_back(
            row_of(query, r),
            row_of(key, r),
            row_of(value, r),
            is_valid[r],
            att_rows[r][1],
            row_of(grad_att, r),
        )
        for r in range(row_count)
    ]
    q_att, grad_key, grad_value = (
        jnp.concatenate([b[i].reshape(seq_len, half) for b in back_rows]) for i in range(3)
    )
    grad_key_w = over_rows(x_in, grad_key)
    grad_value_w = over_rows(x_in, grad_value)
    x_att = by_transpose(grad_key, att_w[0]) + by_transpose(grad_value, att_w[1])
    grad_q = (q_att + q_conv).astype(BF)
    grad_w_query = over_rows(x_in, grad_q)
    input_grad = tok_mask * (grad_pre_one + x_att + x_conv + by_transpose(grad_q, w_query))

    branch_sum = links.sum_branch(
        jnp.stack(
            [
                jnp.concatenate([grad_key_w, grad_value_w]),
                jnp.concatenate([grad_span_w, grad_cv_w]),
            ]
        )
    ).reshape(branch_proj.shape)
    small = [grad_gain_one, grad_bias_one, grad_gain_two, grad_bias_two, grad_depth, grad_gen]
    flat = [grad_w_query.reshape(-1)] + [s.reshape(-1) for s in small]
    unit = links.count * 16 * half
    size = sum(f.size for f in flat)
    flat.append(jnp.zeros((-size) % unit, F32))
    shared = links.sum_all(jnp.concatenate(flat).reshape(-1, half)).reshape(-1)
    outs = []
    start = 0
    for s in [grad_w_query] + small:
        outs.append(shared[start : start + s.size].reshape(s.shape))
        start += s.size
    return (
        layer_out,
        input_grad,
        outs[0],
        branch_sum,
        outs[5],
        outs[6],
        out_sum,
        outs[1],
        outs[2],
        ffn_grads[0],
        ffn_grads[1],
        outs[3],
        outs[4],
    )


def solution(mesh):
    rows = P(AXES, None)
    hidden = P(None, None, AXES)
    weights = P("branch", None, None, None)
    return jax.shard_map(
        partial(per_device, Links(mesh)),
        mesh=mesh,
        in_specs=(
            P("dp", None), P("dp"), P(), weights, P(), P(), P(), P(), P(), hidden, hidden,
            P(), P(), rows,
        ),
        out_specs=(
            rows, rows, P(), weights, P(), P(), P(), P(), P(), hidden, hidden, P(), P(),
        ),
        check_vma=False,
    )
```

```python
from functools import partial

import jax
import jax.numpy as jnp
import ml_dtypes
import numpy as np
from jax import lax
from jax.experimental import pallas as pl
from jax.experimental.pallas import tpu as pltpu
from jax.sharding import PartitionSpec as P

HEADS = 6
HSIZE = 64
KERN = 9
EPS = 1e-12
MASKED = -1000000000.0
SCALE = 0.125
LANE = 128
TILES = HEADS * HSIZE // LANE
PAD = 8
CHUNK = 128
BLOCK = 256
ROOM = 58 << 20
AXES = ("dp", "branch")
BF = jnp.bfloat16
F32 = jnp.float32


class Links:
    def __init__(self, mesh):
        self.dp = mesh.shape["dp"]
        self.count = self.dp * 2
        bits = self.count.bit_length() - 1
        assert mesh.shape["branch"] == 2 and self.count == 1 << bits and bits >= 3
        self.far = [list(range(low, min(low + 2, bits))) for low in range(3, bits, 2)]

    def send(self, value, partner):
        return lax.ppermute(value, AXES, [(d, partner(d)) for d in range(self.count)])

    def core(self, value):
        return self.send(value, lambda d: d ^ 2)

    def first(self, value):
        return self.send(value, lambda d: d ^ 1 if d & 2 else d ^ 4)

    def second(self, value):
        return self.send(value, lambda d: d ^ 4 if d & 2 else d ^ 1)

    def masks(self, group):
        return [i << group[0] for i in range(1, 1 << len(group))]

    def far_send(self, value, mask):
        return self.send(value, lambda d: d ^ mask)

    def place(self):
        me = lax.axis_index("dp") * 2 + lax.axis_index("branch")
        core = (me >> 1) & 1
        branch = me & 1
        side = (me >> 2) & 1
        return me, core, jnp.where(core == 1, branch, side), jnp.where(core == 1, side, branch)

    def gather_slots(self, piece, axis):
        for group in reversed(self.far):
            piece = jnp.concatenate(
                [piece] + [self.far_send(piece, m) for m in self.masks(group)], axis
            )
        for step in (self.second, self.first, self.core):
            piece = jnp.concatenate([piece, step(piece)], axis)
        return piece

    def scatter_slots(self, keep, give, axis):
        total = keep + self.core(give).astype(F32)
        for step in (self.first, self.second):
            keep, give = jnp.split(total, 2, axis)
            total = keep + step(give.astype(BF)).astype(F32)
        for group in self.far:
            masks = self.masks(group)
            parts = jnp.split(total, len(masks) + 1, axis)
            total = parts[0]
            for mask, part in zip(masks, parts[1:]):
                total = total + self.far_send(part.astype(BF), mask).astype(F32)
        return total

    def scatter_far(self, total):
        me = self.place()[0]
        for group in self.far:
            masks = self.masks(group)
            count = len(masks) + 1
            own = (me >> group[0]) & (count - 1)
            parts = total.reshape((count, -1) + total.shape[1:])
            total = lax.dynamic_index_in_dim(parts, own, 0, False)
            for i, mask in enumerate(masks):
                part = lax.dynamic_index_in_dim(parts, own ^ (i + 1), 0, False)
                total = total + self.far_send(part.astype(BF), mask).astype(F32)
        return total

    def gather_far(self, piece):
        me = self.place()[0]
        for group in reversed(self.far):
            masks = self.masks(group)
            own = (me >> group[0]) & len(masks)
            parts = jnp.stack([piece] + [self.far_send(piece, m) for m in masks])
            piece = jnp.concatenate(
                [lax.dynamic_index_in_dim(parts, own ^ i, 0, False) for i in range(len(masks) + 1)]
            )
        return piece

    @staticmethod
    def halve(total, own, step):
        parts = total.reshape((2, -1) + total.shape[1:])
        keep = lax.dynamic_index_in_dim(parts, own, 0, False)
        give = lax.dynamic_index_in_dim(parts, 1 - own, 0, False)
        return keep + step(give.astype(BF)).astype(F32)

    @staticmethod
    def double(piece, own, step):
        other = step(piece)
        return jnp.where(
            own == 0, jnp.concatenate([piece, other]), jnp.concatenate([other, piece])
        )

    def sum_all(self, total):
        _, core, one, two = self.place()
        total = self.halve(total, core, self.core)
        total = self.halve(total, one, self.first)
        total = self.halve(total, two, self.second)
        piece = self.gather_far(self.scatter_far(total).astype(BF))
        piece = self.double(piece, two, self.second)
        piece = self.double(piece, one, self.first)
        return self.double(piece, core, self.core).astype(F32)

    def sum_branch(self, total):
        _, core, one, two = self.place()
        rows, width = total.shape[1:]
        side = (self.place()[0] >> 2) & 1
        grid = total.reshape(2, 2, 2, rows // 4, width)
        keep = lax.dynamic_index_in_dim(grid, core, 1, False)
        give = lax.dynamic_index_in_dim(grid, 1 - core, 1, False)
        part = keep + self.core(give.astype(BF)).astype(F32)
        part = jnp.where(core == 0, jnp.swapaxes(part, 0, 1), part)
        part = self.halve(part.reshape(4, rows // 4, width), one, self.first)
        part = self.halve(part, two, self.second)
        piece = self.gather_far(self.scatter_far(part.reshape(-1, width)).astype(BF))
        piece = self.double(piece, side, lambda v: self.far_send(v, 4))
        return self.double(piece, core, self.core).astype(F32)


def dot(left, right):
    return jnp.dot(left, right, preferred_element_type=F32)


def over_rows(left, right):
    return lax.dot_general(left, right, (((0,), (0,)), ((), ())), preferred_element_type=F32)


def by_transpose(left, right):
    return lax.dot_general(left, right, (((1,), (1,)), ((), ())), preferred_element_type=F32)


def lanes(index):
    return slice(index * LANE, (index + 1) * LANE)


def tap_columns():
    source = np.arange(2 * LANE) % LANE
    column = np.arange(TILES * KERN * LANE)
    tile, tap, lane = column // (KERN * LANE), column // LANE % KERN, column % LANE
    head = tile * 2 + lane // HSIZE
    return (source[:, None] == tap * 8 + head).astype(ml_dtypes.bfloat16)


def over_taps(field, combine):
    for shift in (64, 32, 16, 8):
        field = combine(field, pltpu.roll(field, shift, 1))
    return field


def two_parts(field):
    high = field.astype(BF)
    return high, (field - high.astype(F32)).astype(BF)


def head_only(field, head):
    lane = lax.broadcasted_iota(jnp.int32, field.shape, 1)
    return jnp.where((lane < HSIZE) == (head == 0), field, jnp.zeros_like(field))


def pick_lane(lane, choices):
    block = jnp.zeros(lane.shape, F32)
    for index, value in choices:
        block = jnp.where(lane == index, value, block)
    return block.astype(BF)


def fill_padded(pad_ref, field):
    for tile in range(pad_ref.shape[0]):
        pad_ref[tile, PAD : PAD + field.shape[0], :] = field[:, lanes(tile)]


def clear_edges(pad_ref):
    edge = jnp.zeros((pad_ref.shape[0], PAD, LANE), F32)
    pad_ref[:, :PAD, :] = edge
    pad_ref[:, pad_ref.shape[1] - PAD :, :] = edge


def mix_kernel(
    place_ref, length_ref, tok_ref, wq_ref, wk_ref, wv_ref, ws_ref, wc_ref, depth_ref, gen_ref,
    columns_ref, x_ref, q_ref, k_ref, v_ref, c_ref, spread_ref, span_ref, kern_ref, lse_ref,
    mixed_ref, xpad, cpad,
):
    row = pl.program_id(0)
    seq, width = tok_ref.shape
    half = q_ref.shape[1]
    length = length_ref[place_ref[0] * pl.num_programs(0) + row]

    @pl.when(row == 0)
    def _():
        clear_edges(xpad)
        clear_edges(cpad)

    spot = lax.broadcasted_iota(jnp.int32, (seq, 1), 0)
    x_f = jnp.where(spot < length, tok_ref[...].astype(F32), 0.0)
    x_in = x_f.astype(BF)
    x_ref[...] = x_in
    fill_padded(xpad, x_f)
    q_ref[...] = dot(x_in, wq_ref[...]).astype(BF)
    k_ref[...] = dot(x_in, wk_ref[...]).astype(BF)
    v_ref[...] = dot(x_in, wv_ref[...]).astype(BF)
    c_ref[...] = dot(x_in, wc_ref[...]).astype(BF)
    fill_padded(cpad, c_ref[...].astype(F32))

    for tile in range(width // LANE):
        for start in range(0, seq, CHUNK):
            total = jnp.zeros((CHUNK, LANE), F32)
            for tap in range(KERN):
                begin = PAD - KERN // 2 + tap + start
                total = total + depth_ref[tap : tap + 1, lanes(tile)] * xpad[tile, begin : begin + CHUNK, :]
            spread_ref[start : start + CHUNK, lanes(tile)] = total.astype(BF)

    span = dot(spread_ref[...], ws_ref[...])
    span_ref[...] = span
    mixed_key = (span * q_ref[...].astype(F32)).astype(BF)
    logits = dot(mixed_key, gen_ref[...])
    lane = lax.broadcasted_iota(jnp.int32, (seq, LANE), 1)
    used = (lane < KERN * 8) & (lane % 8 < HEADS)
    logits = jnp.where(used, logits, -1e30)
    expo = jnp.exp(logits - over_taps(logits, jnp.maximum))
    kern = jnp.where(used, expo / over_taps(expo, jnp.add), 0.0)
    kern_ref[...] = kern
    kern_parts = jnp.concatenate(two_parts(kern), 1)
    for tile in range(TILES):
        for start in range(0, seq, BLOCK):
            wide = dot(
                kern_parts[start : start + BLOCK],
                columns_ref[:, tile * KERN * LANE : (tile + 1) * KERN * LANE],
            )
            total = jnp.zeros((BLOCK, LANE), F32)
            for tap in range(KERN):
                begin = PAD - KERN // 2 + tap + start
                total = total + wide[:, lanes(tap)] * cpad[tile, begin : begin + BLOCK, :]
            mixed_ref[start : start + BLOCK, half + tile * LANE : half + (tile + 1) * LANE] = (
                total.astype(BF)
            )

    masked = jnp.where(spot < length, 0.0, MASKED)
    key_side = pick_lane(lane, [(0, masked)])
    query_side = pick_lane(lane, [(0, 1.0)])
    lse = jnp.zeros((seq, LANE), F32)
    for tile in range(TILES):
        query = jnp.concatenate([q_ref[:, lanes(tile)] * SCALE, query_side], 1)
        result = jnp.zeros((seq, LANE), F32)
        for head in range(2):
            key = jnp.concatenate([head_only(k_ref[:, lanes(tile)], head), key_side], 1)
            value = head_only(v_ref[:, lanes(tile)], head)
            scores = by_transpose(query, key)
            top = jnp.max(scores, 1, keepdims=True)
            expo = jnp.exp(scores - top)
            total = jnp.sum(expo, 1, keepdims=True)
            result = result + dot(expo.astype(BF), value) * (1.0 / total)
            lse = jnp.where(lane == tile * 2 + head, top + jnp.log(total), lse)
        mixed_ref[:, lanes(tile)] = result.astype(BF)
    lse_ref[...] = lse


def normalise(field):
    centred = field - jnp.mean(field, -1, keepdims=True)
    inverse = lax.rsqrt(jnp.mean(centred * centred, -1, keepdims=True) + EPS)
    return centred * inverse, inverse


def normalise_back(grad, unit, inverse):
    return inverse * (
        grad - jnp.mean(grad, -1, keepdims=True) - unit * jnp.mean(grad * unit, -1, keepdims=True)
    )


def gelu_and_slope(field):
    bell = jnp.exp(field * field * -0.5)
    step = 1.0 / (1.0 + 0.2316419 * jnp.abs(field))
    norm = 0.3989422804014327
    tail = 1.330274429 * norm
    for coefficient in (-1.821255978, 1.781477937, -0.356563782, 0.319381530):
        tail = tail * step + coefficient * norm
    tail = tail * step * bell
    share = jnp.where(field >= 0.0, 1.0 - tail, tail)
    return field * share, share + field * bell * norm


def feed_kernel(
    place_ref, length_ref, mixed_ref, x_ref, cot_ref, wout_ref, inner_ref, outer_ref, gain1_ref,
    bias1_ref, gain2_ref, bias2_ref, layer_ref, pre_ref, gmixed_ref, keep_ref, give_ref,
    gout_ref, vec_ref, gives, activ, slope, unit_one, normed_s, into, grad_two,
):
    row = pl.program_id(0)
    seq, width = x_ref.shape
    groups, hidden, wide = inner_ref.shape
    part = hidden // 2
    length = length_ref[place_ref[0] * pl.num_programs(0) + row]
    mask = (lax.broadcasted_iota(jnp.int32, (seq, 1), 0) < length).astype(F32)

    @pl.when(row == 0)
    def _():
        keep_ref[...] = jnp.zeros_like(keep_ref)
        gives[...] = jnp.zeros_like(gives)
        gout_ref[...] = jnp.zeros_like(gout_ref)
        vec_ref[...] = jnp.zeros_like(vec_ref)

    unit, inverse_one = normalise(x_ref[...].astype(F32) + dot(mixed_ref[...], wout_ref[...]))
    unit_one[...] = unit
    normed = unit * gain1_ref[...] + bias1_ref[...]
    normed_s[...] = normed
    into[...] = normed.astype(BF)
    sums = []
    for group in range(groups):
        cols = slice(group * wide, (group + 1) * wide)
        total = None
        for piece in range(2):
            rows = slice(piece * part, (piece + 1) * part)
            place = slice(group * hidden + piece * part, group * hidden + (piece + 1) * part)
            value, rise = gelu_and_slope(by_transpose(into[:, cols], inner_ref[group, rows, :]))
            activ[:, place] = value.astype(BF)
            slope[:, place] = rise
            term = dot(activ[:, place], outer_ref[group, rows, :])
            total = term if total is None else total + term
        sums.append(total)
    unit, inverse_two = normalise(normed_s[...] + jnp.concatenate(sums, 1))
    layer_ref[...] = ((unit * gain2_ref[...] + bias2_ref[...]) * mask).astype(BF)
    grad = cot_ref[...].astype(F32) * mask
    vec_ref[2:3, :] += jnp.sum(grad * unit, 0, keepdims=True)
    vec_ref[3:4, :] += jnp.sum(grad, 0, keepdims=True)
    grad = normalise_back(grad * gain2_ref[...], unit, inverse_two)
    grad_two[...] = grad
    grad_ffn = grad.astype(BF)
    sums = []
    for group in range(groups):
        cols = slice(group * wide, (group + 1) * wide)
        total = None
        for piece in range(2):
            rows = slice(piece * part, (piece + 1) * part)
            place = slice(group * hidden + piece * part, group * hidden + (piece + 1) * part)
            target = keep_ref if piece == 0 else gives
            target[1, group] += over_rows(activ[:, place], grad_ffn[:, cols])
            grad_pre = by_transpose(grad_ffn[:, cols], outer_ref[group, rows, :]) * slope[:, place]
            grad_pre = grad_pre.astype(BF)
            target[0, group] += over_rows(grad_pre, into[:, cols])
            term = dot(grad_pre, inner_ref[group, rows, :])
            total = term if total is None else total + term
        sums.append(total)
    grad = grad_two[...] + jnp.concatenate(sums, 1)
    unit = unit_one[...]
    vec_ref[0:1, :] += jnp.sum(grad * unit, 0, keepdims=True)
    vec_ref[1:2, :] += jnp.sum(grad, 0, keepdims=True)
    grad = normalise_back(grad * gain1_ref[...], unit, inverse_one)
    pre_ref[...] = grad
    grad_mix = grad.astype(BF)
    gout_ref[...] += over_rows(mixed_ref[...], grad_mix)
    gmixed_ref[...] = by_transpose(grad_mix, wout_ref[...]).astype(BF)

    @pl.when(row == pl.num_programs(0) - 1)
    def _():
        give_ref[...] = gives[...].astype(BF)


def back_kernel(
    place_ref, length_ref, x_ref, q_ref, k_ref, v_ref, c_ref, spread_ref, span_ref, kern_ref,
    lse_ref, mixed_ref, gmixed_ref, pre_ref, wq_ref, wk_ref, wv_ref, ws_ref, wc_ref, depth_ref,
    gen_ref, columns_ref, grad_ref, gquery_ref, gproj_ref, ggen_ref, gdepth_ref,
    xpad, cpad, gpad, spad, kpad, products, grads, turned, x_total, q_total,
):
    row = pl.program_id(0)
    seq, width = x_ref.shape
    half = q_ref.shape[1]
    length = length_ref[place_ref[0] * pl.num_programs(0) + row]

    @pl.when(row == 0)
    def _():
        for pad in (xpad, cpad, gpad, spad, kpad):
            clear_edges(pad)
        for total in (gquery_ref, gproj_ref, ggen_ref, gdepth_ref):
            total[...] = jnp.zeros_like(total)

    fill_padded(xpad, x_ref[...].astype(F32))
    fill_padded(cpad, c_ref[...].astype(F32))
    fill_padded(gpad, gmixed_ref[:, half:].astype(F32))
    kern = kern_ref[...]
    fill_padded(kpad, kern)
    query_f = q_ref[...].astype(F32)
    span = span_ref[...]
    lane = lax.broadcasted_iota(jnp.int32, (seq, LANE), 1)

    for tile in range(TILES):
        for start in range(0, seq, CHUNK):
            grad = gpad[tile, PAD + start : PAD + start + CHUNK, :]
            for tap in range(KERN):
                begin = PAD - KERN // 2 + tap + start
                products[start : start + CHUNK, lanes(tile * KERN + tap)] = (
                    grad * cpad[tile, begin : begin + CHUNK, :]
                ).astype(BF)
    grad_kern = by_transpose(products[...], columns_ref[:LANE, :])
    inner = over_taps(kern * grad_kern, jnp.add)
    grad_logits = (kern * (grad_kern - inner)).astype(BF)
    mixed_key = (span * query_f).astype(BF)
    ggen_ref[...] += over_rows(mixed_key, grad_logits)
    grad_mix = by_transpose(grad_logits, gen_ref[...])
    grad_span = (grad_mix * query_f).astype(BF)
    q_total[...] = grad_mix * span
    gproj_ref[1, 0] += over_rows(spread_ref[...], grad_span)
    fill_padded(spad, by_transpose(grad_span, ws_ref[...]))

    for tile in range(width // LANE):
        for start in range(0, seq, CHUNK):
            total = jnp.zeros((CHUNK, LANE), F32)
            grad = spad[tile, PAD + start : PAD + start + CHUNK, :]
            for tap in range(KERN):
                begin = PAD - KERN // 2 + tap + start
                moved = grad * xpad[tile, begin : begin + CHUNK, :]
                gdepth_ref[tap, :, lanes(tile)] += jnp.sum(moved.reshape(CHUNK // 8, 8, LANE), 0)
                begin = PAD + KERN // 2 - tap + start
                total = total + depth_ref[tap : tap + 1, lanes(tile)] * spad[tile, begin : begin + CHUNK, :]
            x_total[start : start + CHUNK, lanes(tile)] = total

    moved = jnp.zeros((seq, LANE), F32)
    for tap in range(KERN):
        begin = PAD + KERN // 2 - tap
        moved = jnp.where(lane // 8 == tap, kpad[0, begin : begin + seq, :], moved)
    kern_parts = jnp.concatenate(two_parts(moved), 1)
    for tile in range(TILES):
        for start in range(0, seq, BLOCK):
            wide = dot(
                kern_parts[start : start + BLOCK],
                columns_ref[:, tile * KERN * LANE : (tile + 1) * KERN * LANE],
            )
            total = jnp.zeros((BLOCK, LANE), F32)
            for tap in range(KERN):
                begin = PAD + KERN // 2 - tap + start
                total = total + wide[:, lanes(tap)] * gpad[tile, begin : begin + BLOCK, :]
            grads[start : start + BLOCK, 3 * half + tile * LANE : 3 * half + (tile + 1) * LANE] = (
                total.astype(BF)
            )

    spot = lax.broadcasted_iota(jnp.int32, (seq, 1), 0)
    masked = jnp.where(spot < length, 0.0, MASKED)
    key_side = pick_lane(lane, [(0, masked), (1, 1.0), (2, 1.0), (3, 1.0)])
    value_side = pick_lane(lane, [(0, 1.0), (1, 1.0)])
    for tile in range(TILES):
        query = q_ref[:, lanes(tile)] * SCALE
        grad = gmixed_ref[:, lanes(tile)]
        touch = grad.astype(F32) * mixed_ref[:, lanes(tile)].astype(F32)
        q_sum = jnp.zeros((seq, LANE), F32)
        k_sum = jnp.zeros((seq, LANE), F32)
        v_sum = jnp.zeros((seq, LANE), F32)
        for head in range(2):
            number = tile * 2 + head
            level = -jnp.sum(jnp.where(lane == number, lse_ref[...], 0.0), 1, keepdims=True)
            high = level.astype(BF).astype(F32)
            middle = (level - high).astype(BF).astype(F32)
            query_side = pick_lane(lane, [(0, 1.0), (1, high), (2, middle), (3, level - high - middle)])
            meet = -jnp.sum(head_only(touch, head), 1, keepdims=True)
            high = meet.astype(BF).astype(F32)
            grad_side = pick_lane(lane, [(0, high), (1, meet - high)])
            key_part = head_only(k_ref[:, lanes(tile)], head)
            probs = jnp.exp(
                by_transpose(
                    jnp.concatenate([query, query_side], 1),
                    jnp.concatenate([key_part, key_side], 1),
                )
            )
            grad_probs = by_transpose(
                jnp.concatenate([grad, grad_side], 1),
                jnp.concatenate([head_only(v_ref[:, lanes(tile)], head), value_side], 1),
            )
            grad_scores = (probs * grad_probs).astype(BF)
            q_sum = q_sum + dot(grad_scores, key_part)
            k_sum = k_sum + over_rows(grad_scores, head_only(query, head))
            v_sum = v_sum + over_rows(probs.astype(BF), head_only(grad, head))
        grads[:, lanes(tile)] = (q_sum * SCALE + q_total[:, lanes(tile)]).astype(BF)
        grads[:, half + tile * LANE : half + (tile + 1) * LANE] = k_sum.astype(BF)
        grads[:, 2 * half + tile * LANE : 2 * half + (tile + 1) * LANE] = v_sum.astype(BF)

    turned[...] = x_ref[...].T
    gquery_ref[...] += dot(turned[...], grads[:, :half])
    gproj_ref[0, 0] += dot(turned[...], grads[:, half : 2 * half])
    gproj_ref[0, 1] += dot(turned[...], grads[:, 2 * half : 3 * half])
    gproj_ref[1, 1] += dot(turned[...], grads[:, 3 * half :])
    total = x_total[...] + pre_ref[...]
    for index, weight in enumerate((wq_ref, wk_ref, wv_ref, wc_ref)):
        total = total + by_transpose(grads[:, index * half : (index + 1) * half], weight[...])
    grad_ref[...] = jnp.where(spot < length, total, 0.0)


def fixed(shape):
    return pl.BlockSpec(shape, lambda *_: (0,) * len(shape), pipeline_mode=pl.Buffered(1))


def by_row(seq, width):
    return pl.BlockSpec((seq, width), lambda row, *_: (row, 0))


def call(kernel, rows, in_specs, out_specs, out_shape, scratch, flops, moved, name):
    return pl.pallas_call(
        kernel,
        name=name,
        grid_spec=pltpu.PrefetchScalarGridSpec(
            num_scalar_prefetch=2,
            grid=(rows,),
            in_specs=in_specs,
            out_specs=out_specs,
            scratch_shapes=scratch,
        ),
        out_shape=out_shape,
        compiler_params=pltpu.CompilerParams(
            dimension_semantics=("arbitrary",), vmem_limit_bytes=ROOM
        ),
        cost_estimate=pl.CostEstimate(flops=flops, bytes_accessed=moved, transcendentals=0),
    )


def array(shape, dtype):
    return jax.ShapeDtypeStruct(shape, dtype)


def per_device(
    links,
    tokens,
    lengths,
    w_query,
    branch_proj,
    depth_kernel,
    kernel_gen,
    w_out,
    gain_one,
    bias_one,
    w_inner,
    w_outer,
    gain_two,
    bias_two,
    cotangent,
):
    me, core_bit, _, _ = links.place()
    side = lax.axis_index("branch")
    rows = lengths.shape[0] // 2
    seq = tokens.shape[0] // lengths.shape[0]
    count = rows * seq
    width = tokens.shape[1]
    half = w_query.shape[1]
    groups = w_inner.shape[0]
    hidden = w_inner.shape[2] * links.count
    wide = width // groups

    own_w = branch_proj[0]
    far_w = links.send(
        lax.dynamic_index_in_dim(own_w, core_bit, 0, True), lambda d: d ^ 1
    )
    proj = jnp.concatenate([own_w, far_w, links.core(far_w)])
    other = jnp.stack([2 + core_bit, 3 - core_bit])
    own = jnp.arange(2)
    place = jnp.concatenate(
        [side[None], jnp.where(side == 0, own, other), jnp.where(side == 0, other, own)]
    ).astype(jnp.int32)

    all_w = links.gather_slots(jnp.stack([w_inner, w_outer]).swapaxes(2, 3), 2)

    depth_f = jnp.pad(depth_kernel.astype(F32), ((0, 16 - KERN), (0, 0)))
    gen = kernel_gen.reshape(half, HEADS, KERN).swapaxes(1, 2)
    gen = jnp.pad(gen, ((0, 0), (0, 16 - KERN), (0, 8 - HEADS))).reshape(half, LANE)
    columns = jnp.asarray(tap_columns())

    def weight(index):
        return pl.BlockSpec(
            (None, width, half),
            lambda row, where, length: (where[index], 0, 0),
            pipeline_mode=pl.Buffered(1),
        )

    mine = pl.BlockSpec((seq, width), lambda row, where, length: (where[0] * rows + row, 0))
    row_w, row_h, row_l = by_row(seq, width), by_row(seq, half), by_row(seq, LANE)
    tables = [fixed((16, width)), fixed((half, LANE)), fixed(columns.shape)]
    pads = [pltpu.VMEM((w // LANE, seq + 2 * PAD, LANE), F32) for w in (width, half)]
    square = count * seq * half * 2
    project = count * width * half * 2

    x_in, query, key, value, conv_value, spread, span, kern, lse, mixed = call(
        mix_kernel,
        rows,
        [mine, fixed((width, half))] + [weight(i) for i in (1, 2, 3, 4)] + tables,
        [row_w, row_h, row_h, row_h, row_h, row_w, row_h, row_l, row_l, row_w],
        [
            array((count, width), BF),
            array((count, half), BF),
            array((count, half), BF),
            array((count, half), BF),
            array((count, half), BF),
            array((count, width), BF),
            array((count, half), F32),
            array((count, LANE), F32),
            array((count, LANE), F32),
            array((count, width), BF),
        ],
        pads,
        5 * project + 8 * square,
        16 << 20,
        "mix",
    )(place, lengths, tokens, w_query, proj, proj, proj, proj, depth_f, gen, columns)

    vector = fixed((1, width))
    halves = (2, groups, hidden // 2, wide)
    layer_out, pre_grad, grad_mixed, keep, give, grad_out, vectors = call(
        feed_kernel,
        rows,
        [row_w, row_w, row_w, fixed((width, width))]
        + [
            pl.BlockSpec(
                (None, groups, hidden, wide),
                lambda row, *_, i=i: (i, 0, 0, 0),
                pipeline_mode=pl.Buffered(1),
            )
            for i in range(2)
        ]
        + [vector] * 4,
        [row_w, row_w, row_w, fixed(halves), fixed(halves), fixed((width, width)), fixed((8, width))],
        [
            array((count, width), BF),
            array((count, width), F32),
            array((count, width), BF),
            array(halves, F32),
            array(halves, BF),
            array((width, width), F32),
            array((8, width), F32),
        ],
        [
            pltpu.VMEM(halves, F32),
            pltpu.VMEM((seq, groups * hidden), BF),
            pltpu.VMEM((seq, groups * hidden), F32),
            pltpu.VMEM((seq, width), F32),
            pltpu.VMEM((seq, width), F32),
            pltpu.VMEM((seq, width), BF),
            pltpu.VMEM((seq, width), F32),
        ],
        6 * count * hidden * width * 2 + 6 * project,
        24 << 20,
        "feed",
    )(
        place, lengths, mixed, x_in, cotangent, w_out, all_w, all_w, gain_one[None],
        bias_one[None], gain_two[None], bias_two[None],
    )
    ffn_grads = links.scatter_slots(keep, give, 2).swapaxes(2, 3)
    out_sum = links.sum_all(grad_out)

    input_grad, grad_query, grad_proj, grad_gen, grad_depth = call(
        back_kernel,
        rows,
        [row_w, row_h, row_h, row_h, row_h, row_w, row_h, row_l, row_l, row_w, row_w, row_w]
        + [fixed((width, half))]
        + [weight(i) for i in (1, 2, 3, 4)]
        + tables,
        [
            row_w,
            fixed((width, half)),
            fixed((2, 2, width, half)),
            fixed((half, LANE)),
            fixed((KERN, 8, width)),
        ],
        [
            array((count, width), F32),
            array((width, half), F32),
            array((2, 2, width, half), F32),
            array((half, LANE), F32),
            array((KERN, 8, width), F32),
        ],
        pads
        + [
            pads[1],
            pads[0],
            pltpu.VMEM((1, seq + 2 * PAD, LANE), F32),
            pltpu.VMEM((seq, TILES * KERN * LANE), BF),
            pltpu.VMEM((seq, 4 * half), BF),
            pltpu.VMEM((width, seq), BF),
            pltpu.VMEM((seq, width), F32),
            pltpu.VMEM((seq, half), F32),
        ],
        10 * project + 20 * square,
        24 << 20,
        "back",
    )(
        place, lengths, x_in, query, key, value, conv_value, spread, span, kern, lse, mixed,
        grad_mixed, pre_grad, w_query, proj, proj, proj, proj, depth_f, gen, columns,
    )

    branch_sum = links.sum_branch(grad_proj.reshape(2, 2 * width, half)).reshape(branch_proj.shape)
    gen_part = grad_gen.reshape(half, 16, 8)[:, :KERN, :HEADS].swapaxes(1, 2)
    parts = [
        grad_query,
        vectors[:4].reshape(-1, half),
        jnp.sum(grad_depth, 1).reshape(-1, half),
        gen_part.reshape(half, HEADS * KERN).T,
    ]
    used = sum(p.shape[0] for p in parts)
    parts.append(jnp.zeros(((-used) % links.count, half), F32))
    shared = links.sum_all(jnp.concatenate(parts))
    vec_sum = shared[width : width + 8].reshape(4, width)
    depth_sum = shared[width + 8 : width + 8 + 2 * KERN].reshape(KERN, width)
    return (
        layer_out,
        input_grad,
        shared[:width],
        branch_sum,
        depth_sum,
        shared[width + 8 + 2 * KERN : used].T,
        out_sum,
        vec_sum[0],
        vec_sum[1],
        ffn_grads[0],
        ffn_grads[1],
        vec_sum[2],
        vec_sum[3],
    )


def solution(mesh):
    rows = P(AXES, None)
    hidden = P(None, None, AXES)
    weights = P("branch", None, None, None)
    return jax.shard_map(
        partial(per_device, Links(mesh)),
        mesh=mesh,
        in_specs=(
            P("dp", None), P("dp"), P(), weights, P(), P(), P(), P(), P(), hidden, hidden,
            P(), P(), rows,
        ),
        out_specs=(
            rows, rows, P(), weights, P(), P(), P(), P(), P(), hidden, hidden, P(), P(),
        ),
        check_vma=False,
    )
```

```python
from functools import partial

import jax
import jax.numpy as jnp
import ml_dtypes
import numpy as np
from jax import lax
from jax.experimental import pallas as pl
from jax.experimental.pallas import tpu as pltpu
from jax.sharding import PartitionSpec as P

HEADS = 6
HSIZE = 64
KERN = 9
ROW = 512
FEED = 256
EPS = 1e-12
MASKED = -1000000000.0
SCALE = 0.125
LANE = 128
TILES = HEADS * HSIZE // LANE
PAD = 8
CHUNK = 128
BLOCK = 256
ROOM = 58 << 20
SLOTS = 32
KEPT = SLOTS // 2
FIRST = 5
AXES = ("dp", "branch")
BF = jnp.bfloat16
F32 = jnp.float32


class Links:
    def __init__(self, mesh):
        self.count = mesh.shape["dp"] * 2
        bits = self.count.bit_length() - 1
        assert mesh.shape["branch"] == 2 and self.count == 1 << bits and bits >= 5
        self.more = [tuple(range(low, min(low + 2, bits))) for low in range(5, bits, 2)]

    @staticmethod
    def plane(number, place):
        flipped = place if number & 2 == 0 else place >> 1 | (place & 1) << 1
        return number ^ (flipped & 1) ^ (flipped >> 1) << 2

    def slots(self):
        return [
            [
                self.plane(d ^ core << 1, place) ^ far << 3
                for core in range(2)
                for place in range(4)
                for far in range(4)
            ]
            for d in range(self.count)
        ]

    def send(self, value, partner):
        return lax.ppermute(value, AXES, [(d, partner(d)) for d in range(self.count)])

    def core(self, value):
        return self.send(value, lambda d: d ^ 2)

    def near(self, value, place):
        return self.send(value, lambda d: self.plane(d, place))

    def far(self, value, place):
        return self.send(value, lambda d: d ^ place << 3)

    def gather(self, piece, step):
        return jnp.concatenate([piece] + [step(piece, i) for i in range(1, 4)])

    def scatter(self, total, step):
        parts = total.reshape((4, -1) + total.shape[1:])
        total = parts[0]
        for i in range(1, 4):
            total = total + step(parts[i].astype(BF), i).astype(F32)
        return total

    def halve(self, total, place):
        keep, give = jnp.split(total, 2)
        return keep + self.near(give.astype(BF), place).astype(F32)

    def sum_more(self, total):
        me = self.number()
        for stage in self.more:
            size = 1 << len(stage)
            own = (me >> stage[0]) & (size - 1)
            parts = total.reshape((size, -1) + total.shape[1:])
            total = lax.dynamic_index_in_dim(parts, own, 0, False)
            for i in range(1, size):
                part = lax.dynamic_index_in_dim(parts, own ^ i, 0, False).astype(BF)
                total = total + self.send(part, lambda d: d ^ i << stage[0]).astype(F32)
        piece = total.astype(BF)
        for stage in reversed(self.more):
            size = 1 << len(stage)
            own = (me >> stage[0]) & (size - 1)
            parts = jnp.stack(
                [piece] + [self.send(piece, lambda d: d ^ i << stage[0]) for i in range(1, size)]
            )
            piece = jnp.concatenate(
                [lax.dynamic_index_in_dim(parts, own ^ i, 0, False) for i in range(size)]
            )
        return piece

    def gather_more(self, piece):
        for stage in reversed(self.more):
            size = 1 << len(stage)
            others = [self.send(piece, lambda d: d ^ i << stage[0]) for i in range(1, size)]
            piece = jnp.concatenate([piece] + others, 1)
        return piece

    def scatter_more(self, total):
        for stage in self.more:
            size = 1 << len(stage)
            parts = jnp.split(total, size, 1)
            total = parts[0]
            for i in range(1, size):
                total = total + self.send(
                    parts[i].astype(BF), lambda d: d ^ i << stage[0]
                ).astype(F32)
        return total

    @staticmethod
    def number():
        return lax.axis_index("dp") * 2 + lax.axis_index("branch")


def dot(left, right):
    return jnp.dot(left, right, preferred_element_type=F32)


def over_rows(left, right):
    return lax.dot_general(left, right, (((0,), (0,)), ((), ())), preferred_element_type=F32)


def by_transpose(left, right):
    return lax.dot_general(left, right, (((1,), (1,)), ((), ())), preferred_element_type=F32)


def lanes(index):
    return slice(index * LANE, (index + 1) * LANE)


def tap_columns():
    source = np.arange(2 * LANE) % LANE
    column = np.arange(TILES * KERN * LANE)
    tile, tap, lane = column // (KERN * LANE), column // LANE % KERN, column % LANE
    head = tile * 2 + lane // HSIZE
    return (source[:, None] == tap * 8 + head).astype(ml_dtypes.bfloat16)


def over_taps(field, combine):
    for shift in (64, 32, 16, 8):
        field = combine(field, pltpu.roll(field, shift, 1))
    return field


def two_parts(field):
    high = field.astype(BF)
    return high, (field - high.astype(F32)).astype(BF)


def head_only(field, head):
    lane = lax.broadcasted_iota(jnp.int32, field.shape, 1)
    return jnp.where((lane < HSIZE) == (head == 0), field, jnp.zeros_like(field))


def pick_lane(lane, choices):
    block = jnp.zeros(lane.shape, F32)
    for index, value in choices:
        block = jnp.where(lane == index, value, block)
    return block.astype(BF)


def fill_padded(pad_ref, field):
    for tile in range(pad_ref.shape[0]):
        pad_ref[tile, PAD : PAD + field.shape[0], :] = field[:, lanes(tile)]


def clear_edges(pad_ref):
    edge = jnp.zeros((pad_ref.shape[0], PAD, LANE), F32)
    pad_ref[:, :PAD, :] = edge
    pad_ref[:, pad_ref.shape[1] - PAD :, :] = edge


def deal(place_ref, sources, keep_ref, give_ref, spare_ref):
    for slot in range(SLOTS):
        target = keep_ref if slot < KEPT else spare_ref
        offset = target.shape[1] - sum(rows for _, _, rows in sources)
        for total_ref, columns, rows in sources:
            begin = pl.multiple_of(place_ref[FIRST + slot] * rows, 8)
            target[slot % KEPT, offset : offset + rows, :] = total_ref[pl.ds(begin, rows), columns]
            offset += rows
    give_ref[...] = spare_ref[...].astype(BF)


def mix_kernel(
    place_ref, length_ref, tok_ref, wq_ref, wk_ref, wv_ref, ws_ref, wc_ref, depth_ref, gen_ref,
    columns_ref, x_ref, q_ref, k_ref, v_ref, c_ref, spread_ref, span_ref, kern_ref, lse_ref,
    mixed_ref, xpad, cpad,
):
    row = pl.program_id(0)
    seq, width = tok_ref.shape
    half = q_ref.shape[1]
    length = length_ref[place_ref[0] * pl.num_programs(0) + row]

    @pl.when(row == 0)
    def _():
        clear_edges(xpad)
        clear_edges(cpad)

    spot = lax.broadcasted_iota(jnp.int32, (seq, 1), 0)
    x_f = jnp.where(spot < length, tok_ref[...].astype(F32), 0.0)
    x_in = x_f.astype(BF)
    x_ref[...] = x_in
    fill_padded(xpad, x_f)
    q_ref[...] = dot(x_in, wq_ref[...]).astype(BF)
    k_ref[...] = dot(x_in, wk_ref[...]).astype(BF)
    v_ref[...] = dot(x_in, wv_ref[...]).astype(BF)
    c_ref[...] = dot(x_in, wc_ref[...]).astype(BF)
    fill_padded(cpad, c_ref[...].astype(F32))

    for tile in range(width // LANE):
        for start in range(0, seq, CHUNK):
            total = jnp.zeros((CHUNK, LANE), F32)
            for tap in range(KERN):
                begin = PAD - KERN // 2 + tap + start
                total = total + depth_ref[tap : tap + 1, lanes(tile)] * xpad[tile, begin : begin + CHUNK, :]
            spread_ref[start : start + CHUNK, lanes(tile)] = total.astype(BF)

    span = dot(spread_ref[...], ws_ref[...])
    span_ref[...] = span
    mixed_key = (span * q_ref[...].astype(F32)).astype(BF)
    logits = dot(mixed_key, gen_ref[...])
    lane = lax.broadcasted_iota(jnp.int32, (seq, LANE), 1)
    used = (lane < KERN * 8) & (lane % 8 < HEADS)
    logits = jnp.where(used, logits, -1e30)
    expo = jnp.exp(logits - over_taps(logits, jnp.maximum))
    kern = jnp.where(used, expo / over_taps(expo, jnp.add), 0.0)
    kern_ref[...] = kern
    kern_parts = jnp.concatenate(two_parts(kern), 1)
    for tile in range(TILES):
        for start in range(0, seq, BLOCK):
            wide = dot(
                kern_parts[start : start + BLOCK],
                columns_ref[:, tile * KERN * LANE : (tile + 1) * KERN * LANE],
            )
            total = jnp.zeros((BLOCK, LANE), F32)
            for tap in range(KERN):
                begin = PAD - KERN // 2 + tap + start
                total = total + wide[:, lanes(tap)] * cpad[tile, begin : begin + BLOCK, :]
            mixed_ref[start : start + BLOCK, half + tile * LANE : half + (tile + 1) * LANE] = (
                total.astype(BF)
            )

    masked = jnp.where(spot < length, 0.0, MASKED)
    key_side = pick_lane(lane, [(0, masked)])
    query_side = pick_lane(lane, [(0, 1.0)])
    lse = jnp.zeros((seq, LANE), F32)
    for tile in range(TILES):
        query = jnp.concatenate([q_ref[:, lanes(tile)] * SCALE, query_side], 1)
        result = jnp.zeros((seq, LANE), F32)
        for head in range(2):
            key = jnp.concatenate([head_only(k_ref[:, lanes(tile)], head), key_side], 1)
            value = head_only(v_ref[:, lanes(tile)], head)
            scores = by_transpose(query, key)
            top = jnp.max(scores, 1, keepdims=True)
            expo = jnp.exp(scores - top)
            total = jnp.sum(expo, 1, keepdims=True)
            result = result + dot(expo.astype(BF), value) * (1.0 / total)
            lse = jnp.where(lane == tile * 2 + head, top + jnp.log(total), lse)
        mixed_ref[:, lanes(tile)] = result.astype(BF)
    lse_ref[...] = lse


def normalise(field):
    centred = field - jnp.mean(field, -1, keepdims=True)
    inverse = lax.rsqrt(jnp.mean(centred * centred, -1, keepdims=True) + EPS)
    return centred * inverse, inverse


def normalise_back(grad, unit, inverse):
    return inverse * (
        grad - jnp.mean(grad, -1, keepdims=True) - unit * jnp.mean(grad * unit, -1, keepdims=True)
    )


def gelu_and_slope(field):
    bell = jnp.exp(field * field * -0.5)
    step = 1.0 / (1.0 + 0.2316419 * jnp.abs(field))
    norm = 0.3989422804014327
    tail = 1.330274429 * norm
    for coefficient in (-1.821255978, 1.781477937, -0.356563782, 0.319381530):
        tail = tail * step + coefficient * norm
    tail = tail * step * bell
    share = jnp.where(field >= 0.0, 1.0 - tail, tail)
    return field * share, share + field * bell * norm


def whole(weights_ref, which, group):
    slots, rows, wide = weights_ref.shape
    units = rows // 4
    begin = (which * 2 + group) * units
    return weights_ref[:, begin : begin + units, :].reshape(slots * units, wide)


def add_units(target, which, group, value):
    slots, _, wide = target.shape
    units = value.shape[0] // slots
    begin = (which * 2 + group) * units
    target[:, begin : begin + units, :] += value.reshape(slots, units, wide)


def feed_kernel(
    place_ref, length_ref, mixed_ref, x_ref, cot_ref, wout_ref, own_ref, other_ref, gain1_ref,
    bias1_ref, gain2_ref, bias2_ref, layer_ref, pre_ref, gmixed_ref, keep_ref, give_ref, vec_ref,
    gives, gout, activ, slope, unit_one, normed_s, into, grad_two,
):
    row = pl.program_id(0)
    seq, width = x_ref.shape
    half = width // 2
    part = activ.shape[1] // 4
    steps = ROW // seq
    length = length_ref[place_ref[0] * (pl.num_programs(0) // steps) + row // steps] - row % steps * seq
    mask = (lax.broadcasted_iota(jnp.int32, (seq, 1), 0) < length).astype(F32)

    @pl.when(row == 0)
    def _():
        keep_ref[...] = jnp.zeros_like(keep_ref)
        gives[...] = jnp.zeros_like(gives)
        gout[...] = jnp.zeros_like(gout)
        vec_ref[...] = jnp.zeros_like(vec_ref)

    unit, inverse_one = normalise(x_ref[...].astype(F32) + dot(mixed_ref[...], wout_ref[...]))
    unit_one[...] = unit
    normed = unit * gain1_ref[...] + bias1_ref[...]
    normed_s[...] = normed
    into[...] = normed.astype(BF)
    sums = []
    for group in range(2):
        cols = slice(group * half, (group + 1) * half)
        total = None
        for core, weights_ref in enumerate((own_ref, other_ref)):
            place = slice((group * 2 + core) * part, (group * 2 + core + 1) * part)
            value, rise = gelu_and_slope(by_transpose(into[:, cols], whole(weights_ref, 0, group)))
            activ[:, place] = value.astype(BF)
            slope[:, place] = rise.astype(BF)
            term = dot(activ[:, place], whole(weights_ref, 1, group))
            total = term if total is None else total + term
        sums.append(total)
    unit, inverse_two = normalise(normed_s[...] + jnp.concatenate(sums, 1))
    layer_ref[...] = ((unit * gain2_ref[...] + bias2_ref[...]) * mask).astype(BF)
    grad = cot_ref[...].astype(F32) * mask
    vec_ref[2:3, :] += jnp.sum(grad * unit, 0, keepdims=True)
    vec_ref[3:4, :] += jnp.sum(grad, 0, keepdims=True)
    grad = normalise_back(grad * gain2_ref[...], unit, inverse_two)
    grad_two[...] = grad
    grad_ffn = grad.astype(BF)
    sums = []
    for group in range(2):
        cols = slice(group * half, (group + 1) * half)
        total = None
        for core, weights_ref in enumerate((own_ref, other_ref)):
            place = slice((group * 2 + core) * part, (group * 2 + core + 1) * part)
            target = gives if core else keep_ref
            add_units(target, 1, group, over_rows(activ[:, place], grad_ffn[:, cols]))
            grad_pre = by_transpose(grad_ffn[:, cols], whole(weights_ref, 1, group))
            grad_pre = (grad_pre * slope[:, place].astype(F32)).astype(BF)
            add_units(target, 0, group, over_rows(grad_pre, into[:, cols]))
            term = dot(grad_pre, whole(weights_ref, 0, group))
            total = term if total is None else total + term
        sums.append(total)
    grad = grad_two[...] + jnp.concatenate(sums, 1)
    unit = unit_one[...]
    vec_ref[0:1, :] += jnp.sum(grad * unit, 0, keepdims=True)
    vec_ref[1:2, :] += jnp.sum(grad, 0, keepdims=True)
    grad = normalise_back(grad * gain1_ref[...], unit, inverse_one)
    pre_ref[...] = grad
    grad_mix = grad.astype(BF)
    gout[...] += over_rows(mixed_ref[...], grad_mix)
    gmixed_ref[...] = by_transpose(grad_mix, wout_ref[...]).astype(BF)

    @pl.when(row == pl.num_programs(0) - 1)
    def _():
        rows = width // SLOTS
        columns = slice(0, half), slice(half, width)
        deal(place_ref, [(gout, c, rows) for c in columns], keep_ref, give_ref, gives)


def conv_kernel(
    place_ref, length_ref, x_ref, q_ref, c_ref, spread_ref, span_ref, kern_ref, gmixed_ref, ws_ref,
    depth_ref, gen_ref, columns_ref, keep_ref, give_ref, gcv_ref, qconv_ref, xconv_ref, ggen_ref,
    gdepth_ref, xpad, cpad, gpad, spad, kpad, products, total, spare,
):
    row = pl.program_id(0)
    seq, width = x_ref.shape
    half = q_ref.shape[1]

    @pl.when(row == 0)
    def _():
        for pad in (xpad, cpad, gpad, spad, kpad):
            clear_edges(pad)
        for sums in (total, ggen_ref, gdepth_ref):
            sums[...] = jnp.zeros_like(sums)

    fill_padded(xpad, x_ref[...].astype(F32))
    fill_padded(cpad, c_ref[...].astype(F32))
    fill_padded(gpad, gmixed_ref[...].astype(F32))
    kern = kern_ref[...]
    fill_padded(kpad, kern)
    query_f = q_ref[...].astype(F32)
    span = span_ref[...]
    lane = lax.broadcasted_iota(jnp.int32, (seq, LANE), 1)

    for tile in range(TILES):
        for start in range(0, seq, CHUNK):
            grad = gpad[tile, PAD + start : PAD + start + CHUNK, :]
            for tap in range(KERN):
                begin = PAD - KERN // 2 + tap + start
                products[start : start + CHUNK, lanes(tile * KERN + tap)] = (
                    grad * cpad[tile, begin : begin + CHUNK, :]
                ).astype(BF)
    grad_kern = by_transpose(products[...], columns_ref[:LANE, :])
    inner = over_taps(kern * grad_kern, jnp.add)
    grad_logits = (kern * (grad_kern - inner)).astype(BF)
    mixed_key = (span * query_f).astype(BF)
    ggen_ref[...] += over_rows(mixed_key, grad_logits)
    grad_mix = by_transpose(grad_logits, gen_ref[...])
    grad_span = (grad_mix * query_f).astype(BF)
    qconv_ref[...] = grad_mix * span
    total[:, :half] += over_rows(spread_ref[...], grad_span)
    fill_padded(spad, by_transpose(grad_span, ws_ref[...]))

    for tile in range(width // LANE):
        for start in range(0, seq, CHUNK):
            moved_sum = jnp.zeros((CHUNK, LANE), F32)
            grad = spad[tile, PAD + start : PAD + start + CHUNK, :]
            for tap in range(KERN):
                begin = PAD - KERN // 2 + tap + start
                moved = grad * xpad[tile, begin : begin + CHUNK, :]
                gdepth_ref[tap, :, lanes(tile)] += jnp.sum(moved.reshape(CHUNK // 8, 8, LANE), 0)
                begin = PAD + KERN // 2 - tap + start
                moved_sum = moved_sum + depth_ref[tap : tap + 1, lanes(tile)] * spad[tile, begin : begin + CHUNK, :]
            xconv_ref[start : start + CHUNK, lanes(tile)] = moved_sum

    moved = jnp.zeros((seq, LANE), F32)
    for tap in range(KERN):
        begin = PAD + KERN // 2 - tap
        moved = jnp.where(lane // 8 == tap, kpad[0, begin : begin + seq, :], moved)
    kern_parts = jnp.concatenate(two_parts(moved), 1)
    for tile in range(TILES):
        for start in range(0, seq, BLOCK):
            wide = dot(
                kern_parts[start : start + BLOCK],
                columns_ref[:, tile * KERN * LANE : (tile + 1) * KERN * LANE],
            )
            back = jnp.zeros((BLOCK, LANE), F32)
            for tap in range(KERN):
                begin = PAD + KERN // 2 - tap + start
                back = back + wide[:, lanes(tap)] * gpad[tile, begin : begin + BLOCK, :]
            gcv_ref[start : start + BLOCK, lanes(tile)] = back.astype(BF)
    total[:, half:] += over_rows(x_ref[...], gcv_ref[...])

    @pl.when(row == pl.num_programs(0) - 1)
    def _():
        rows = width // SLOTS
        deal(place_ref, [(total, slice(0, half), rows), (total, slice(half, width), rows)], keep_ref, give_ref, spare)


def att_kernel(
    place_ref, length_ref, x_ref, q_ref, k_ref, v_ref, lse_ref, mixed_ref, gmixed_ref, qconv_ref,
    small_ref, keep_ref, give_ref, grads_ref, turned, total, spare,
):
    row = pl.program_id(0)
    seq, width = x_ref.shape
    half = q_ref.shape[1]
    length = length_ref[place_ref[0] * pl.num_programs(0) + row]

    @pl.when(row == 0)
    def _():
        total[...] = jnp.zeros_like(total)

    lane = lax.broadcasted_iota(jnp.int32, (seq, LANE), 1)
    spot = lax.broadcasted_iota(jnp.int32, (seq, 1), 0)
    masked = jnp.where(spot < length, 0.0, MASKED)
    key_side = pick_lane(lane, [(0, masked), (1, 1.0), (2, 1.0), (3, 1.0)])
    value_side = pick_lane(lane, [(0, 1.0), (1, 1.0)])
    for tile in range(TILES):
        query = q_ref[:, lanes(tile)] * SCALE
        grad = gmixed_ref[:, lanes(tile)]
        touch = grad.astype(F32) * mixed_ref[:, lanes(tile)].astype(F32)
        q_sum = jnp.zeros((seq, LANE), F32)
        k_sum = jnp.zeros((seq, LANE), F32)
        v_sum = jnp.zeros((seq, LANE), F32)
        for head in range(2):
            number = tile * 2 + head
            level = -jnp.sum(jnp.where(lane == number, lse_ref[...], 0.0), 1, keepdims=True)
            high = level.astype(BF).astype(F32)
            middle = (level - high).astype(BF).astype(F32)
            query_side = pick_lane(lane, [(0, 1.0), (1, high), (2, middle), (3, level - high - middle)])
            meet = -jnp.sum(head_only(touch, head), 1, keepdims=True)
            high = meet.astype(BF).astype(F32)
            grad_side = pick_lane(lane, [(0, high), (1, meet - high)])
            key_part = head_only(k_ref[:, lanes(tile)], head)
            probs = jnp.exp(
                by_transpose(
                    jnp.concatenate([query, query_side], 1),
                    jnp.concatenate([key_part, key_side], 1),
                )
            )
            grad_probs = by_transpose(
                jnp.concatenate([grad, grad_side], 1),
                jnp.concatenate([head_only(v_ref[:, lanes(tile)], head), value_side], 1),
            )
            grad_scores = (probs * grad_probs).astype(BF)
            q_sum = q_sum + dot(grad_scores, key_part)
            k_sum = k_sum + over_rows(grad_scores, head_only(query, head))
            v_sum = v_sum + over_rows(probs.astype(BF), head_only(grad, head))
        grads_ref[:, lanes(tile)] = (q_sum * SCALE + qconv_ref[:, lanes(tile)]).astype(BF)
        grads_ref[:, half + tile * LANE : half + (tile + 1) * LANE] = k_sum.astype(BF)
        grads_ref[:, 2 * half + tile * LANE : 2 * half + (tile + 1) * LANE] = v_sum.astype(BF)
    turned[...] = x_ref[...].T
    for part in range(3):
        total[part] += dot(turned[...], grads_ref[:, part * half : (part + 1) * half])

    @pl.when(row == pl.num_programs(0) - 1)
    def _():
        rows = width // SLOTS
        sources = [(total.at[part], slice(0, half), rows) for part in range(3)]
        sources.append((small_ref, slice(0, half), small_ref.shape[0] // SLOTS))
        deal(place_ref, sources, keep_ref, give_ref, spare)


def dx_kernel(
    place_ref, length_ref, grads_ref, gcv_ref, pre_ref, xconv_ref, wq_ref, wk_ref, wv_ref, wc_ref,
    out_ref,
):
    seq, half = gcv_ref.shape
    length = length_ref[place_ref[0] * pl.num_programs(0) + pl.program_id(0)]
    total = xconv_ref[...] + pre_ref[...] + by_transpose(gcv_ref[...], wc_ref[...])
    for index, weight in enumerate((wq_ref, wk_ref, wv_ref)):
        total = total + by_transpose(grads_ref[:, index * half : (index + 1) * half], weight[...])
    spot = lax.broadcasted_iota(jnp.int32, (seq, 1), 0)
    out_ref[...] = jnp.where(spot < length, total, 0.0)


def last_kernel(
    place_ref, length_ref, conv0_ref, conv1_ref, att0_ref, att1_ref, query_ref, branch_ref,
    out_ref, small_ref, conv, att,
):
    width, half = query_ref.shape
    rows = width // SLOTS
    few = small_ref.shape[0] // SLOTS
    attends = place_ref[0] == 0
    for core, (conv_ref, att_ref) in enumerate(((conv0_ref, att0_ref), (conv1_ref, att1_ref))):
        conv[...] = conv_ref[...].astype(F32)
        att[...] = att_ref[...].astype(F32)
        for slot in range(KEPT):
            piece = place_ref[FIRST + core * KEPT + slot]
            here = pl.ds(pl.multiple_of(piece * rows, 8), rows)
            query_ref[here, :] = att[slot, :rows, :]
            for part in range(2):
                branch_ref[part, here, :] = jnp.where(
                    attends,
                    att[slot, (part + 1) * rows : (part + 2) * rows, :],
                    conv[slot, part * rows : (part + 1) * rows, :],
                )
                out_ref[here, part * half : (part + 1) * half] = conv[
                    slot, (part + 2) * rows : (part + 3) * rows, :
                ]
            small_ref[pl.ds(pl.multiple_of(piece * few, 8), few), :] = att[slot, 3 * rows :, :]


def fixed(shape):
    return pl.BlockSpec(shape, lambda *_: (0,) * len(shape), pipeline_mode=pl.Buffered(1))


def by_row(seq, width):
    return pl.BlockSpec((seq, width), lambda row, *_: (row, 0))


def array(shape, dtype):
    return jax.ShapeDtypeStruct(shape, dtype)


def call(kernel, name, rows, operands, in_specs, outs, out_specs, scratch, flops, moved):
    return pl.pallas_call(
        kernel,
        name=name,
        grid_spec=pltpu.PrefetchScalarGridSpec(
            num_scalar_prefetch=2,
            grid=(rows,),
            in_specs=in_specs,
            out_specs=out_specs,
            scratch_shapes=scratch,
        ),
        out_shape=outs,
        compiler_params=pltpu.CompilerParams(
            dimension_semantics=("arbitrary",), vmem_limit_bytes=ROOM
        ),
        cost_estimate=pl.CostEstimate(flops=flops, bytes_accessed=moved, transcendentals=0),
    )(*operands)


def tie(*values):
    return lax.optimization_barrier(values)


def per_device(
    links,
    tokens,
    lengths,
    w_query,
    branch_proj,
    depth_kernel,
    kernel_gen,
    w_out,
    gain_one,
    bias_one,
    w_inner,
    w_outer,
    gain_two,
    bias_two,
    cotangent,
):
    me = links.number()
    core_bit = (me >> 1) & 1
    side = lax.axis_index("branch")
    rows = lengths.shape[0] // 2
    seq = tokens.shape[0] // lengths.shape[0]
    count = rows * seq
    width = tokens.shape[1]
    half = w_query.shape[1]
    groups = w_inner.shape[0]
    units = w_inner.shape[2] * links.count // SLOTS
    hidden = groups * units * SLOTS
    wide = width // groups

    own_w = branch_proj[0]
    far_w = links.send(lax.dynamic_index_in_dim(own_w, core_bit, 0, True), lambda d: d ^ 1)
    near_w = links.core(far_w)
    other = jnp.stack([2 + core_bit, 3 - core_bit])
    own = jnp.arange(2)
    place = jnp.concatenate(
        [
            side[None],
            jnp.where(side == 0, own, other),
            jnp.where(side == 0, other, own),
            jnp.array(links.slots())[me] & (SLOTS - 1),
        ]
    ).astype(jnp.int32)

    weights = jnp.stack([w_inner, w_outer]).swapaxes(2, 3).reshape((2 * groups, -1, wide))
    weights = links.gather_more(weights).reshape(1, 2 * groups * units, wide)
    weights = links.gather(weights, links.far)

    proj = jnp.concatenate([own_w, far_w, near_w])
    depth_f = jnp.pad(depth_kernel.astype(F32), ((0, 16 - KERN), (0, 0)))
    gen = kernel_gen.reshape(half, HEADS, KERN).swapaxes(1, 2)
    gen = jnp.pad(gen, ((0, 0), (0, 16 - KERN), (0, 8 - HEADS))).reshape(half, LANE)
    columns = jnp.asarray(tap_columns())

    def weight(index):
        return pl.BlockSpec(
            (None, width, half),
            lambda row, where, length: (where[index], 0, 0),
            pipeline_mode=pl.Buffered(1),
        )

    wk, wv, ws, wc = (weight(i) for i in (1, 2, 3, 4))
    wq = fixed((width, half))
    mine = pl.BlockSpec((seq, width), lambda row, where, length: (where[0] * rows + row, 0))
    row_w, row_h, row_l = by_row(seq, width), by_row(seq, half), by_row(seq, LANE)
    row_f = by_row(FEED, width)
    vector, square_w = fixed((1, width)), fixed((width, width))
    tables = [fixed((16, width)), fixed((half, LANE)), fixed(columns.shape)]
    pad_w, pad_h = (pltpu.VMEM((w // LANE, seq + 2 * PAD, LANE), F32) for w in (width, half))
    square = count * seq * half * 2
    project = count * width * half * 2
    norm_one = [gain_one[None], bias_one[None]]
    norm_two = [gain_two[None], bias_two[None]]

    def two_halves(rows_of):
        shape = (KEPT, rows_of, half)
        return [array(shape, F32), array(shape, BF)], [fixed(shape)] * 2, pltpu.VMEM(shape, F32)

    proj, weights = tie(proj, weights)
    weights = links.gather(weights, links.near)

    x_in, query, key, value, conv_value, spread, span, kern, lse, mixed = call(
        mix_kernel,
        "mix",
        rows,
        [place, lengths, tokens, w_query, proj, proj, proj, proj, depth_f, gen, columns],
        [mine, wq, wk, wv, ws, wc] + tables,
        [
            array((count, width), BF),
            array((count, half), BF),
            array((count, half), BF),
            array((count, half), BF),
            array((count, half), BF),
            array((count, width), BF),
            array((count, half), F32),
            array((count, LANE), F32),
            array((count, LANE), F32),
            array((count, width), BF),
        ],
        [row_w, row_h, row_h, row_h, row_h, row_w, row_h, row_l, row_l, row_w],
        [pad_w, pad_h],
        5 * project + 8 * square,
        16 << 20,
    )
    mixed, weights = tie(mixed, weights)
    other_weights = links.core(weights)
    ffn_rows = 2 * groups * units
    outs, specs, spare = two_halves(ffn_rows + width * 2 // SLOTS)
    layer_out, pre_grad, grad_mixed, ffn_keep, ffn_give, vectors = call(
        feed_kernel,
        "feed",
        count // FEED,
        [place, lengths, mixed, x_in, cotangent, w_out, weights, other_weights]
        + norm_one
        + norm_two,
        [row_f, row_f, row_f, square_w] + [fixed((KEPT, ffn_rows, wide))] * 2 + [vector] * 4,
        [array((count, width), BF), array((count, width), F32), array((count, width), BF)]
        + outs
        + [array((8, width), F32)],
        [row_f, row_f, row_f] + specs + [fixed((8, width))],
        [
            spare,
            pltpu.VMEM((width, width), F32),
            pltpu.VMEM((FEED, hidden), BF),
            pltpu.VMEM((FEED, hidden), BF),
            pltpu.VMEM((FEED, width), F32),
            pltpu.VMEM((FEED, width), F32),
            pltpu.VMEM((FEED, width), BF),
            pltpu.VMEM((FEED, width), F32),
        ],
        30 * project,
        32 << 20,
    )
    ffn_more = links.core(ffn_give)

    outs, specs, spare = two_halves(width * 2 // SLOTS)
    conv_keep, conv_give, grad_cv, q_conv, x_conv, grad_gen, grad_depth = call(
        conv_kernel,
        "conv",
        rows,
        [place, lengths, x_in, query, conv_value, spread, span, kern, grad_mixed, proj, depth_f]
        + [gen, columns],
        [row_w, row_h, row_h, row_w, row_h, row_l]
        + [pl.BlockSpec((seq, half), lambda row, *_: (row, 1)), ws]
        + tables,
        outs
        + [
            array((count, half), BF),
            array((count, half), F32),
            array((count, width), F32),
            array((half, LANE), F32),
            array((KERN, 8, width), F32),
        ],
        specs + [row_h, row_h, row_w, fixed((half, LANE)), fixed((KERN, 8, width))],
        [
            pad_w,
            pad_h,
            pad_h,
            pad_w,
            pltpu.VMEM((1, seq + 2 * PAD, LANE), F32),
            pltpu.VMEM((seq, TILES * KERN * LANE), BF),
            pltpu.VMEM((width, width), F32),
            spare,
        ],
        8 * project,
        16 << 20,
    )
    conv_more = links.core(conv_give)
    small = jnp.concatenate(
        [
            vectors[:4].reshape(-1, half),
            jnp.sum(grad_depth, 1).reshape(-1, half),
            grad_gen.T[: KERN * 8],
        ]
    )
    used = small.shape[0]
    small = jnp.pad(small, ((0, SLOTS * 8 - used), (0, 0)))

    ffn_more, q_conv = tie(ffn_more, q_conv)
    ffn_sum = ffn_keep + ffn_more.astype(F32)
    q_conv, ffn_sum = tie(q_conv, ffn_sum)
    ffn_sum = links.halve(ffn_sum, 2)
    outs, specs, spare = two_halves(width * 3 // SLOTS + 8)
    att_keep, att_give, grads = call(
        att_kernel,
        "att",
        rows,
        [place, lengths, x_in, query, key, value, lse, mixed, grad_mixed, q_conv, small],
        [row_w, row_h, row_h, row_h, row_l, row_h, row_h, row_h, fixed((SLOTS * 8, half))],
        outs + [array((count, 3 * half), BF)],
        specs + [by_row(seq, 3 * half)],
        [pltpu.VMEM((width, seq), BF), pltpu.VMEM((3, width, half), F32), spare],
        3 * project + 20 * square,
        16 << 20,
    )
    att_give, conv_more, ffn_sum = tie(att_give, conv_more, ffn_sum)
    att_more = links.core(att_give)
    conv_sum = conv_keep + conv_more.astype(F32)
    att_sum = att_keep + att_more.astype(F32)
    grads, att_sum, conv_sum = tie(grads, att_sum, conv_sum)
    att_sum = links.scatter(att_sum, links.near)
    conv_sum = links.scatter(conv_sum, links.near)
    ffn_sum = links.halve(ffn_sum, 1)

    input_grad = call(
        dx_kernel,
        "dx",
        rows,
        [place, lengths, grads, grad_cv, pre_grad, x_conv, w_query, proj, proj, proj],
        [by_row(seq, 3 * half), row_h, row_w, row_w, wq, wk, wv, wc],
        array((count, width), F32),
        row_w,
        [],
        4 * project,
        16 << 20,
    )
    input_grad, att_sum, conv_sum = tie(input_grad, att_sum, conv_sum)
    conv_sum = links.scatter(conv_sum, links.far)
    ffn_sum = links.scatter(ffn_sum, links.far)[0]
    att_sum = links.scatter(att_sum, links.far)
    rest = jnp.concatenate([conv_sum[0], ffn_sum[ffn_rows:]])
    conv_own = links.gather(links.gather(links.sum_more(rest)[None], links.far), links.near)
    conv_other = links.core(conv_own)
    att_own = links.gather(links.gather(links.sum_more(att_sum[0])[None], links.far), links.near)
    att_other = links.core(att_own)
    ffn_grads = links.scatter_more(ffn_sum[:ffn_rows].reshape(2 * groups, units, wide))
    ffn_grads = ffn_grads.swapaxes(1, 2).reshape((2,) + w_inner.shape)
    grad_query, branch_sum, out_grad, small = call(
        last_kernel,
        "place",
        1,
        [place, lengths, conv_own, conv_other, att_own, att_other],
        [fixed(conv_own.shape)] * 2 + [fixed(att_own.shape)] * 2,
        [
            array((width, half), F32),
            array((2, width, half), F32),
            array((width, width), F32),
            array((SLOTS * 8, half), F32),
        ],
        [wq, fixed((2, width, half)), square_w, fixed((SLOTS * 8, half))],
        [pltpu.VMEM(conv_own.shape, F32), pltpu.VMEM(att_own.shape, F32)],
        0,
        8 << 20,
    )
    vec_sum = small[:8].reshape(4, width)
    depth_sum = small[8 : 8 + 2 * KERN].reshape(KERN, width)
    gen_sum = small[8 + 2 * KERN : used].reshape(KERN, 8, half)[:, :HEADS]
    return (
        layer_out,
        input_grad,
        grad_query,
        branch_sum[None],
        depth_sum,
        gen_sum.transpose(2, 1, 0).reshape(kernel_gen.shape),
        out_grad,
        vec_sum[0],
        vec_sum[1],
        ffn_grads[0],
        ffn_grads[1],
        vec_sum[2],
        vec_sum[3],
    )


def solution(mesh):
    rows = P(AXES, None)
    hidden = P(None, None, AXES)
    weights = P("branch", None, None, None)
    return jax.shard_map(
        partial(per_device, Links(mesh)),
        mesh=mesh,
        in_specs=(
            P("dp", None), P("dp"), P(), weights, P(), P(), P(), P(), P(), hidden, hidden,
            P(), P(), rows,
        ),
        out_specs=(
            rows, rows, P(), weights, P(), P(), P(), P(), P(), hidden, hidden, P(), P(),
        ),
        check_vma=False,
    )
```

```python
from functools import partial

import jax
import jax.numpy as jnp
import ml_dtypes
import numpy as np
from jax import lax
from jax.experimental import pallas as pl
from jax.experimental.pallas import tpu as pltpu
from jax.sharding import PartitionSpec as P

HEADS = 6
HSIZE = 64
KERN = 9
ROW = 512
FEED = 256
EPS = 1e-12
MASKED = -1000000000.0
SCALE = 0.125
LANE = 128
TILES = HEADS * HSIZE // LANE
PAD = 8
CHUNK = 128
BLOCK = 256
ROOM = 58 << 20
SLOTS = 32
KEPT = SLOTS // 2
FIRST = 5
GEN_ROW = 32
AXES = ("dp", "branch")
BF = jnp.bfloat16
F32 = jnp.float32


class Links:
    def __init__(self, mesh):
        self.count = mesh.shape["dp"] * 2
        bits = self.count.bit_length() - 1
        assert mesh.shape["branch"] == 2 and self.count == 1 << bits and bits >= 5
        self.more = [tuple(range(low, min(low + 2, bits))) for low in range(5, bits, 2)]

    @staticmethod
    def plane(number, place):
        flipped = place if number & 2 == 0 else place >> 1 | (place & 1) << 1
        return number ^ (flipped & 1) ^ (flipped >> 1) << 2

    def slots(self):
        return [
            [
                self.plane(d ^ core << 1, place) ^ far << 3
                for core in range(2)
                for place in range(4)
                for far in range(4)
            ]
            for d in range(self.count)
        ]

    def send(self, value, partner):
        return lax.ppermute(value, AXES, [(d, partner(d)) for d in range(self.count)])

    def core(self, value):
        return self.send(value, lambda d: d ^ 2)

    def near(self, value, place):
        return self.send(value, lambda d: self.plane(d, place))

    def far(self, value, place):
        return self.send(value, lambda d: d ^ place << 3)

    def gather(self, piece, step):
        return jnp.concatenate([piece] + [step(piece, i) for i in range(1, 4)])

    @staticmethod
    def quarters(total):
        first, *others = total.reshape((4, -1) + total.shape[1:])
        return [first] + [other.astype(BF) for other in others]

    def scatter(self, total, step):
        total, *gives = self.quarters(total)
        for i, give in enumerate(gives, 1):
            total = total + step(give, i).astype(F32)
        return total

    def gather_chosen(self, piece, side, core_bit, rows):
        def rows_for(branch):
            begin = jnp.where(branch == 1, 0, piece.shape[1] - rows)
            return lax.dynamic_slice_in_dim(piece, begin, rows, 1)

        branches = [side ^ 1 ^ core_bit, side ^ core_bit, side ^ 1]
        others = [self.near(rows_for(branch), i) for i, branch in enumerate(branches, 1)]
        return jnp.concatenate([rows_for(side)] + others)

    def sum_more(self, total):
        me = self.number()
        for stage in self.more:
            size = 1 << len(stage)
            own = (me >> stage[0]) & (size - 1)
            parts = total.reshape((size, -1) + total.shape[1:])
            total = lax.dynamic_index_in_dim(parts, own, 0, False)
            for i in range(1, size):
                part = lax.dynamic_index_in_dim(parts, own ^ i, 0, False).astype(BF)
                total = total + self.send(part, lambda d: d ^ i << stage[0]).astype(F32)
        piece = total.astype(BF)
        for stage in reversed(self.more):
            size = 1 << len(stage)
            own = (me >> stage[0]) & (size - 1)
            parts = jnp.stack(
                [piece] + [self.send(piece, lambda d: d ^ i << stage[0]) for i in range(1, size)]
            )
            piece = jnp.concatenate(
                [lax.dynamic_index_in_dim(parts, own ^ i, 0, False) for i in range(size)]
            )
        return piece

    def gather_more(self, piece):
        for stage in reversed(self.more):
            size = 1 << len(stage)
            others = [self.send(piece, lambda d: d ^ i << stage[0]) for i in range(1, size)]
            piece = jnp.concatenate([piece] + others, 1)
        return piece

    def scatter_more(self, total):
        for stage in self.more:
            size = 1 << len(stage)
            parts = jnp.split(total, size, 1)
            total = parts[0]
            for i in range(1, size):
                total = total + self.send(
                    parts[i].astype(BF), lambda d: d ^ i << stage[0]
                ).astype(F32)
        return total

    @staticmethod
    def number():
        return lax.axis_index("dp") * 2 + lax.axis_index("branch")


def dot(left, right):
    return jnp.dot(left, right, preferred_element_type=F32)


def over_rows(left, right):
    return lax.dot_general(left, right, (((0,), (0,)), ((), ())), preferred_element_type=F32)


def by_transpose(left, right):
    return lax.dot_general(left, right, (((1,), (1,)), ((), ())), preferred_element_type=F32)


def lanes(index):
    return slice(index * LANE, (index + 1) * LANE)


def tap_columns():
    source = np.arange(2 * LANE) % LANE
    column = np.arange(TILES * KERN * LANE)
    tile, tap, lane = column // (KERN * LANE), column // LANE % KERN, column % LANE
    head = tile * 2 + lane // HSIZE
    return (source[:, None] == tap * 8 + head).astype(ml_dtypes.bfloat16)


def over_taps(field, combine):
    for shift in (64, 32, 16, 8):
        field = combine(field, pltpu.roll(field, shift, 1))
    return field


def two_parts(field):
    high = field.astype(BF)
    return high, (field - high.astype(F32)).astype(BF)


def head_only(field, head):
    lane = lax.broadcasted_iota(jnp.int32, field.shape, 1)
    return jnp.where((lane < HSIZE) == (head == 0), field, jnp.zeros_like(field))


def pick_lane(lane, choices):
    block = jnp.zeros(lane.shape, F32)
    for index, value in choices:
        block = jnp.where(lane == index, value, block)
    return block.astype(BF)


def fill_padded(pad_ref, field):
    for tile in range(pad_ref.shape[0]):
        pad_ref[tile, PAD : PAD + field.shape[0], :] = field[:, lanes(tile)]


def clear_edges(pad_ref):
    edge = jnp.zeros((pad_ref.shape[0], PAD, LANE), F32)
    pad_ref[:, :PAD, :] = edge
    pad_ref[:, pad_ref.shape[1] - PAD :, :] = edge


def deal(place_ref, sources, keep_ref, give_ref, spare_ref):
    for slot in range(SLOTS):
        target = keep_ref if slot < KEPT else spare_ref
        offset = target.shape[1] - sum(rows for _, _, rows in sources)
        for total_ref, columns, rows in sources:
            begin = pl.multiple_of(place_ref[FIRST + slot] * rows, 8)
            target[slot % KEPT, offset : offset + rows, :] = total_ref[pl.ds(begin, rows), columns]
            offset += rows
    give_ref[...] = spare_ref[...].astype(BF)


def mix_kernel(
    place_ref, length_ref, tok_ref, wq_ref, wk_ref, wv_ref, ws_ref, wc_ref, depth_ref, gen_ref,
    columns_ref, x_ref, q_ref, k_ref, v_ref, c_ref, spread_ref, span_ref, kern_ref, lse_ref,
    mixed_ref, xpad, cpad,
):
    row = pl.program_id(0)
    seq, width = tok_ref.shape
    half = q_ref.shape[1]
    length = length_ref[place_ref[0] * pl.num_programs(0) + row]

    @pl.when(row == 0)
    def _():
        clear_edges(xpad)
        clear_edges(cpad)

    spot = lax.broadcasted_iota(jnp.int32, (seq, 1), 0)
    x_f = jnp.where(spot < length, tok_ref[...].astype(F32), 0.0)
    x_in = x_f.astype(BF)
    x_ref[...] = x_in
    fill_padded(xpad, x_f)
    q_ref[...] = dot(x_in, wq_ref[...]).astype(BF)
    k_ref[...] = dot(x_in, wk_ref[...]).astype(BF)
    v_ref[...] = dot(x_in, wv_ref[...]).astype(BF)
    c_ref[...] = dot(x_in, wc_ref[...]).astype(BF)
    fill_padded(cpad, c_ref[...].astype(F32))

    for tile in range(width // LANE):
        for start in range(0, seq, CHUNK):
            total = jnp.zeros((CHUNK, LANE), F32)
            for tap in range(KERN):
                begin = PAD - KERN // 2 + tap + start
                total = total + depth_ref[tap : tap + 1, lanes(tile)] * xpad[tile, begin : begin + CHUNK, :]
            spread_ref[start : start + CHUNK, lanes(tile)] = total.astype(BF)

    span = dot(spread_ref[...], ws_ref[...])
    span_ref[...] = span
    mixed_key = (span * q_ref[...].astype(F32)).astype(BF)
    logits = dot(mixed_key, gen_ref[...])
    lane = lax.broadcasted_iota(jnp.int32, (seq, LANE), 1)
    used = (lane < KERN * 8) & (lane % 8 < HEADS)
    logits = jnp.where(used, logits, -1e30)
    expo = jnp.exp(logits - over_taps(logits, jnp.maximum))
    kern = jnp.where(used, expo / over_taps(expo, jnp.add), 0.0)
    kern_ref[...] = kern
    kern_parts = jnp.concatenate(two_parts(kern), 1)
    for tile in range(TILES):
        for start in range(0, seq, BLOCK):
            wide = dot(
                kern_parts[start : start + BLOCK],
                columns_ref[:, tile * KERN * LANE : (tile + 1) * KERN * LANE],
            )
            total = jnp.zeros((BLOCK, LANE), F32)
            for tap in range(KERN):
                begin = PAD - KERN // 2 + tap + start
                total = total + wide[:, lanes(tap)] * cpad[tile, begin : begin + BLOCK, :]
            mixed_ref[start : start + BLOCK, half + tile * LANE : half + (tile + 1) * LANE] = (
                total.astype(BF)
            )

    masked = jnp.where(spot < length, 0.0, MASKED)
    key_side = pick_lane(lane, [(0, masked)])
    query_side = pick_lane(lane, [(0, 1.0)])
    lse = jnp.zeros((seq, LANE), F32)
    for tile in range(TILES):
        query = jnp.concatenate([q_ref[:, lanes(tile)] * SCALE, query_side], 1)
        result = jnp.zeros((seq, LANE), F32)
        for head in range(2):
            key = jnp.concatenate([head_only(k_ref[:, lanes(tile)], head), key_side], 1)
            value = head_only(v_ref[:, lanes(tile)], head)
            scores = by_transpose(query, key)
            top = jnp.max(scores, 1, keepdims=True)
            expo = jnp.exp(scores - top)
            total = jnp.sum(expo, 1, keepdims=True)
            result = result + dot(expo.astype(BF), value) * (1.0 / total)
            lse = jnp.where(lane == tile * 2 + head, top + jnp.log(total), lse)
        mixed_ref[:, lanes(tile)] = result.astype(BF)
    lse_ref[...] = lse


def normalise(field):
    centred = field - jnp.mean(field, -1, keepdims=True)
    inverse = lax.rsqrt(jnp.mean(centred * centred, -1, keepdims=True) + EPS)
    return centred * inverse, inverse


def normalise_back(grad, unit, inverse):
    return inverse * (
        grad - jnp.mean(grad, -1, keepdims=True) - unit * jnp.mean(grad * unit, -1, keepdims=True)
    )


def gelu_and_slope(field):
    bell = jnp.exp(field * field * -0.5)
    step = 1.0 / (1.0 + 0.2316419 * jnp.abs(field))
    norm = 0.3989422804014327
    tail = 1.330274429 * norm
    for coefficient in (-1.821255978, 1.781477937, -0.356563782, 0.319381530):
        tail = tail * step + coefficient * norm
    tail = tail * step * bell
    share = jnp.where(field >= 0.0, 1.0 - tail, tail)
    return field * share, share + field * bell * norm


def whole(weights_ref, which, group):
    slots, rows, wide = weights_ref.shape
    units = rows // 4
    begin = (which * 2 + group) * units
    return weights_ref[:, begin : begin + units, :].reshape(slots * units, wide)


def add_units(target, which, group, value):
    slots, _, wide = target.shape
    units = value.shape[0] // slots
    begin = (which * 2 + group) * units
    target[:, begin : begin + units, :] += value.reshape(slots, units, wide)


def feed_kernel(
    place_ref, length_ref, mixed_ref, x_ref, cot_ref, wout_ref, own_ref, other_ref, gain1_ref,
    bias1_ref, gain2_ref, bias2_ref, layer_ref, pre_ref, gmixed_ref, keep_ref, give_ref,
    okeep_ref, ogive_ref, vec_ref, gives, gout, spare, activ, slope, unit_one, normed_s, into, grad_two,
):
    row = pl.program_id(0)
    seq, width = x_ref.shape
    half = width // 2
    part = activ.shape[1] // 4
    steps = ROW // seq
    length = length_ref[place_ref[0] * (pl.num_programs(0) // steps) + row // steps] - row % steps * seq
    mask = (lax.broadcasted_iota(jnp.int32, (seq, 1), 0) < length).astype(F32)

    @pl.when(row == 0)
    def _():
        keep_ref[...] = jnp.zeros_like(keep_ref)
        gives[...] = jnp.zeros_like(gives)
        gout[...] = jnp.zeros_like(gout)
        vec_ref[...] = jnp.zeros_like(vec_ref)

    unit, inverse_one = normalise(x_ref[...].astype(F32) + dot(mixed_ref[...], wout_ref[...]))
    unit_one[...] = unit
    normed = unit * gain1_ref[...] + bias1_ref[...]
    normed_s[...] = normed
    into[...] = normed.astype(BF)
    sums = []
    for group in range(2):
        cols = slice(group * half, (group + 1) * half)
        total = None
        for core, weights_ref in enumerate((own_ref, other_ref)):
            place = slice((group * 2 + core) * part, (group * 2 + core + 1) * part)
            value, rise = gelu_and_slope(by_transpose(into[:, cols], whole(weights_ref, 0, group)))
            activ[:, place] = value.astype(BF)
            slope[:, place] = rise.astype(BF)
            term = dot(activ[:, place], whole(weights_ref, 1, group))
            total = term if total is None else total + term
        sums.append(total)
    unit, inverse_two = normalise(normed_s[...] + jnp.concatenate(sums, 1))
    layer_ref[...] = ((unit * gain2_ref[...] + bias2_ref[...]) * mask).astype(BF)
    grad = cot_ref[...].astype(F32) * mask
    vec_ref[2:3, :] += jnp.sum(grad * unit, 0, keepdims=True)
    vec_ref[3:4, :] += jnp.sum(grad, 0, keepdims=True)
    grad = normalise_back(grad * gain2_ref[...], unit, inverse_two)
    grad_two[...] = grad
    grad_ffn = grad.astype(BF)
    sums = []
    for group in range(2):
        cols = slice(group * half, (group + 1) * half)
        total = None
        for core, weights_ref in enumerate((own_ref, other_ref)):
            place = slice((group * 2 + core) * part, (group * 2 + core + 1) * part)
            target = gives if core else keep_ref
            add_units(target, 1, group, over_rows(activ[:, place], grad_ffn[:, cols]))
            grad_pre = by_transpose(grad_ffn[:, cols], whole(weights_ref, 1, group))
            grad_pre = (grad_pre * slope[:, place].astype(F32)).astype(BF)
            add_units(target, 0, group, over_rows(grad_pre, into[:, cols]))
            term = dot(grad_pre, whole(weights_ref, 0, group))
            total = term if total is None else total + term
        sums.append(total)
    grad = grad_two[...] + jnp.concatenate(sums, 1)
    unit = unit_one[...]
    vec_ref[0:1, :] += jnp.sum(grad * unit, 0, keepdims=True)
    vec_ref[1:2, :] += jnp.sum(grad, 0, keepdims=True)
    grad = normalise_back(grad * gain1_ref[...], unit, inverse_one)
    pre_ref[...] = grad
    grad_mix = grad.astype(BF)
    gout[...] += over_rows(mixed_ref[...], grad_mix)
    gmixed_ref[...] = by_transpose(grad_mix, wout_ref[...]).astype(BF)

    @pl.when(row == pl.num_programs(0) - 1)
    def _():
        rows = width // SLOTS
        columns = slice(0, half), slice(half, width)
        deal(place_ref, [(gout, c, rows) for c in columns], okeep_ref, ogive_ref, spare)
        give_ref[...] = gives[...].astype(BF)


def conv_kernel(
    place_ref, length_ref, x_ref, q_ref, c_ref, spread_ref, span_ref, kern_ref, gmixed_ref, ws_ref,
    depth_ref, gen_ref, columns_ref, keep_ref, give_ref, gcv_ref, qconv_ref, xconv_ref, ggen_ref,
    gdepth_ref, cpad, gpad, spad, kpad, products, total, spare,
):
    row = pl.program_id(0)
    seq, width = x_ref.shape
    half = q_ref.shape[1]

    @pl.when(row == 0)
    def _():
        for pad in (cpad, gpad, spad, kpad):
            clear_edges(pad)
        for sums in (total, ggen_ref, gdepth_ref):
            sums[...] = jnp.zeros_like(sums)

    fill_padded(cpad, c_ref[...].astype(F32))
    fill_padded(gpad, gmixed_ref[...].astype(F32))
    kern = kern_ref[...]
    fill_padded(kpad, kern)
    query_f = q_ref[...].astype(F32)
    span = span_ref[...]
    lane = lax.broadcasted_iota(jnp.int32, (seq, LANE), 1)

    for tile in range(TILES):
        for start in range(0, seq, CHUNK):
            grad = gpad[tile, PAD + start : PAD + start + CHUNK, :]
            for tap in range(KERN):
                begin = PAD - KERN // 2 + tap + start
                products[start : start + CHUNK, lanes(tile * KERN + tap)] = (
                    grad * cpad[tile, begin : begin + CHUNK, :]
                ).astype(BF)
    grad_kern = by_transpose(products[...], columns_ref[:LANE, :])
    inner = over_taps(kern * grad_kern, jnp.add)
    grad_logits = (kern * (grad_kern - inner)).astype(BF)
    mixed_key = (span * query_f).astype(BF)
    ggen_ref[...] += over_rows(mixed_key, grad_logits)
    grad_mix = by_transpose(grad_logits, gen_ref[...])
    grad_span = (grad_mix * query_f).astype(BF)
    qconv_ref[...] = grad_mix * span
    total[:, :half] += over_rows(spread_ref[...], grad_span)
    fill_padded(spad, by_transpose(grad_span, ws_ref[...]))

    for tile in range(width // LANE):
        for start in range(0, seq, CHUNK):
            moved_sum = jnp.zeros((CHUNK, LANE), F32)
            field = x_ref[start : start + CHUNK, lanes(tile)].astype(F32)
            for tap in range(KERN):
                begin = PAD + KERN // 2 - tap + start
                grad = spad[tile, begin : begin + CHUNK, :]
                moved = (grad * field).reshape(CHUNK // 8, 8, LANE)
                gdepth_ref[tap, :, lanes(tile)] += jnp.sum(moved, 0)
                moved_sum = moved_sum + depth_ref[tap : tap + 1, lanes(tile)] * grad
            xconv_ref[start : start + CHUNK, lanes(tile)] = moved_sum

    moved = jnp.zeros((seq, LANE), F32)
    for tap in range(KERN):
        begin = PAD + KERN // 2 - tap
        moved = jnp.where(lane // 8 == tap, kpad[0, begin : begin + seq, :], moved)
    kern_parts = jnp.concatenate(two_parts(moved), 1)
    for tile in range(TILES):
        for start in range(0, seq, BLOCK):
            wide = dot(
                kern_parts[start : start + BLOCK],
                columns_ref[:, tile * KERN * LANE : (tile + 1) * KERN * LANE],
            )
            back = jnp.zeros((BLOCK, LANE), F32)
            for tap in range(KERN):
                begin = PAD + KERN // 2 - tap + start
                back = back + wide[:, lanes(tap)] * gpad[tile, begin : begin + BLOCK, :]
            gcv_ref[start : start + BLOCK, lanes(tile)] = back.astype(BF)
    total[:, half:] += over_rows(x_ref[...], gcv_ref[...])

    @pl.when(row == pl.num_programs(0) - 1)
    def _():
        rows = width // SLOTS
        deal(place_ref, [(total, slice(0, half), rows), (total, slice(half, width), rows)], keep_ref, give_ref, spare)


def put_row(target, row, value):
    half = target.shape[1]
    target[row : row + 1, :] = value[:, :half]
    target[row + 1 : row + 2, :] = value[:, half:]


def att_kernel(
    place_ref, length_ref, x_ref, q_ref, k_ref, v_ref, lse_ref, mixed_ref, gmixed_ref, qconv_ref,
    vec_ref, gdepth_ref, ggen_ref, keep_ref, give_ref, grads_ref, turned, total, small, spare,
):
    row = pl.program_id(0)
    seq, width = x_ref.shape
    half = q_ref.shape[1]
    length = length_ref[place_ref[0] * pl.num_programs(0) + row]

    @pl.when(row == 0)
    def _():
        total[...] = jnp.zeros_like(total)

    lane = lax.broadcasted_iota(jnp.int32, (seq, LANE), 1)
    spot = lax.broadcasted_iota(jnp.int32, (seq, 1), 0)
    masked = jnp.where(spot < length, 0.0, MASKED)
    key_side = pick_lane(lane, [(0, masked), (1, 1.0), (2, 1.0), (3, 1.0)])
    value_side = pick_lane(lane, [(0, 1.0), (1, 1.0)])
    for tile in range(TILES):
        query = q_ref[:, lanes(tile)] * SCALE
        grad = gmixed_ref[:, lanes(tile)]
        touch = grad.astype(F32) * mixed_ref[:, lanes(tile)].astype(F32)
        q_sum = jnp.zeros((seq, LANE), F32)
        k_sum = jnp.zeros((seq, LANE), F32)
        v_sum = jnp.zeros((seq, LANE), F32)
        for head in range(2):
            number = tile * 2 + head
            level = -jnp.sum(jnp.where(lane == number, lse_ref[...], 0.0), 1, keepdims=True)
            high = level.astype(BF).astype(F32)
            middle = (level - high).astype(BF).astype(F32)
            query_side = pick_lane(lane, [(0, 1.0), (1, high), (2, middle), (3, level - high - middle)])
            meet = -jnp.sum(head_only(touch, head), 1, keepdims=True)
            high = meet.astype(BF).astype(F32)
            grad_side = pick_lane(lane, [(0, high), (1, meet - high)])
            key_part = head_only(k_ref[:, lanes(tile)], head)
            probs = jnp.exp(
                by_transpose(
                    jnp.concatenate([query, query_side], 1),
                    jnp.concatenate([key_part, key_side], 1),
                )
            )
            grad_probs = by_transpose(
                jnp.concatenate([grad, grad_side], 1),
                jnp.concatenate([head_only(v_ref[:, lanes(tile)], head), value_side], 1),
            )
            grad_scores = (probs * grad_probs).astype(BF)
            q_sum = q_sum + dot(grad_scores, key_part)
            k_sum = k_sum + over_rows(grad_scores, head_only(query, head))
            v_sum = v_sum + over_rows(probs.astype(BF), head_only(grad, head))
        grads_ref[:, lanes(tile)] = (q_sum * SCALE + qconv_ref[:, lanes(tile)]).astype(BF)
        grads_ref[:, half + tile * LANE : half + (tile + 1) * LANE] = k_sum.astype(BF)
        grads_ref[:, 2 * half + tile * LANE : 2 * half + (tile + 1) * LANE] = v_sum.astype(BF)
    turned[...] = x_ref[...].T
    for part in range(3):
        total[part] += dot(turned[...], grads_ref[:, part * half : (part + 1) * half])

    @pl.when(row == pl.num_programs(0) - 1)
    def _():
        rows = width // SLOTS
        query, key, value = [(total.at[part], slice(0, half), rows) for part in range(3)]
        few = (small, slice(0, half), small.shape[0] // SLOTS)
        sources = [query, few, key, value]
        small[...] = jnp.zeros_like(small)
        for index in range(4):
            put_row(small, index * 2, vec_ref[index : index + 1, :])
        for tap in range(KERN):
            put_row(small, 8 + tap * 2, jnp.sum(gdepth_ref[tap], 0, keepdims=True))
        small[GEN_ROW : GEN_ROW + KERN * 8, :] = ggen_ref[...].T[: KERN * 8]
        deal(place_ref, sources, keep_ref, give_ref, spare)


def dx_kernel(
    place_ref, length_ref, grads_ref, gcv_ref, pre_ref, xconv_ref, wq_ref, wk_ref, wv_ref, wc_ref,
    out_ref,
):
    seq, half = gcv_ref.shape
    length = length_ref[place_ref[0] * pl.num_programs(0) + pl.program_id(0)]
    total = xconv_ref[...] + pre_ref[...] + by_transpose(gcv_ref[...], wc_ref[...])
    for index, weight in enumerate((wq_ref, wk_ref, wv_ref)):
        total = total + by_transpose(grads_ref[:, index * half : (index + 1) * half], weight[...])
    spot = lax.broadcasted_iota(jnp.int32, (seq, 1), 0)
    out_ref[...] = jnp.where(spot < length, total, 0.0)


def out_kernel(place_ref, length_ref, own_ref, other_ref, out_ref, part):
    half = own_ref.shape[2]
    rows = own_ref.shape[1] // 2
    for core, part_ref in enumerate((own_ref, other_ref)):
        part[...] = part_ref[...].astype(F32)
        for slot in range(KEPT):
            piece = place_ref[FIRST + core * KEPT + slot]
            here = pl.ds(pl.multiple_of(piece * rows, 8), rows)
            out_ref[here, :half] = part[slot, :rows, :]
            out_ref[here, half:] = part[slot, rows:, :]


def last_kernel(
    place_ref, length_ref, own_ref, other_ref, query_ref, branch_ref, small_ref, part
):
    width = query_ref.shape[0]
    rows = width // SLOTS
    few = small_ref.shape[0] // SLOTS
    attends = place_ref[0] == 0
    for core, part_ref in enumerate((own_ref, other_ref)):
        part[...] = part_ref[...].astype(F32)
        for slot in range(KEPT):
            piece = place_ref[FIRST + core * KEPT + slot]
            here = pl.ds(pl.multiple_of(piece * rows, 8), rows)

            def rows_at(first, second, size):
                return jnp.where(
                    attends, part[slot, first : first + size, :], part[slot, second : second + size, :]
                )

            query_ref[here, :] = rows_at(0, 2 * rows, rows)
            branch_ref[0, here, :] = rows_at(rows + few, 0, rows)
            branch_ref[1, here, :] = rows_at(2 * rows + few, rows, rows)
            here = pl.ds(pl.multiple_of(piece * few, 8), few)
            small_ref[here, :] = rows_at(rows, 3 * rows, few)


def fixed(shape):
    return pl.BlockSpec(shape, lambda *_: (0,) * len(shape), pipeline_mode=pl.Buffered(1))


def by_row(seq, width):
    return pl.BlockSpec((seq, width), lambda row, *_: (row, 0))


def array(shape, dtype):
    return jax.ShapeDtypeStruct(shape, dtype)


def call(kernel, name, rows, operands, in_specs, outs, out_specs, scratch, flops, moved):
    return pl.pallas_call(
        kernel,
        name=name,
        grid_spec=pltpu.PrefetchScalarGridSpec(
            num_scalar_prefetch=2,
            grid=(rows,),
            in_specs=in_specs,
            out_specs=out_specs,
            scratch_shapes=scratch,
        ),
        out_shape=outs,
        compiler_params=pltpu.CompilerParams(
            dimension_semantics=("arbitrary",), vmem_limit_bytes=ROOM
        ),
        cost_estimate=pl.CostEstimate(flops=flops, bytes_accessed=moved, transcendentals=0),
    )(*operands)


def total_of(terms, begin, end):
    return sum(term[begin:end].astype(F32) for term in terms)


def tie(*values):
    return lax.optimization_barrier(values)


def per_device(
    links,
    tokens,
    lengths,
    w_query,
    branch_proj,
    depth_kernel,
    kernel_gen,
    w_out,
    gain_one,
    bias_one,
    w_inner,
    w_outer,
    gain_two,
    bias_two,
    cotangent,
):
    me = links.number()
    core_bit = (me >> 1) & 1
    side = lax.axis_index("branch")
    rows = lengths.shape[0] // 2
    seq = tokens.shape[0] // lengths.shape[0]
    count = rows * seq
    width = tokens.shape[1]
    half = w_query.shape[1]
    groups = w_inner.shape[0]
    units = w_inner.shape[2] * links.count // SLOTS
    hidden = groups * units * SLOTS
    wide = width // groups

    own_w = branch_proj[0]
    far_w = links.send(lax.dynamic_index_in_dim(own_w, core_bit, 0, True), lambda d: d ^ 1)
    other = jnp.stack([2 + core_bit, 3 - core_bit])
    own = jnp.arange(2)
    place = jnp.concatenate(
        [
            side[None],
            jnp.where(side == 0, own, other),
            jnp.where(side == 0, other, own),
            jnp.array(links.slots())[me] & (SLOTS - 1),
        ]
    ).astype(jnp.int32)

    weights = jnp.stack([w_inner, w_outer]).swapaxes(2, 3).reshape((2 * groups, -1, wide))
    weights = links.gather_more(weights).reshape(1, 2 * groups * units, wide)
    weights = links.gather(weights, links.far)
    far_w, weights = tie(far_w, weights)
    near_w = links.core(far_w)

    proj = jnp.concatenate([own_w, far_w, near_w])
    depth_f = jnp.pad(depth_kernel.astype(F32), ((0, 16 - KERN), (0, 0)))
    gen = kernel_gen.reshape(half, HEADS, KERN).swapaxes(1, 2)
    gen = jnp.pad(gen, ((0, 0), (0, 16 - KERN), (0, 8 - HEADS))).reshape(half, LANE)
    columns = jnp.asarray(tap_columns())

    def weight(index):
        return pl.BlockSpec(
            (None, width, half),
            lambda row, where, length: (where[index], 0, 0),
            pipeline_mode=pl.Buffered(1),
        )

    wk, wv, ws, wc = (weight(i) for i in (1, 2, 3, 4))
    wq = fixed((width, half))
    mine = pl.BlockSpec((seq, width), lambda row, where, length: (where[0] * rows + row, 0))
    row_w, row_h, row_l = by_row(seq, width), by_row(seq, half), by_row(seq, LANE)
    row_f = by_row(FEED, width)
    vector, square_w = fixed((1, width)), fixed((width, width))
    tables = [fixed((16, width)), fixed((half, LANE)), fixed(columns.shape)]
    pad_w, pad_h = (pltpu.VMEM((w // LANE, seq + 2 * PAD, LANE), F32) for w in (width, half))
    square = count * seq * half * 2
    project = count * width * half * 2
    norm_one = [gain_one[None], bias_one[None]]
    norm_two = [gain_two[None], bias_two[None]]

    def two_halves(rows_of):
        shape = (KEPT, rows_of, half)
        return [array(shape, F32), array(shape, BF)], [fixed(shape)] * 2, pltpu.VMEM(shape, F32)

    weights = links.gather(weights, links.near)

    x_in, query, key, value, conv_value, spread, span, kern, lse, mixed = call(
        mix_kernel,
        "mix",
        rows,
        [place, lengths, tokens, w_query, proj, proj, proj, proj, depth_f, gen, columns],
        [mine, wq, wk, wv, ws, wc] + tables,
        [
            array((count, width), BF),
            array((count, half), BF),
            array((count, half), BF),
            array((count, half), BF),
            array((count, half), BF),
            array((count, width), BF),
            array((count, half), F32),
            array((count, LANE), F32),
            array((count, LANE), F32),
            array((count, width), BF),
        ],
        [row_w, row_h, row_h, row_h, row_h, row_w, row_h, row_l, row_l, row_w],
        [pad_w, pad_h],
        5 * project + 8 * square,
        16 << 20,
    )
    mixed, weights = tie(mixed, weights)
    other_weights = links.core(weights)
    ffn_rows = 2 * groups * units
    outs, specs, gives = two_halves(ffn_rows)
    out_outs, out_specs, spare = two_halves(width * 2 // SLOTS)
    layer_out, pre_grad, grad_mixed, ffn_keep, ffn_give, out_keep, out_give, vectors = call(
        feed_kernel,
        "feed",
        count // FEED,
        [place, lengths, mixed, x_in, cotangent, w_out, weights, other_weights]
        + norm_one
        + norm_two,
        [row_f, row_f, row_f, square_w] + [fixed((KEPT, ffn_rows, wide))] * 2 + [vector] * 4,
        [array((count, width), BF), array((count, width), F32), array((count, width), BF)]
        + outs
        + out_outs
        + [array((8, width), F32)],
        [row_f, row_f, row_f] + specs + out_specs + [fixed((8, width))],
        [
            gives,
            pltpu.VMEM((width, width), F32),
            spare,
            pltpu.VMEM((FEED, hidden), BF),
            pltpu.VMEM((FEED, hidden), BF),
            pltpu.VMEM((FEED, width), F32),
            pltpu.VMEM((FEED, width), F32),
            pltpu.VMEM((FEED, width), BF),
            pltpu.VMEM((FEED, width), F32),
        ],
        30 * project,
        32 << 20,
    )
    ffn_more = links.core(ffn_give)
    out_more = links.core(out_give)

    outs, specs, spare = two_halves(width * 2 // SLOTS)
    conv_keep, conv_give, grad_cv, q_conv, x_conv, grad_gen, grad_depth = call(
        conv_kernel,
        "conv",
        rows,
        [place, lengths, x_in, query, conv_value, spread, span, kern, grad_mixed, proj, depth_f]
        + [gen, columns],
        [row_w, row_h, row_h, row_w, row_h, row_l]
        + [pl.BlockSpec((seq, half), lambda row, *_: (row, 1)), ws]
        + tables,
        outs
        + [
            array((count, half), BF),
            array((count, half), F32),
            array((count, width), F32),
            array((half, LANE), F32),
            array((KERN, 8, width), F32),
        ],
        specs + [row_h, row_h, row_w, fixed((half, LANE)), fixed((KERN, 8, width))],
        [
            pad_h,
            pad_h,
            pad_w,
            pltpu.VMEM((1, seq + 2 * PAD, LANE), F32),
            pltpu.VMEM((seq, TILES * KERN * LANE), BF),
            pltpu.VMEM((width, width), F32),
            spare,
        ],
        8 * project,
        16 << 20,
    )
    conv_more = links.core(conv_give)
    ffn_more, out_more, q_conv = tie(ffn_more, out_more, q_conv)
    ffn_terms = [ffn_keep, ffn_more]
    ffn_give = total_of(ffn_terms, KEPT // 2, KEPT).astype(BF)
    out_keep, *out_gives = links.quarters(out_keep + out_more.astype(F32))
    q_conv, ffn_give, out_gives = tie(q_conv, ffn_give, out_gives)
    ffn_terms = [*ffn_terms, links.near(ffn_give, 2)]
    out_mores = [links.near(give, i) for i, give in enumerate(out_gives, 1)]
    outs, specs, spare = two_halves(width * 3 // SLOTS + 8)
    att_keep, att_give, grads = call(
        att_kernel,
        "att",
        rows,
        [place, lengths, x_in, query, key, value, lse, mixed, grad_mixed, q_conv]
        + [vectors, grad_depth, grad_gen],
        [row_w, row_h, row_h, row_h, row_l, row_h, row_h, row_h]
        + [fixed((8, width)), fixed((KERN, 8, width)), fixed((half, LANE))],
        outs + [array((count, 3 * half), BF)],
        specs + [by_row(seq, 3 * half)],
        [
            pltpu.VMEM((width, seq), BF),
            pltpu.VMEM((3, width, half), F32),
            pltpu.VMEM((SLOTS * 8, half), F32),
            spare,
        ],
        3 * project + 20 * square,
        16 << 20,
    )
    att_give, conv_more, ffn_terms, out_mores = tie(att_give, conv_more, ffn_terms, out_mores)
    att_more = links.core(att_give)
    out_sum = out_keep + sum(more.astype(F32) for more in out_mores)
    both_sum = jnp.concatenate(
        [conv_keep + conv_more.astype(F32), att_keep + att_more.astype(F32)], 1
    )
    both_keep, *both_gives = links.quarters(both_sum)
    out_keep, *out_gives = links.quarters(out_sum)
    grads, both_gives, out_gives = tie(grads, both_gives, out_gives)
    both_mores = [links.near(give, i) for i, give in enumerate(both_gives, 1)]
    out_mores = [links.far(give, i) for i, give in enumerate(out_gives, 1)]

    input_grad = call(
        dx_kernel,
        "dx",
        rows,
        [place, lengths, grads, grad_cv, pre_grad, x_conv, w_query, proj, proj, proj],
        [by_row(seq, 3 * half), row_h, row_w, row_w, wq, wk, wv, wc],
        array((count, width), F32),
        row_w,
        [],
        4 * project,
        16 << 20,
    )
    input_grad, both_mores, out_mores = tie(input_grad, both_mores, out_mores)
    out_sum = out_keep + sum(more.astype(F32) for more in out_mores)
    both_sum = both_keep + sum(more.astype(F32) for more in both_mores)
    both_keep, *both_gives = links.quarters(both_sum)
    both_mores = [links.far(give, i) for i, give in enumerate(both_gives, 1)]
    ffn_give = total_of(ffn_terms, KEPT // 4, KEPT // 2).astype(BF)
    both_gives, ffn_give = tie(both_gives, ffn_give)
    ffn_terms = [*ffn_terms, links.near(ffn_give, 1)]
    out_own = links.gather(links.sum_more(out_sum[0])[None], links.far)
    both_mores, out_own, ffn_terms = tie(both_mores, out_own, ffn_terms)
    both_sum = both_keep + sum(more.astype(F32) for more in both_mores)
    both_own = links.gather(links.sum_more(both_sum[0])[None], links.far)
    out_own = links.gather(out_own, links.near)
    both_own, out_own, ffn_terms = tie(both_own, out_own, ffn_terms)
    both_own = links.gather_chosen(both_own, side, core_bit, width * 3 // SLOTS + 8)
    ffn_sum = links.scatter(total_of(ffn_terms, 0, KEPT // 4), links.far)[0]
    out_other = links.core(out_own)
    both_own, ffn_sum, out_other = tie(both_own, ffn_sum, out_other)
    both_other = links.core(both_own)
    ffn_grads = links.scatter_more(ffn_sum.reshape(2 * groups, units, wide))
    ffn_grads = ffn_grads.swapaxes(1, 2).reshape((2,) + w_inner.shape)
    out_grad = call(
        out_kernel,
        "place_out",
        1,
        [place, lengths, out_own, out_other],
        [fixed(out_own.shape)] * 2,
        array((width, width), F32),
        square_w,
        [pltpu.VMEM(out_own.shape, F32)],
        0,
        4 << 20,
    )
    grad_query, branch_sum, small = call(
        last_kernel,
        "place",
        1,
        [place, lengths, both_own, both_other],
        [fixed(both_own.shape)] * 2,
        [
            array((width, half), F32),
            array((2, width, half), F32),
            array((SLOTS * 8, half), F32),
        ],
        [wq, fixed((2, width, half)), fixed((SLOTS * 8, half))],
        [pltpu.VMEM(both_own.shape, F32)],
        0,
        8 << 20,
    )
    vec_sum = small[:8].reshape(4, width)
    depth_sum = small[8 : 8 + 2 * KERN].reshape(KERN, width)
    gen_sum = small[GEN_ROW : GEN_ROW + KERN * 8].reshape(KERN, 8, half)[:, :HEADS]
    return (
        layer_out,
        input_grad,
        grad_query,
        branch_sum[None],
        depth_sum,
        gen_sum.transpose(2, 1, 0).reshape(kernel_gen.shape),
        out_grad,
        vec_sum[0],
        vec_sum[1],
        ffn_grads[0],
        ffn_grads[1],
        vec_sum[2],
        vec_sum[3],
    )


def solution(mesh):
    rows = P(AXES, None)
    hidden = P(None, None, AXES)
    weights = P("branch", None, None, None)
    return jax.shard_map(
        partial(per_device, Links(mesh)),
        mesh=mesh,
        in_specs=(
            P("dp", None), P("dp"), P(), weights, P(), P(), P(), P(), P(), hidden, hidden,
            P(), P(), rows,
        ),
        out_specs=(
            rows, rows, P(), weights, P(), P(), P(), P(), P(), hidden, hidden, P(), P(),
        ),
        check_vma=False,
    )
```

```python
from functools import partial

import jax
import jax.numpy as jnp
import ml_dtypes
import numpy as np
from jax import lax
from jax.experimental import pallas as pl
from jax.experimental.pallas import tpu as pltpu
from jax.sharding import PartitionSpec as P

HEADS = 6
HSIZE = 64
KERN = 9
ROW = 512
FEED = 256
EPS = 1e-12
MASKED = -1000000000.0
SCALE = 0.125
LANE = 128
TILES = HEADS * HSIZE // LANE
PAD = 8
CHUNK = 128
BLOCK = 256
ROOM = 58 << 20
SLOTS = 32
KEPT = SLOTS // 2
FIRST = 5
GEN_ROW = 32
AXES = ("dp", "branch")
BF = jnp.bfloat16
F32 = jnp.float32


class Links:
    def __init__(self, mesh):
        self.count = mesh.shape["dp"] * 2
        bits = self.count.bit_length() - 1
        assert mesh.shape["branch"] == 2 and self.count == 1 << bits and bits >= 5
        self.more = [tuple(range(low, min(low + 2, bits))) for low in range(5, bits, 2)]

    @staticmethod
    def plane(number, place):
        flipped = place if number & 2 == 0 else place >> 1 | (place & 1) << 1
        return number ^ (flipped & 1) ^ (flipped >> 1) << 2

    def slots(self):
        return [
            [
                self.plane(d ^ core << 1, place) ^ far << 3
                for core in range(2)
                for place in range(4)
                for far in range(4)
            ]
            for d in range(self.count)
        ]

    def send(self, value, partner):
        return lax.ppermute(value, AXES, [(d, partner(d)) for d in range(self.count)])

    def core(self, value):
        return self.send(value, lambda d: d ^ 2)

    def near(self, value, place):
        return self.send(value, lambda d: self.plane(d, place))

    def far(self, value, place):
        return self.send(value, lambda d: d ^ place << 3)

    def gather(self, piece, step):
        return jnp.concatenate([piece] + [step(piece, i) for i in range(1, 4)])

    @staticmethod
    def quarters(total):
        first, *others = total.reshape((4, -1) + total.shape[1:])
        return [first] + [other.astype(BF) for other in others]

    def scatter(self, total, step):
        total, *gives = self.quarters(total)
        for i, give in enumerate(gives, 1):
            total = total + step(give, i).astype(F32)
        return total

    def send_chosen(self, piece, side, core_bit, rows):
        def rows_for(branch):
            begin = jnp.where(branch == 1, 0, piece.shape[1] - rows)
            return lax.dynamic_slice_in_dim(piece, begin, rows, 1)

        branches = [side ^ 1 ^ core_bit, side ^ core_bit, side ^ 1]
        others = [self.near(rows_for(branch), i) for i, branch in enumerate(branches, 1)]
        return [rows_for(side)] + others

    def sum_more(self, total):
        me = self.number()
        for stage in self.more:
            size = 1 << len(stage)
            own = (me >> stage[0]) & (size - 1)
            parts = total.reshape((size, -1) + total.shape[1:])
            total = lax.dynamic_index_in_dim(parts, own, 0, False)
            for i in range(1, size):
                part = lax.dynamic_index_in_dim(parts, own ^ i, 0, False).astype(BF)
                total = total + self.send(part, lambda d: d ^ i << stage[0]).astype(F32)
        piece = total.astype(BF)
        for stage in reversed(self.more):
            size = 1 << len(stage)
            own = (me >> stage[0]) & (size - 1)
            parts = jnp.stack(
                [piece] + [self.send(piece, lambda d: d ^ i << stage[0]) for i in range(1, size)]
            )
            piece = jnp.concatenate(
                [lax.dynamic_index_in_dim(parts, own ^ i, 0, False) for i in range(size)]
            )
        return piece

    def gather_more(self, piece):
        for stage in reversed(self.more):
            size = 1 << len(stage)
            others = [self.send(piece, lambda d: d ^ i << stage[0]) for i in range(1, size)]
            piece = jnp.concatenate([piece] + others, 1)
        return piece

    def scatter_more(self, total):
        for stage in self.more:
            size = 1 << len(stage)
            parts = jnp.split(total, size, 1)
            total = parts[0]
            for i in range(1, size):
                total = total + self.send(
                    parts[i].astype(BF), lambda d: d ^ i << stage[0]
                ).astype(F32)
        return total

    @staticmethod
    def number():
        return lax.axis_index("dp") * 2 + lax.axis_index("branch")


def dot(left, right):
    return jnp.dot(left, right, preferred_element_type=F32)


def over_rows(left, right):
    return lax.dot_general(left, right, (((0,), (0,)), ((), ())), preferred_element_type=F32)


def by_transpose(left, right):
    return lax.dot_general(left, right, (((1,), (1,)), ((), ())), preferred_element_type=F32)


def lanes(index):
    return slice(index * LANE, (index + 1) * LANE)


def tap_columns():
    source = np.arange(2 * LANE) % LANE
    column = np.arange(TILES * KERN * LANE)
    tile, tap, lane = column // (KERN * LANE), column // LANE % KERN, column % LANE
    head = tile * 2 + lane // HSIZE
    return (source[:, None] == tap * 8 + head).astype(ml_dtypes.bfloat16)


def over_taps(field, combine):
    for shift in (64, 32, 16, 8):
        field = combine(field, pltpu.roll(field, shift, 1))
    return field


def two_parts(field):
    high = field.astype(BF)
    return high, (field - high.astype(F32)).astype(BF)


def head_only(field, head):
    lane = lax.broadcasted_iota(jnp.int32, field.shape, 1)
    return jnp.where((lane < HSIZE) == (head == 0), field, jnp.zeros_like(field))


def pick_lane(lane, choices):
    block = jnp.zeros(lane.shape, F32)
    for index, value in choices:
        block = jnp.where(lane == index, value, block)
    return block.astype(BF)


def fill_padded(pad_ref, field):
    for tile in range(pad_ref.shape[0]):
        pad_ref[tile, PAD : PAD + field.shape[0], :] = field[:, lanes(tile)]


def clear_edges(pad_ref):
    edge = jnp.zeros((pad_ref.shape[0], PAD, LANE), F32)
    pad_ref[:, :PAD, :] = edge
    pad_ref[:, pad_ref.shape[1] - PAD :, :] = edge


def deal(place_ref, sources, keep_ref, give_ref, spare_ref):
    for slot in range(SLOTS):
        target = keep_ref if slot < KEPT else spare_ref
        offset = target.shape[1] - sum(rows for _, _, rows in sources)
        for total_ref, columns, rows in sources:
            begin = pl.multiple_of(place_ref[FIRST + slot] * rows, 8)
            target[slot % KEPT, offset : offset + rows, :] = total_ref[pl.ds(begin, rows), columns]
            offset += rows
    give_ref[...] = spare_ref[...].astype(BF)


def mix_kernel(
    place_ref, length_ref, tok_ref, wq_ref, wk_ref, wv_ref, ws_ref, wc_ref, depth_ref, gen_ref,
    columns_ref, x_ref, q_ref, k_ref, v_ref, c_ref, spread_ref, span_ref, kern_ref, lse_ref,
    mixed_ref, xpad, cpad,
):
    row = pl.program_id(0)
    seq, width = tok_ref.shape
    half = q_ref.shape[1]
    length = length_ref[place_ref[0] * pl.num_programs(0) + row]

    @pl.when(row == 0)
    def _():
        clear_edges(xpad)
        clear_edges(cpad)

    spot = lax.broadcasted_iota(jnp.int32, (seq, 1), 0)
    x_f = jnp.where(spot < length, tok_ref[...].astype(F32), 0.0)
    x_in = x_f.astype(BF)
    x_ref[...] = x_in
    fill_padded(xpad, x_f)
    q_ref[...] = dot(x_in, wq_ref[...]).astype(BF)
    k_ref[...] = dot(x_in, wk_ref[...]).astype(BF)
    v_ref[...] = dot(x_in, wv_ref[...]).astype(BF)
    c_ref[...] = dot(x_in, wc_ref[...]).astype(BF)
    fill_padded(cpad, c_ref[...].astype(F32))

    for tile in range(width // LANE):
        for start in range(0, seq, CHUNK):
            total = jnp.zeros((CHUNK, LANE), F32)
            for tap in range(KERN):
                begin = PAD - KERN // 2 + tap + start
                total = total + depth_ref[tap : tap + 1, lanes(tile)] * xpad[tile, begin : begin + CHUNK, :]
            spread_ref[start : start + CHUNK, lanes(tile)] = total.astype(BF)

    span = dot(spread_ref[...], ws_ref[...])
    span_ref[...] = span
    mixed_key = (span * q_ref[...].astype(F32)).astype(BF)
    logits = dot(mixed_key, gen_ref[...])
    lane = lax.broadcasted_iota(jnp.int32, (seq, LANE), 1)
    used = (lane < KERN * 8) & (lane % 8 < HEADS)
    logits = jnp.where(used, logits, -1e30)
    expo = jnp.exp(logits - over_taps(logits, jnp.maximum))
    kern = jnp.where(used, expo / over_taps(expo, jnp.add), 0.0)
    kern_ref[...] = kern
    kern_parts = jnp.concatenate(two_parts(kern), 1)
    for tile in range(TILES):
        for start in range(0, seq, BLOCK):
            wide = dot(
                kern_parts[start : start + BLOCK],
                columns_ref[:, tile * KERN * LANE : (tile + 1) * KERN * LANE],
            )
            total = jnp.zeros((BLOCK, LANE), F32)
            for tap in range(KERN):
                begin = PAD - KERN // 2 + tap + start
                total = total + wide[:, lanes(tap)] * cpad[tile, begin : begin + BLOCK, :]
            mixed_ref[start : start + BLOCK, half + tile * LANE : half + (tile + 1) * LANE] = (
                total.astype(BF)
            )

    masked = jnp.where(spot < length, 0.0, MASKED)
    key_side = pick_lane(lane, [(0, masked)])
    query_side = pick_lane(lane, [(0, 1.0)])
    lse = jnp.zeros((seq, LANE), F32)
    for tile in range(TILES):
        query = jnp.concatenate([q_ref[:, lanes(tile)] * SCALE, query_side], 1)
        result = jnp.zeros((seq, LANE), F32)
        for head in range(2):
            key = jnp.concatenate([head_only(k_ref[:, lanes(tile)], head), key_side], 1)
            value = head_only(v_ref[:, lanes(tile)], head)
            scores = by_transpose(query, key)
            top = jnp.max(scores, 1, keepdims=True)
            expo = jnp.exp(scores - top)
            total = jnp.sum(expo, 1, keepdims=True)
            result = result + dot(expo.astype(BF), value) * (1.0 / total)
            lse = jnp.where(lane == tile * 2 + head, top + jnp.log(total), lse)
        mixed_ref[:, lanes(tile)] = result.astype(BF)
    lse_ref[...] = lse


def normalise(field):
    centred = field - jnp.mean(field, -1, keepdims=True)
    inverse = lax.rsqrt(jnp.mean(centred * centred, -1, keepdims=True) + EPS)
    return centred * inverse, inverse


def normalise_back(grad, unit, inverse):
    return inverse * (
        grad - jnp.mean(grad, -1, keepdims=True) - unit * jnp.mean(grad * unit, -1, keepdims=True)
    )


def gelu_and_slope(field):
    share = 0.5 + 0.5 * lax.erf(field * 0.7071067811865476)
    bell = jnp.exp(field * field * -0.5)
    return field * share, share + field * bell * 0.3989422804014327


def whole(weights_ref, which, group):
    slots, rows, wide = weights_ref.shape
    units = rows // 4
    begin = (which * 2 + group) * units
    return weights_ref[:, begin : begin + units, :].reshape(slots * units, wide)


def put_units(target, which, group, value):
    slots, _, wide = target.shape
    units = value.shape[0] // slots
    begin = (which * 2 + group) * units
    target[:, begin : begin + units, :] = value.reshape(slots, units, wide).astype(target.dtype)


def feed_kernel(
    place_ref, length_ref, mixed_ref, x_ref, cot_ref, wout_ref, own_ref, other_ref, gain1_ref,
    bias1_ref, gain2_ref, bias2_ref, layer_ref, pre_ref, gmixed_ref, keep_ref, give_ref,
    okeep_ref, ogive_ref, vec_ref, gout, spare, activ, ginner, slope, unit_one, normed_s, into, outof,
):
    row = pl.program_id(0)
    seq, width = x_ref.shape
    half = width // 2
    part = activ.shape[1] // 4
    here = pl.ds(pl.multiple_of(row * seq, seq), seq)
    steps = ROW // seq
    length = length_ref[place_ref[0] * (pl.num_programs(0) // steps) + row // steps] - row % steps * seq
    mask = (lax.broadcasted_iota(jnp.int32, (seq, 1), 0) < length).astype(F32)

    @pl.when(row == 0)
    def _():
        gout[...] = jnp.zeros_like(gout)
        vec_ref[...] = jnp.zeros_like(vec_ref)

    unit, inverse_one = normalise(x_ref[...].astype(F32) + dot(mixed_ref[...], wout_ref[...]))
    unit_one[...] = unit
    normed = unit * gain1_ref[...] + bias1_ref[...]
    normed_s[...] = normed
    into[here, :] = normed.astype(BF)
    sums = []
    for group in range(2):
        cols = slice(group * half, (group + 1) * half)
        total = None
        for core, weights_ref in enumerate((own_ref, other_ref)):
            place = slice((group * 2 + core) * part, (group * 2 + core + 1) * part)
            value, rise = gelu_and_slope(
                by_transpose(into[here, cols], whole(weights_ref, 0, group))
            )
            activ[here, place] = value.astype(BF)
            slope[:, place] = rise.astype(BF)
            term = dot(activ[here, place], whole(weights_ref, 1, group))
            total = term if total is None else total + term
        sums.append(total)
    unit, inverse_two = normalise(normed_s[...] + jnp.concatenate(sums, 1))
    layer_ref[...] = ((unit * gain2_ref[...] + bias2_ref[...]) * mask).astype(BF)
    grad = cot_ref[...].astype(F32) * mask
    vec_ref[2:3, :] += jnp.sum(grad * unit, 0, keepdims=True)
    vec_ref[3:4, :] += jnp.sum(grad, 0, keepdims=True)
    grad = normalise_back(grad * gain2_ref[...], unit, inverse_two)
    normed_s[...] = grad
    grad_ffn = grad.astype(BF)
    outof[here, :] = grad_ffn
    sums = []
    for group in range(2):
        cols = slice(group * half, (group + 1) * half)
        total = None
        for core, weights_ref in enumerate((own_ref, other_ref)):
            place = slice((group * 2 + core) * part, (group * 2 + core + 1) * part)
            grad_pre = by_transpose(grad_ffn[:, cols], whole(weights_ref, 1, group))
            grad_pre = (grad_pre * slope[:, place].astype(F32)).astype(BF)
            ginner[here, place] = grad_pre
            term = dot(grad_pre, whole(weights_ref, 0, group))
            total = term if total is None else total + term
        sums.append(total)
    grad = normed_s[...] + jnp.concatenate(sums, 1)
    unit = unit_one[...]
    vec_ref[0:1, :] += jnp.sum(grad * unit, 0, keepdims=True)
    vec_ref[1:2, :] += jnp.sum(grad, 0, keepdims=True)
    grad = normalise_back(grad * gain1_ref[...], unit, inverse_one)
    pre_ref[...] = grad
    grad_mix = grad.astype(BF)
    gout[...] += over_rows(mixed_ref[...], grad_mix)
    gmixed_ref[...] = by_transpose(grad_mix, wout_ref[...]).astype(BF)

    @pl.when(row == pl.num_programs(0) - 1)
    def _():
        rows = width // SLOTS
        columns = slice(0, half), slice(half, width)
        deal(place_ref, [(gout, c, rows) for c in columns], okeep_ref, ogive_ref, spare)
        for group in range(2):
            cols = slice(group * half, (group + 1) * half)
            for core, target in enumerate((keep_ref, give_ref)):
                place = slice((group * 2 + core) * part, (group * 2 + core + 1) * part)
                put_units(target, 0, group, over_rows(ginner[:, place], into[:, cols]))
                put_units(target, 1, group, over_rows(activ[:, place], outof[:, cols]))


def conv_kernel(
    place_ref, length_ref, x_ref, q_ref, c_ref, spread_ref, span_ref, kern_ref, gmixed_ref, ws_ref,
    depth_ref, gen_ref, columns_ref, keep_ref, give_ref, gcv_ref, qconv_ref, xconv_ref, ggen_ref,
    gdepth_ref, cpad, gpad, spad, kpad, products, total, spare,
):
    row = pl.program_id(0)
    seq, width = x_ref.shape
    half = q_ref.shape[1]

    @pl.when(row == 0)
    def _():
        for pad in (cpad, gpad, spad, kpad):
            clear_edges(pad)
        for sums in (total, ggen_ref, gdepth_ref):
            sums[...] = jnp.zeros_like(sums)

    fill_padded(cpad, c_ref[...].astype(F32))
    fill_padded(gpad, gmixed_ref[...].astype(F32))
    kern = kern_ref[...]
    fill_padded(kpad, kern)
    query_f = q_ref[...].astype(F32)
    span = span_ref[...]
    lane = lax.broadcasted_iota(jnp.int32, (seq, LANE), 1)

    for tile in range(TILES):
        for start in range(0, seq, CHUNK):
            grad = gpad[tile, PAD + start : PAD + start + CHUNK, :]
            for tap in range(KERN):
                begin = PAD - KERN // 2 + tap + start
                products[start : start + CHUNK, lanes(tile * KERN + tap)] = (
                    grad * cpad[tile, begin : begin + CHUNK, :]
                ).astype(BF)
    grad_kern = by_transpose(products[...], columns_ref[:LANE, :])
    inner = over_taps(kern * grad_kern, jnp.add)
    grad_logits = (kern * (grad_kern - inner)).astype(BF)
    mixed_key = (span * query_f).astype(BF)
    ggen_ref[...] += over_rows(mixed_key, grad_logits)
    grad_mix = by_transpose(grad_logits, gen_ref[...])
    grad_span = (grad_mix * query_f).astype(BF)
    qconv_ref[...] = grad_mix * span
    total[:, :half] += over_rows(spread_ref[...], grad_span)
    fill_padded(spad, by_transpose(grad_span, ws_ref[...]))

    for tile in range(width // LANE):
        for start in range(0, seq, CHUNK):
            moved_sum = jnp.zeros((CHUNK, LANE), F32)
            field = x_ref[start : start + CHUNK, lanes(tile)].astype(F32)
            for tap in range(KERN):
                begin = PAD + KERN // 2 - tap + start
                grad = spad[tile, begin : begin + CHUNK, :]
                moved = (grad * field).reshape(CHUNK // 8, 8, LANE)
                gdepth_ref[tap, :, lanes(tile)] += jnp.sum(moved, 0)
                moved_sum = moved_sum + depth_ref[tap : tap + 1, lanes(tile)] * grad
            xconv_ref[start : start + CHUNK, lanes(tile)] = moved_sum

    moved = jnp.zeros((seq, LANE), F32)
    for tap in range(KERN):
        begin = PAD + KERN // 2 - tap
        moved = jnp.where(lane // 8 == tap, kpad[0, begin : begin + seq, :], moved)
    kern_parts = jnp.concatenate(two_parts(moved), 1)
    for tile in range(TILES):
        for start in range(0, seq, BLOCK):
            wide = dot(
                kern_parts[start : start + BLOCK],
                columns_ref[:, tile * KERN * LANE : (tile + 1) * KERN * LANE],
            )
            back = jnp.zeros((BLOCK, LANE), F32)
            for tap in range(KERN):
                begin = PAD + KERN // 2 - tap + start
                back = back + wide[:, lanes(tap)] * gpad[tile, begin : begin + BLOCK, :]
            gcv_ref[start : start + BLOCK, lanes(tile)] = back.astype(BF)
    total[:, half:] += over_rows(x_ref[...], gcv_ref[...])

    @pl.when(row == pl.num_programs(0) - 1)
    def _():
        rows = width // SLOTS
        deal(place_ref, [(total, slice(0, half), rows), (total, slice(half, width), rows)], keep_ref, give_ref, spare)


def put_row(target, row, value):
    half = target.shape[1]
    target[row : row + 1, :] = value[:, :half]
    target[row + 1 : row + 2, :] = value[:, half:]


def att_kernel(
    place_ref, length_ref, x_ref, q_ref, k_ref, v_ref, lse_ref, mixed_ref, gmixed_ref, qconv_ref,
    vec_ref, gdepth_ref, ggen_ref, keep_ref, give_ref, grads_ref, turned, total, small, spare,
):
    row = pl.program_id(0)
    seq, width = x_ref.shape
    half = q_ref.shape[1]
    length = length_ref[place_ref[0] * pl.num_programs(0) + row]

    @pl.when(row == 0)
    def _():
        total[...] = jnp.zeros_like(total)

    lane = lax.broadcasted_iota(jnp.int32, (seq, LANE), 1)
    spot = lax.broadcasted_iota(jnp.int32, (seq, 1), 0)
    masked = jnp.where(spot < length, 0.0, MASKED)
    key_side = pick_lane(lane, [(0, masked), (1, 1.0), (2, 1.0), (3, 1.0)])
    value_side = pick_lane(lane, [(0, 1.0), (1, 1.0)])
    for tile in range(TILES):
        query = q_ref[:, lanes(tile)] * SCALE
        grad = gmixed_ref[:, lanes(tile)]
        touch = grad.astype(F32) * mixed_ref[:, lanes(tile)].astype(F32)
        q_sum = jnp.zeros((seq, LANE), F32)
        k_sum = jnp.zeros((seq, LANE), F32)
        v_sum = jnp.zeros((seq, LANE), F32)
        for head in range(2):
            number = tile * 2 + head
            level = -jnp.sum(jnp.where(lane == number, lse_ref[...], 0.0), 1, keepdims=True)
            high = level.astype(BF).astype(F32)
            middle = (level - high).astype(BF).astype(F32)
            query_side = pick_lane(lane, [(0, 1.0), (1, high), (2, middle), (3, level - high - middle)])
            meet = -jnp.sum(head_only(touch, head), 1, keepdims=True)
            high = meet.astype(BF).astype(F32)
            grad_side = pick_lane(lane, [(0, high), (1, meet - high)])
            key_part = head_only(k_ref[:, lanes(tile)], head)
            probs = jnp.exp(
                by_transpose(
                    jnp.concatenate([query, query_side], 1),
                    jnp.concatenate([key_part, key_side], 1),
                )
            )
            grad_probs = by_transpose(
                jnp.concatenate([grad, grad_side], 1),
                jnp.concatenate([head_only(v_ref[:, lanes(tile)], head), value_side], 1),
            )
            grad_scores = (probs * grad_probs).astype(BF)
            q_sum = q_sum + dot(grad_scores, key_part)
            k_sum = k_sum + over_rows(grad_scores, head_only(query, head))
            v_sum = v_sum + over_rows(probs.astype(BF), head_only(grad, head))
        grads_ref[:, lanes(tile)] = (q_sum * SCALE + qconv_ref[:, lanes(tile)]).astype(BF)
        grads_ref[:, half + tile * LANE : half + (tile + 1) * LANE] = k_sum.astype(BF)
        grads_ref[:, 2 * half + tile * LANE : 2 * half + (tile + 1) * LANE] = v_sum.astype(BF)
    turned[...] = x_ref[...].T
    for part in range(3):
        total[part] += dot(turned[...], grads_ref[:, part * half : (part + 1) * half])

    @pl.when(row == pl.num_programs(0) - 1)
    def _():
        rows = width // SLOTS
        query, key, value = [(total.at[part], slice(0, half), rows) for part in range(3)]
        few = (small, slice(0, half), small.shape[0] // SLOTS)
        sources = [query, few, key, value]
        small[...] = jnp.zeros_like(small)
        for index in range(4):
            put_row(small, index * 2, vec_ref[index : index + 1, :])
        for tap in range(KERN):
            put_row(small, 8 + tap * 2, jnp.sum(gdepth_ref[tap], 0, keepdims=True))
        small[GEN_ROW : GEN_ROW + KERN * 8, :] = ggen_ref[...].T[: KERN * 8]
        deal(place_ref, sources, keep_ref, give_ref, spare)


def dx_kernel(
    place_ref, length_ref, grads_ref, gcv_ref, pre_ref, xconv_ref, wq_ref, wk_ref, wv_ref, wc_ref,
    out_ref,
):
    seq, half = gcv_ref.shape
    length = length_ref[place_ref[0] * pl.num_programs(0) + pl.program_id(0)]
    total = xconv_ref[...] + pre_ref[...] + by_transpose(gcv_ref[...], wc_ref[...])
    for index, weight in enumerate((wq_ref, wk_ref, wv_ref)):
        total = total + by_transpose(grads_ref[:, index * half : (index + 1) * half], weight[...])
    spot = lax.broadcasted_iota(jnp.int32, (seq, 1), 0)
    out_ref[...] = jnp.where(spot < length, total, 0.0)


def out_kernel(place_ref, length_ref, own_ref, other_ref, out_ref, part):
    half = own_ref.shape[2]
    rows = own_ref.shape[1] // 2
    for core, part_ref in enumerate((own_ref, other_ref)):
        part[...] = part_ref[...].astype(F32)
        for slot in range(KEPT):
            piece = place_ref[FIRST + core * KEPT + slot]
            here = pl.ds(pl.multiple_of(piece * rows, 8), rows)
            out_ref[here, :half] = part[slot, :rows, :]
            out_ref[here, half:] = part[slot, rows:, :]


def last_kernel(
    place_ref, length_ref, own_ref, other_ref, query_ref, branch_ref, depth_ref, gen_ref, gain1_ref,
    bias1_ref, gain2_ref, bias2_ref, small, part,
):
    width = query_ref.shape[0]
    rows = width // SLOTS
    few = small.shape[0] // SLOTS
    attends = place_ref[0] == 0
    for core, part_ref in enumerate((own_ref, other_ref)):
        part[...] = part_ref[...].astype(F32)
        for slot in range(KEPT):
            piece = place_ref[FIRST + core * KEPT + slot]
            here = pl.ds(pl.multiple_of(piece * rows, 8), rows)

            def rows_at(first, second, size):
                return jnp.where(
                    attends, part[slot, first : first + size, :], part[slot, second : second + size, :]
                )

            query_ref[here, :] = rows_at(0, 2 * rows, rows)
            branch_ref[0, here, :] = rows_at(rows + few, 0, rows)
            branch_ref[1, here, :] = rows_at(2 * rows + few, rows, rows)
            here = pl.ds(pl.multiple_of(piece * few, 8), few)
            small[here, :] = rows_at(rows, 3 * rows, few)

    def wide_row(row):
        return jnp.concatenate([small[row : row + 1, :], small[row + 1 : row + 2, :]], 1)

    for index, vector_ref in enumerate((gain1_ref, bias1_ref, gain2_ref, bias2_ref)):
        vector_ref[...] = wide_row(index * 2).reshape(vector_ref.shape)
    for tap in range(KERN):
        depth_ref[tap : tap + 1, :] = wide_row(8 + tap * 2)
    column = lax.broadcasted_iota(jnp.int32, (gen_ref.shape[0], LANE), 0)
    source = lax.broadcasted_iota(jnp.int32, (gen_ref.shape[0], LANE), 1)
    order = (source == column % KERN * 8 + column // KERN).astype(BF)
    gen_ref[...] = dot(order, small[GEN_ROW : GEN_ROW + LANE, :].astype(BF))


def fixed(shape):
    return pl.BlockSpec(shape, lambda *_: (0,) * len(shape), pipeline_mode=pl.Buffered(1))


def by_row(seq, width):
    return pl.BlockSpec((seq, width), lambda row, *_: (row, 0))


def array(shape, dtype):
    return jax.ShapeDtypeStruct(shape, dtype)


def call(kernel, name, rows, operands, in_specs, outs, out_specs, scratch, flops, moved):
    return pl.pallas_call(
        kernel,
        name=name,
        grid_spec=pltpu.PrefetchScalarGridSpec(
            num_scalar_prefetch=2,
            grid=(rows,),
            in_specs=in_specs,
            out_specs=out_specs,
            scratch_shapes=scratch,
        ),
        out_shape=outs,
        compiler_params=pltpu.CompilerParams(
            dimension_semantics=("arbitrary",), vmem_limit_bytes=ROOM
        ),
        cost_estimate=pl.CostEstimate(flops=flops, bytes_accessed=moved, transcendentals=0),
    )(*operands)


def total_of(terms, begin, end):
    return sum(term[begin:end].astype(F32) for term in terms)


def tie(*values):
    return lax.optimization_barrier(values)


def per_device(
    links,
    tokens,
    lengths,
    w_query,
    branch_proj,
    depth_kernel,
    kernel_gen,
    w_out,
    gain_one,
    bias_one,
    w_inner,
    w_outer,
    gain_two,
    bias_two,
    cotangent,
):
    me = links.number()
    core_bit = (me >> 1) & 1
    side = lax.axis_index("branch")
    rows = lengths.shape[0] // 2
    seq = tokens.shape[0] // lengths.shape[0]
    count = rows * seq
    width = tokens.shape[1]
    half = w_query.shape[1]
    groups = w_inner.shape[0]
    units = w_inner.shape[2] * links.count // SLOTS
    hidden = groups * units * SLOTS
    wide = width // groups

    own_w = branch_proj[0]
    far_w = links.send(lax.dynamic_index_in_dim(own_w, core_bit, 0, True), lambda d: d ^ 1)
    other = jnp.stack([2 + core_bit, 3 - core_bit])
    own = jnp.arange(2)
    place = jnp.concatenate(
        [
            side[None],
            jnp.where(side == 0, own, other),
            jnp.where(side == 0, other, own),
            jnp.array(links.slots())[me] & (SLOTS - 1),
        ]
    ).astype(jnp.int32)

    weights = jnp.stack([w_inner, w_outer]).swapaxes(2, 3).reshape((2 * groups, -1, wide))
    weights = links.gather_more(weights).reshape(1, 2 * groups * units, wide)
    weights = links.gather(weights, links.far)
    far_w, weights = tie(far_w, weights)
    near_w = links.core(far_w)

    proj = jnp.concatenate([own_w, far_w, near_w])
    depth_f = jnp.pad(depth_kernel.astype(F32), ((0, 16 - KERN), (0, 0)))
    gen = kernel_gen.reshape(half, HEADS, KERN).swapaxes(1, 2)
    gen = jnp.pad(gen, ((0, 0), (0, 16 - KERN), (0, 8 - HEADS))).reshape(half, LANE)
    columns = jnp.asarray(tap_columns())

    def weight(index):
        return pl.BlockSpec(
            (None, width, half),
            lambda row, where, length: (where[index], 0, 0),
            pipeline_mode=pl.Buffered(1),
        )

    wk, wv, ws, wc = (weight(i) for i in (1, 2, 3, 4))
    wq = fixed((width, half))
    mine = pl.BlockSpec((seq, width), lambda row, where, length: (where[0] * rows + row, 0))
    row_w, row_h, row_l = by_row(seq, width), by_row(seq, half), by_row(seq, LANE)
    row_f = by_row(FEED, width)
    vector, square_w = fixed((1, width)), fixed((width, width))
    tables = [fixed((16, width)), fixed((half, LANE)), fixed(columns.shape)]
    pad_w, pad_h = (pltpu.VMEM((w // LANE, seq + 2 * PAD, LANE), F32) for w in (width, half))
    square = count * seq * half * 2
    project = count * width * half * 2
    norm_one = [gain_one[None], bias_one[None]]
    norm_two = [gain_two[None], bias_two[None]]

    def two_halves(rows_of):
        shape = (KEPT, rows_of, half)
        return [array(shape, F32), array(shape, BF)], [fixed(shape)] * 2, pltpu.VMEM(shape, F32)

    weights = links.gather(weights, links.near)

    x_in, query, key, value, conv_value, spread, span, kern, lse, mixed = call(
        mix_kernel,
        "mix",
        rows,
        [place, lengths, tokens, w_query, proj, proj, proj, proj, depth_f, gen, columns],
        [mine, wq, wk, wv, ws, wc] + tables,
        [
            array((count, width), BF),
            array((count, half), BF),
            array((count, half), BF),
            array((count, half), BF),
            array((count, half), BF),
            array((count, width), BF),
            array((count, half), F32),
            array((count, LANE), F32),
            array((count, LANE), F32),
            array((count, width), BF),
        ],
        [row_w, row_h, row_h, row_h, row_h, row_w, row_h, row_l, row_l, row_w],
        [pad_w, pad_h],
        5 * project + 8 * square,
        16 << 20,
    )
    mixed, weights = tie(mixed, weights)
    other_weights = links.core(weights)
    ffn_rows = 2 * groups * units
    outs, specs, _ = two_halves(ffn_rows)
    out_outs, out_specs, spare = two_halves(width * 2 // SLOTS)
    layer_out, pre_grad, grad_mixed, ffn_keep, ffn_give, out_keep, out_give, vectors = call(
        feed_kernel,
        "feed",
        count // FEED,
        [place, lengths, mixed, x_in, cotangent, w_out, weights, other_weights]
        + norm_one
        + norm_two,
        [row_f, row_f, row_f, square_w] + [fixed((KEPT, ffn_rows, wide))] * 2 + [vector] * 4,
        [array((count, width), BF), array((count, width), F32), array((count, width), BF)]
        + outs
        + out_outs
        + [array((8, width), F32)],
        [row_f, row_f, row_f] + specs + out_specs + [fixed((8, width))],
        [
            pltpu.VMEM((width, width), F32),
            spare,
            pltpu.VMEM((count, hidden), BF),
            pltpu.VMEM((count, hidden), BF),
            pltpu.VMEM((FEED, hidden), BF),
            pltpu.VMEM((FEED, width), F32),
            pltpu.VMEM((FEED, width), F32),
            pltpu.VMEM((count, width), BF),
            pltpu.VMEM((count, width), BF),
        ],
        30 * project,
        32 << 20,
    )
    ffn_more = links.core(ffn_give)
    out_more = links.core(out_give)

    outs, specs, spare = two_halves(width * 2 // SLOTS)
    conv_keep, conv_give, grad_cv, q_conv, x_conv, grad_gen, grad_depth = call(
        conv_kernel,
        "conv",
        rows,
        [place, lengths, x_in, query, conv_value, spread, span, kern, grad_mixed, proj, depth_f]
        + [gen, columns],
        [row_w, row_h, row_h, row_w, row_h, row_l]
        + [pl.BlockSpec((seq, half), lambda row, *_: (row, 1)), ws]
        + tables,
        outs
        + [
            array((count, half), BF),
            array((count, half), F32),
            array((count, width), F32),
            array((half, LANE), F32),
            array((KERN, 8, width), F32),
        ],
        specs + [row_h, row_h, row_w, fixed((half, LANE)), fixed((KERN, 8, width))],
        [
            pad_h,
            pad_h,
            pad_w,
            pltpu.VMEM((1, seq + 2 * PAD, LANE), F32),
            pltpu.VMEM((seq, TILES * KERN * LANE), BF),
            pltpu.VMEM((width, width), F32),
            spare,
        ],
        8 * project,
        16 << 20,
    )
    conv_more = links.core(conv_give)
    ffn_more, out_more, q_conv = tie(ffn_more, out_more, q_conv)
    ffn_terms = [ffn_keep, ffn_more]
    ffn_give = total_of(ffn_terms, KEPT // 2, KEPT).astype(BF)
    out_keep, *out_gives = links.quarters(out_keep + out_more.astype(F32))
    q_conv, ffn_give, out_gives = tie(q_conv, ffn_give, out_gives)
    ffn_terms = [*ffn_terms, links.near(ffn_give, 2)]
    out_mores = [links.near(give, i) for i, give in enumerate(out_gives, 1)]
    outs, specs, spare = two_halves(width * 3 // SLOTS + 8)
    att_keep, att_give, grads = call(
        att_kernel,
        "att",
        rows,
        [place, lengths, x_in, query, key, value, lse, mixed, grad_mixed, q_conv]
        + [vectors, grad_depth, grad_gen],
        [row_w, row_h, row_h, row_h, row_l, row_h, row_h, row_h]
        + [fixed((8, width)), fixed((KERN, 8, width)), fixed((half, LANE))],
        outs + [array((count, 3 * half), BF)],
        specs + [by_row(seq, 3 * half)],
        [
            pltpu.VMEM((width, seq), BF),
            pltpu.VMEM((3, width, half), F32),
            pltpu.VMEM((SLOTS * 8, half), F32),
            spare,
        ],
        3 * project + 20 * square,
        16 << 20,
    )
    att_give, conv_more, ffn_terms, out_mores = tie(att_give, conv_more, ffn_terms, out_mores)
    att_more = links.core(att_give)
    out_sum = out_keep + sum(more.astype(F32) for more in out_mores)
    both_sum = jnp.concatenate(
        [conv_keep + conv_more.astype(F32), att_keep + att_more.astype(F32)], 1
    )
    both_keep, *both_gives = links.quarters(both_sum)
    out_keep, *out_gives = links.quarters(out_sum)
    grads, both_gives, out_gives = tie(grads, both_gives, out_gives)
    both_mores = [links.near(give, i) for i, give in enumerate(both_gives, 1)]
    out_mores = [links.far(give, i) for i, give in enumerate(out_gives, 1)]

    input_grad = call(
        dx_kernel,
        "dx",
        rows,
        [place, lengths, grads, grad_cv, pre_grad, x_conv, w_query, proj, proj, proj],
        [by_row(seq, 3 * half), row_h, row_w, row_w, wq, wk, wv, wc],
        array((count, width), F32),
        row_w,
        [],
        4 * project,
        16 << 20,
    )
    input_grad, both_mores, out_mores = tie(input_grad, both_mores, out_mores)
    out_sum = out_keep + sum(more.astype(F32) for more in out_mores)
    both_sum = both_keep + sum(more.astype(F32) for more in both_mores)
    both_keep, *both_gives = links.quarters(both_sum)
    ffn_give = total_of(ffn_terms, KEPT // 4, KEPT // 2).astype(BF)
    out_piece = links.sum_more(out_sum[0])[None]
    joined = [jnp.concatenate([give, out_piece], 1) for give in both_gives]
    joined, ffn_give = tie(joined, ffn_give)
    joined = [links.far(give, i) for i, give in enumerate(joined, 1)]
    ffn_terms = [*ffn_terms, links.near(ffn_give, 1)]
    joined, ffn_terms = tie(joined, ffn_terms)
    cut = both_keep.shape[1]
    out_own = jnp.concatenate([out_piece] + [more[:, cut:] for more in joined])
    both_sum = both_keep + sum(more[:, :cut].astype(F32) for more in joined)
    both_own = links.gather(links.sum_more(both_sum[0])[None], links.far)
    out_own = links.gather(out_own, links.near)
    both_own, out_own = tie(both_own, out_own)
    chosen = links.send_chosen(both_own, side, core_bit, width * 3 // SLOTS + 8)
    out_other = links.core(out_own)
    chosen[1], ffn_terms = tie(chosen[1], ffn_terms)
    ffn_keep, *ffn_gives = links.quarters(total_of(ffn_terms, 0, KEPT // 4))
    ffn_mores = [links.far(give, i) for i, give in enumerate(ffn_gives, 1)]
    both_own = jnp.concatenate(chosen)
    both_own, out_other, ffn_gives = tie(both_own, out_other, ffn_gives)
    both_other = links.core(both_own)
    out_grad = call(
        out_kernel,
        "place_out",
        1,
        [place, lengths, out_own, out_other],
        [fixed(out_own.shape)] * 2,
        array((width, width), F32),
        square_w,
        [pltpu.VMEM(out_own.shape, F32)],
        0,
        4 << 20,
    )
    grad_query, branch_sum, grad_depth, grad_gen, *vectors = call(
        last_kernel,
        "place",
        1,
        [place, lengths, both_own, both_other],
        [fixed(both_own.shape)] * 2,
        [
            array((width, half), F32),
            array((2, width, half), F32),
            array((KERN, width), F32),
            array(kernel_gen.shape[::-1], F32),
        ]
        + [array((width,), F32)] * 4,
        [wq, fixed((2, width, half)), fixed((KERN, width)), fixed(kernel_gen.shape[::-1])]
        + [fixed((width,))] * 4,
        [pltpu.VMEM((SLOTS * 8, half), F32), pltpu.VMEM(both_own.shape, F32)],
        0,
        8 << 20,
    )
    grad_query, ffn_mores = tie(grad_query, ffn_mores)
    ffn_sum = (ffn_keep + sum(more.astype(F32) for more in ffn_mores))[0]
    ffn_grads = links.scatter_more(ffn_sum.reshape(2 * groups, units, wide))
    ffn_grads = ffn_grads.swapaxes(1, 2).reshape((2,) + w_inner.shape)
    grad_gain_one, grad_bias_one, grad_gain_two, grad_bias_two = vectors
    return (
        layer_out,
        input_grad,
        grad_query,
        branch_sum[None],
        grad_depth,
        grad_gen.T,
        out_grad,
        grad_gain_one,
        grad_bias_one,
        ffn_grads[0],
        ffn_grads[1],
        grad_gain_two,
        grad_bias_two,
    )


def solution(mesh):
    rows = P(AXES, None)
    hidden = P(None, None, AXES)
    weights = P("branch", None, None, None)
    return jax.shard_map(
        partial(per_device, Links(mesh)),
        mesh=mesh,
        in_specs=(
            P("dp", None), P("dp"), P(), weights, P(), P(), P(), P(), P(), hidden, hidden,
            P(), P(), rows,
        ),
        out_specs=(
            rows, rows, P(), weights, P(), P(), P(), P(), P(), hidden, hidden, P(), P(),
        ),
        check_vma=False,
    )
```

```python
from functools import partial

import jax
import jax.numpy as jnp
import ml_dtypes
import numpy as np
from jax import lax
from jax.experimental import pallas as pl
from jax.experimental.pallas import tpu as pltpu
from jax.sharding import PartitionSpec as P

HEADS = 6
HSIZE = 64
KERN = 9
ROW = 512
FEED = 256
EPS = 1e-12
MASKED = -1000000000.0
SCALE = 0.125
LANE = 128
TILES = HEADS * HSIZE // LANE
PAD = 8
CHUNK = 128
BLOCK = 256
ROOM = 58 << 20
FEED_ROOM = 48 << 20
SLOTS = 32
KEPT = SLOTS // 2
FIRST = 5
GEN_ROW = 32
AXES = ("dp", "branch")
BF = jnp.bfloat16
F32 = jnp.float32


class Links:
    def __init__(self, mesh):
        self.count = mesh.shape["dp"] * 2
        bits = self.count.bit_length() - 1
        assert mesh.shape["branch"] == 2 and self.count == 1 << bits and bits >= 5
        self.more = [tuple(range(low, min(low + 2, bits))) for low in range(5, bits, 2)]

    @staticmethod
    def plane(number, place):
        flipped = place if number & 2 == 0 else place >> 1 | (place & 1) << 1
        return number ^ (flipped & 1) ^ (flipped >> 1) << 2

    def slots(self):
        return [
            [
                self.plane(d ^ core << 1, place) ^ far << 3
                for core in range(2)
                for place in range(4)
                for far in range(4)
            ]
            for d in range(self.count)
        ]

    def send(self, value, partner):
        return lax.ppermute(value, AXES, [(d, partner(d)) for d in range(self.count)])

    def core(self, value):
        return self.send(value, lambda d: d ^ 2)

    def near(self, value, place):
        return self.send(value, lambda d: self.plane(d, place))

    def far(self, value, place):
        return self.send(value, lambda d: d ^ place << 3)

    def gather(self, piece, step):
        return jnp.concatenate([piece] + [step(piece, i) for i in range(1, 4)])

    @staticmethod
    def quarters(total):
        first, *others = total.reshape((4, -1) + total.shape[1:])
        return [first] + [other.astype(BF) for other in others]

    def scatter(self, total, step):
        total, *gives = self.quarters(total)
        for i, give in enumerate(gives, 1):
            total = total + step(give, i).astype(F32)
        return total

    def send_chosen(self, piece, side, core_bit, rows):
        def rows_for(branch):
            begin = jnp.where(branch == 1, 0, piece.shape[1] - rows)
            return lax.dynamic_slice_in_dim(piece, begin, rows, 1)

        branches = [side ^ 1 ^ core_bit, side ^ core_bit, side ^ 1]
        others = [self.near(rows_for(branch), i) for i, branch in enumerate(branches, 1)]
        return [rows_for(side)] + others

    def sum_more(self, total):
        me = self.number()
        for stage in self.more:
            size = 1 << len(stage)
            own = (me >> stage[0]) & (size - 1)
            parts = total.reshape((size, -1) + total.shape[1:])
            total = lax.dynamic_index_in_dim(parts, own, 0, False)
            for i in range(1, size):
                part = lax.dynamic_index_in_dim(parts, own ^ i, 0, False).astype(BF)
                total = total + self.send(part, lambda d: d ^ i << stage[0]).astype(F32)
        piece = total.astype(BF)
        for stage in reversed(self.more):
            size = 1 << len(stage)
            own = (me >> stage[0]) & (size - 1)
            parts = jnp.stack(
                [piece] + [self.send(piece, lambda d: d ^ i << stage[0]) for i in range(1, size)]
            )
            piece = jnp.concatenate(
                [lax.dynamic_index_in_dim(parts, own ^ i, 0, False) for i in range(size)]
            )
        return piece

    def gather_more(self, piece):
        for stage in reversed(self.more):
            size = 1 << len(stage)
            others = [self.send(piece, lambda d: d ^ i << stage[0]) for i in range(1, size)]
            piece = jnp.concatenate([piece] + others, 1)
        return piece

    def scatter_more(self, total):
        for stage in self.more:
            size = 1 << len(stage)
            parts = jnp.split(total, size, 1)
            total = parts[0]
            for i in range(1, size):
                total = total + self.send(
                    parts[i].astype(BF), lambda d: d ^ i << stage[0]
                ).astype(F32)
        return total

    @staticmethod
    def number():
        return lax.axis_index("dp") * 2 + lax.axis_index("branch")


def dot(left, right):
    return jnp.dot(left, right, preferred_element_type=F32)


def over_rows(left, right):
    return lax.dot_general(left, right, (((0,), (0,)), ((), ())), preferred_element_type=F32)


def by_transpose(left, right):
    return lax.dot_general(left, right, (((1,), (1,)), ((), ())), preferred_element_type=F32)


def lanes(index):
    return slice(index * LANE, (index + 1) * LANE)


def tap_columns():
    source = np.arange(2 * LANE) % LANE
    column = np.arange(TILES * KERN * LANE)
    tile, tap, lane = column // (KERN * LANE), column // LANE % KERN, column % LANE
    head = tile * 2 + lane // HSIZE
    return (source[:, None] == tap * 8 + head).astype(ml_dtypes.bfloat16)


def over_taps(field, combine):
    for shift in (64, 32, 16, 8):
        field = combine(field, pltpu.roll(field, shift, 1))
    return field


def two_parts(field):
    high = field.astype(BF)
    return high, (field - high.astype(F32)).astype(BF)


def head_only(field, head):
    lane = lax.broadcasted_iota(jnp.int32, field.shape, 1)
    return jnp.where((lane < HSIZE) == (head == 0), field, jnp.zeros_like(field))


def pick_lane(lane, choices):
    block = jnp.zeros(lane.shape, F32)
    for index, value in choices:
        block = jnp.where(lane == index, value, block)
    return block.astype(BF)


def fill_padded(pad_ref, field):
    for tile in range(pad_ref.shape[0]):
        pad_ref[tile, PAD : PAD + field.shape[0], :] = field[:, lanes(tile)]


def clear_edges(pad_ref):
    edge = jnp.zeros((pad_ref.shape[0], PAD, LANE), F32)
    pad_ref[:, :PAD, :] = edge
    pad_ref[:, pad_ref.shape[1] - PAD :, :] = edge


def deal(place_ref, sources, keep_ref, give_ref, spare_ref):
    for slot in range(SLOTS):
        target = keep_ref if slot < KEPT else spare_ref
        offset = target.shape[1] - sum(rows for _, _, rows in sources)
        for total_ref, columns, rows in sources:
            begin = pl.multiple_of(place_ref[FIRST + slot] * rows, 8)
            target[slot % KEPT, offset : offset + rows, :] = total_ref[pl.ds(begin, rows), columns]
            offset += rows
    give_ref[...] = spare_ref[...].astype(BF)


def mix_kernel(
    place_ref, length_ref, tok_ref, wq_ref, wk_ref, wv_ref, ws_ref, wc_ref, depth_ref, gen_ref,
    columns_ref, x_ref, q_ref, k_ref, v_ref, c_ref, spread_ref, span_ref, kern_ref, lse_ref,
    mixed_ref, xpad, cpad,
):
    row = pl.program_id(0)
    seq, width = tok_ref.shape
    half = q_ref.shape[1]
    length = length_ref[place_ref[0] * pl.num_programs(0) + row]

    @pl.when(row == 0)
    def _():
        clear_edges(xpad)
        clear_edges(cpad)

    spot = lax.broadcasted_iota(jnp.int32, (seq, 1), 0)
    x_f = jnp.where(spot < length, tok_ref[...].astype(F32), 0.0)
    x_in = x_f.astype(BF)
    x_ref[...] = x_in
    fill_padded(xpad, x_f)
    q_ref[...] = dot(x_in, wq_ref[...]).astype(BF)
    k_ref[...] = dot(x_in, wk_ref[...]).astype(BF)
    v_ref[...] = dot(x_in, wv_ref[...]).astype(BF)
    c_ref[...] = dot(x_in, wc_ref[...]).astype(BF)
    fill_padded(cpad, c_ref[...].astype(F32))

    for tile in range(width // LANE):
        for start in range(0, seq, CHUNK):
            total = jnp.zeros((CHUNK, LANE), F32)
            for tap in range(KERN):
                begin = PAD - KERN // 2 + tap + start
                total = total + depth_ref[tap : tap + 1, lanes(tile)] * xpad[tile, begin : begin + CHUNK, :]
            spread_ref[start : start + CHUNK, lanes(tile)] = total.astype(BF)

    span = dot(spread_ref[...], ws_ref[...])
    span_ref[...] = span
    mixed_key = (span * q_ref[...].astype(F32)).astype(BF)
    logits = dot(mixed_key, gen_ref[...])
    lane = lax.broadcasted_iota(jnp.int32, (seq, LANE), 1)
    used = (lane < KERN * 8) & (lane % 8 < HEADS)
    logits = jnp.where(used, logits, -1e30)
    expo = jnp.exp(logits - over_taps(logits, jnp.maximum))
    kern = jnp.where(used, expo / over_taps(expo, jnp.add), 0.0)
    kern_ref[...] = kern
    kern_parts = jnp.concatenate(two_parts(kern), 1)
    for tile in range(TILES):
        for start in range(0, seq, BLOCK):
            wide = dot(
                kern_parts[start : start + BLOCK],
                columns_ref[:, tile * KERN * LANE : (tile + 1) * KERN * LANE],
            )
            total = jnp.zeros((BLOCK, LANE), F32)
            for tap in range(KERN):
                begin = PAD - KERN // 2 + tap + start
                total = total + wide[:, lanes(tap)] * cpad[tile, begin : begin + BLOCK, :]
            mixed_ref[start : start + BLOCK, half + tile * LANE : half + (tile + 1) * LANE] = (
                total.astype(BF)
            )

    masked = jnp.where(spot < length, 0.0, MASKED)
    key_side = pick_lane(lane, [(0, masked)])
    query_side = pick_lane(lane, [(0, 1.0)])
    lse = jnp.zeros((seq, LANE), F32)
    for tile in range(TILES):
        query = jnp.concatenate([q_ref[:, lanes(tile)] * SCALE, query_side], 1)
        result = jnp.zeros((seq, LANE), F32)
        for head in range(2):
            key = jnp.concatenate([head_only(k_ref[:, lanes(tile)], head), key_side], 1)
            value = head_only(v_ref[:, lanes(tile)], head)
            scores = by_transpose(query, key)
            top = jnp.max(scores, 1, keepdims=True)
            expo = jnp.exp(scores - top)
            total = jnp.sum(expo, 1, keepdims=True)
            result = result + dot(expo.astype(BF), value) * (1.0 / total)
            lse = jnp.where(lane == tile * 2 + head, top + jnp.log(total), lse)
        mixed_ref[:, lanes(tile)] = result.astype(BF)
    lse_ref[...] = lse


def normalise(field):
    centred = field - jnp.mean(field, -1, keepdims=True)
    inverse = lax.rsqrt(jnp.mean(centred * centred, -1, keepdims=True) + EPS)
    return centred * inverse, inverse


def normalise_back(grad, unit, inverse):
    return inverse * (
        grad - jnp.mean(grad, -1, keepdims=True) - unit * jnp.mean(grad * unit, -1, keepdims=True)
    )


def gelu_and_slope(field):
    share = 0.5 + 0.5 * lax.erf(field * 0.7071067811865476)
    bell = jnp.exp(field * field * -0.5)
    return field * share, share + field * bell * 0.3989422804014327


def whole(weights_ref, which, group):
    slots, rows, wide = weights_ref.shape
    units = rows // 4
    begin = (which * 2 + group) * units
    return weights_ref[:, begin : begin + units, :].reshape(slots * units, wide)


def put_units(target, which, group, value):
    slots, _, wide = target.shape
    units = value.shape[0] // slots
    begin = (which * 2 + group) * units
    target[:, begin : begin + units, :] = value.reshape(slots, units, wide).astype(target.dtype)


def feed_kernel(
    place_ref, length_ref, mixed_ref, x_ref, cot_ref, wout_ref, own_ref, other_ref, gain1_ref,
    bias1_ref, gain2_ref, bias2_ref, layer_ref, pre_ref, gmixed_ref, keep_ref, give_ref,
    okeep_ref, ogive_ref, vec_ref, gout, spare, activ, ginner, slope, unit_one, normed_s, into, outof,
):
    row = pl.program_id(0)
    seq, width = x_ref.shape
    half = width // 2
    part = activ.shape[1] // 4
    here = pl.ds(pl.multiple_of(row * seq, seq), seq)
    steps = ROW // seq
    length = length_ref[place_ref[0] * (pl.num_programs(0) // steps) + row // steps] - row % steps * seq
    mask = (lax.broadcasted_iota(jnp.int32, (seq, 1), 0) < length).astype(F32)

    @pl.when(row == 0)
    def _():
        gout[...] = jnp.zeros_like(gout)
        vec_ref[...] = jnp.zeros_like(vec_ref)

    unit, inverse_one = normalise(x_ref[...].astype(F32) + dot(mixed_ref[...], wout_ref[...]))
    unit_one[...] = unit
    normed = unit * gain1_ref[...] + bias1_ref[...]
    normed_s[...] = normed
    into[here, :] = normed.astype(BF)
    sums = []
    for group in range(2):
        cols = slice(group * half, (group + 1) * half)
        total = None
        for core, weights_ref in enumerate((own_ref, other_ref)):
            place = slice((group * 2 + core) * part, (group * 2 + core + 1) * part)
            value, rise = gelu_and_slope(
                by_transpose(into[here, cols], whole(weights_ref, 0, group))
            )
            activ[here, place] = value.astype(BF)
            slope[:, place] = rise.astype(BF)
            term = dot(activ[here, place], whole(weights_ref, 1, group))
            total = term if total is None else total + term
        sums.append(total)
    unit, inverse_two = normalise(normed_s[...] + jnp.concatenate(sums, 1))
    layer_ref[...] = ((unit * gain2_ref[...] + bias2_ref[...]) * mask).astype(BF)
    grad = cot_ref[...].astype(F32) * mask
    vec_ref[2:3, :] += jnp.sum(grad * unit, 0, keepdims=True)
    vec_ref[3:4, :] += jnp.sum(grad, 0, keepdims=True)
    grad = normalise_back(grad * gain2_ref[...], unit, inverse_two)
    normed_s[...] = grad
    grad_ffn = grad.astype(BF)
    outof[here, :] = grad_ffn
    sums = []
    for group in range(2):
        cols = slice(group * half, (group + 1) * half)
        total = None
        for core, weights_ref in enumerate((own_ref, other_ref)):
            place = slice((group * 2 + core) * part, (group * 2 + core + 1) * part)
            grad_pre = by_transpose(grad_ffn[:, cols], whole(weights_ref, 1, group))
            grad_pre = (grad_pre * slope[:, place].astype(F32)).astype(BF)
            ginner[here, place] = grad_pre
            term = dot(grad_pre, whole(weights_ref, 0, group))
            total = term if total is None else total + term
        sums.append(total)
    grad = normed_s[...] + jnp.concatenate(sums, 1)
    unit = unit_one[...]
    vec_ref[0:1, :] += jnp.sum(grad * unit, 0, keepdims=True)
    vec_ref[1:2, :] += jnp.sum(grad, 0, keepdims=True)
    grad = normalise_back(grad * gain1_ref[...], unit, inverse_one)
    pre_ref[...] = grad
    grad_mix = grad.astype(BF)
    gout[...] += over_rows(mixed_ref[...], grad_mix)
    gmixed_ref[...] = by_transpose(grad_mix, wout_ref[...]).astype(BF)

    @pl.when(row == pl.num_programs(0) - 1)
    def _():
        rows = width // SLOTS
        columns = slice(0, half), slice(half, width)
        deal(place_ref, [(gout, c, rows) for c in columns], okeep_ref, ogive_ref, spare)
        for group in range(2):
            cols = slice(group * half, (group + 1) * half)
            for core, target in enumerate((keep_ref, give_ref)):
                place = slice((group * 2 + core) * part, (group * 2 + core + 1) * part)
                put_units(target, 0, group, over_rows(ginner[:, place], into[:, cols]))
                put_units(target, 1, group, over_rows(activ[:, place], outof[:, cols]))


def conv_kernel(
    place_ref, length_ref, x_ref, q_ref, c_ref, spread_ref, span_ref, kern_ref, gmixed_ref, ws_ref,
    depth_ref, gen_ref, columns_ref, keep_ref, give_ref, gcv_ref, qconv_ref, xconv_ref, ggen_ref,
    gdepth_ref, cpad, gpad, spad, kpad, products, total, spare,
):
    row = pl.program_id(0)
    seq, width = x_ref.shape
    half = q_ref.shape[1]

    @pl.when(row == 0)
    def _():
        for pad in (cpad, gpad, spad, kpad):
            clear_edges(pad)
        for sums in (total, ggen_ref, gdepth_ref):
            sums[...] = jnp.zeros_like(sums)

    fill_padded(cpad, c_ref[...].astype(F32))
    fill_padded(gpad, gmixed_ref[...].astype(F32))
    kern = kern_ref[...]
    fill_padded(kpad, kern)
    query_f = q_ref[...].astype(F32)
    span = span_ref[...]
    lane = lax.broadcasted_iota(jnp.int32, (seq, LANE), 1)

    for tile in range(TILES):
        for start in range(0, seq, CHUNK):
            grad = gpad[tile, PAD + start : PAD + start + CHUNK, :]
            for tap in range(KERN):
                begin = PAD - KERN // 2 + tap + start
                products[start : start + CHUNK, lanes(tile * KERN + tap)] = (
                    grad * cpad[tile, begin : begin + CHUNK, :]
                ).astype(BF)
    grad_kern = by_transpose(products[...], columns_ref[:LANE, :])
    inner = over_taps(kern * grad_kern, jnp.add)
    grad_logits = (kern * (grad_kern - inner)).astype(BF)
    mixed_key = (span * query_f).astype(BF)
    ggen_ref[...] += over_rows(mixed_key, grad_logits)
    grad_mix = by_transpose(grad_logits, gen_ref[...])
    grad_span = (grad_mix * query_f).astype(BF)
    qconv_ref[...] = grad_mix * span
    total[:, :half] += over_rows(spread_ref[...], grad_span)
    fill_padded(spad, by_transpose(grad_span, ws_ref[...]))

    for tile in range(width // LANE):
        for start in range(0, seq, CHUNK):
            moved_sum = jnp.zeros((CHUNK, LANE), F32)
            field = x_ref[start : start + CHUNK, lanes(tile)].astype(F32)
            for tap in range(KERN):
                begin = PAD + KERN // 2 - tap + start
                grad = spad[tile, begin : begin + CHUNK, :]
                moved = (grad * field).reshape(CHUNK // 8, 8, LANE)
                gdepth_ref[tap, :, lanes(tile)] += jnp.sum(moved, 0)
                moved_sum = moved_sum + depth_ref[tap : tap + 1, lanes(tile)] * grad
            xconv_ref[start : start + CHUNK, lanes(tile)] = moved_sum

    moved = jnp.zeros((seq, LANE), F32)
    for tap in range(KERN):
        begin = PAD + KERN // 2 - tap
        moved = jnp.where(lane // 8 == tap, kpad[0, begin : begin + seq, :], moved)
    kern_parts = jnp.concatenate(two_parts(moved), 1)
    for tile in range(TILES):
        for start in range(0, seq, BLOCK):
            wide = dot(
                kern_parts[start : start + BLOCK],
                columns_ref[:, tile * KERN * LANE : (tile + 1) * KERN * LANE],
            )
            back = jnp.zeros((BLOCK, LANE), F32)
            for tap in range(KERN):
                begin = PAD + KERN // 2 - tap + start
                back = back + wide[:, lanes(tap)] * gpad[tile, begin : begin + BLOCK, :]
            gcv_ref[start : start + BLOCK, lanes(tile)] = back.astype(BF)
    total[:, half:] += over_rows(x_ref[...], gcv_ref[...])

    @pl.when(row == pl.num_programs(0) - 1)
    def _():
        rows = width // SLOTS
        deal(place_ref, [(total, slice(0, half), rows), (total, slice(half, width), rows)], keep_ref, give_ref, spare)


def put_row(target, row, value):
    half = target.shape[1]
    target[row : row + 1, :] = value[:, :half]
    target[row + 1 : row + 2, :] = value[:, half:]


def att_kernel(
    place_ref, length_ref, x_ref, q_ref, k_ref, v_ref, lse_ref, mixed_ref, gmixed_ref, qconv_ref,
    vec_ref, gdepth_ref, ggen_ref, keep_ref, give_ref, grads_ref, turned, total, small, spare,
):
    row = pl.program_id(0)
    seq, width = x_ref.shape
    half = q_ref.shape[1]
    length = length_ref[place_ref[0] * pl.num_programs(0) + row]

    @pl.when(row == 0)
    def _():
        total[...] = jnp.zeros_like(total)

    lane = lax.broadcasted_iota(jnp.int32, (seq, LANE), 1)
    spot = lax.broadcasted_iota(jnp.int32, (seq, 1), 0)
    masked = jnp.where(spot < length, 0.0, MASKED)
    key_side = pick_lane(lane, [(0, masked), (1, 1.0), (2, 1.0), (3, 1.0)])
    value_side = pick_lane(lane, [(0, 1.0), (1, 1.0)])
    for tile in range(TILES):
        query = q_ref[:, lanes(tile)] * SCALE
        grad = gmixed_ref[:, lanes(tile)]
        touch = grad.astype(F32) * mixed_ref[:, lanes(tile)].astype(F32)
        q_sum = jnp.zeros((seq, LANE), F32)
        k_sum = jnp.zeros((seq, LANE), F32)
        v_sum = jnp.zeros((seq, LANE), F32)
        for head in range(2):
            number = tile * 2 + head
            level = -jnp.sum(jnp.where(lane == number, lse_ref[...], 0.0), 1, keepdims=True)
            high = level.astype(BF).astype(F32)
            middle = (level - high).astype(BF).astype(F32)
            query_side = pick_lane(lane, [(0, 1.0), (1, high), (2, middle), (3, level - high - middle)])
            meet = -jnp.sum(head_only(touch, head), 1, keepdims=True)
            high = meet.astype(BF).astype(F32)
            grad_side = pick_lane(lane, [(0, high), (1, meet - high)])
            key_part = head_only(k_ref[:, lanes(tile)], head)
            probs = jnp.exp(
                by_transpose(
                    jnp.concatenate([query, query_side], 1),
                    jnp.concatenate([key_part, key_side], 1),
                )
            )
            grad_probs = by_transpose(
                jnp.concatenate([grad, grad_side], 1),
                jnp.concatenate([head_only(v_ref[:, lanes(tile)], head), value_side], 1),
            )
            grad_scores = (probs * grad_probs).astype(BF)
            q_sum = q_sum + dot(grad_scores, key_part)
            k_sum = k_sum + over_rows(grad_scores, head_only(query, head))
            v_sum = v_sum + over_rows(probs.astype(BF), head_only(grad, head))
        grads_ref[:, lanes(tile)] = (q_sum * SCALE + qconv_ref[:, lanes(tile)]).astype(BF)
        grads_ref[:, half + tile * LANE : half + (tile + 1) * LANE] = k_sum.astype(BF)
        grads_ref[:, 2 * half + tile * LANE : 2 * half + (tile + 1) * LANE] = v_sum.astype(BF)
    turned[...] = x_ref[...].T
    for part in range(3):
        total[part] += dot(turned[...], grads_ref[:, part * half : (part + 1) * half])

    @pl.when(row == pl.num_programs(0) - 1)
    def _():
        rows = width // SLOTS
        query, key, value = [(total.at[part], slice(0, half), rows) for part in range(3)]
        few = (small, slice(0, half), small.shape[0] // SLOTS)
        sources = [query, few, key, value]
        small[...] = jnp.zeros_like(small)
        for index in range(4):
            put_row(small, index * 2, vec_ref[index : index + 1, :])
        for tap in range(KERN):
            put_row(small, 8 + tap * 2, jnp.sum(gdepth_ref[tap], 0, keepdims=True))
        small[GEN_ROW : GEN_ROW + KERN * 8, :] = ggen_ref[...].T[: KERN * 8]
        deal(place_ref, sources, keep_ref, give_ref, spare)


def dx_kernel(
    place_ref, length_ref, grads_ref, gcv_ref, pre_ref, xconv_ref, wq_ref, wk_ref, wv_ref, wc_ref,
    out_ref,
):
    seq, half = gcv_ref.shape
    length = length_ref[place_ref[0] * pl.num_programs(0) + pl.program_id(0)]
    total = xconv_ref[...] + pre_ref[...] + by_transpose(gcv_ref[...], wc_ref[...])
    for index, weight in enumerate((wq_ref, wk_ref, wv_ref)):
        total = total + by_transpose(grads_ref[:, index * half : (index + 1) * half], weight[...])
    spot = lax.broadcasted_iota(jnp.int32, (seq, 1), 0)
    out_ref[...] = jnp.where(spot < length, total, 0.0)


def out_kernel(place_ref, length_ref, own_ref, other_ref, out_ref, part):
    half = own_ref.shape[2]
    rows = own_ref.shape[1] // 2
    for core, part_ref in enumerate((own_ref, other_ref)):
        part[...] = part_ref[...].astype(F32)
        for slot in range(KEPT):
            piece = place_ref[FIRST + core * KEPT + slot]
            here = pl.ds(pl.multiple_of(piece * rows, 8), rows)
            out_ref[here, :half] = part[slot, :rows, :]
            out_ref[here, half:] = part[slot, rows:, :]


def last_kernel(
    place_ref, length_ref, own_ref, other_ref, query_ref, branch_ref, depth_ref, gen_ref, gain1_ref,
    bias1_ref, gain2_ref, bias2_ref, small, part,
):
    width = query_ref.shape[0]
    rows = width // SLOTS
    few = small.shape[0] // SLOTS
    attends = place_ref[0] == 0
    for core, part_ref in enumerate((own_ref, other_ref)):
        part[...] = part_ref[...].astype(F32)
        for slot in range(KEPT):
            piece = place_ref[FIRST + core * KEPT + slot]
            here = pl.ds(pl.multiple_of(piece * rows, 8), rows)

            def rows_at(first, second, size):
                return jnp.where(
                    attends, part[slot, first : first + size, :], part[slot, second : second + size, :]
                )

            query_ref[here, :] = rows_at(0, 2 * rows, rows)
            branch_ref[0, here, :] = rows_at(rows + few, 0, rows)
            branch_ref[1, here, :] = rows_at(2 * rows + few, rows, rows)
            here = pl.ds(pl.multiple_of(piece * few, 8), few)
            small[here, :] = rows_at(rows, 3 * rows, few)

    def wide_row(row):
        return jnp.concatenate([small[row : row + 1, :], small[row + 1 : row + 2, :]], 1)

    for index, vector_ref in enumerate((gain1_ref, bias1_ref, gain2_ref, bias2_ref)):
        vector_ref[...] = wide_row(index * 2).reshape(vector_ref.shape)
    for tap in range(KERN):
        depth_ref[tap : tap + 1, :] = wide_row(8 + tap * 2)
    column = lax.broadcasted_iota(jnp.int32, (gen_ref.shape[0], LANE), 0)
    source = lax.broadcasted_iota(jnp.int32, (gen_ref.shape[0], LANE), 1)
    order = (source == column % KERN * 8 + column // KERN).astype(BF)
    gen_ref[...] = dot(order, small[GEN_ROW : GEN_ROW + LANE, :].astype(BF))


def fixed(shape):
    return pl.BlockSpec(shape, lambda *_: (0,) * len(shape), pipeline_mode=pl.Buffered(1))


def by_row(seq, width):
    return pl.BlockSpec((seq, width), lambda row, *_: (row, 0))


def array(shape, dtype):
    return jax.ShapeDtypeStruct(shape, dtype)


def call(kernel, name, rows, operands, in_specs, outs, out_specs, scratch, flops, moved):
    return pl.pallas_call(
        kernel,
        name=name,
        grid_spec=pltpu.PrefetchScalarGridSpec(
            num_scalar_prefetch=2,
            grid=(rows,),
            in_specs=in_specs,
            out_specs=out_specs,
            scratch_shapes=scratch,
        ),
        out_shape=outs,
        compiler_params=pltpu.CompilerParams(
            dimension_semantics=("arbitrary",), vmem_limit_bytes=FEED_ROOM if kernel is feed_kernel else ROOM
        ),
        cost_estimate=pl.CostEstimate(flops=flops, bytes_accessed=moved, transcendentals=0),
    )(*operands)


def total_of(terms, begin, end):
    return sum(term[begin:end].astype(F32) for term in terms)


def tie(*values):
    return lax.optimization_barrier(values)


def per_device(
    links,
    tokens,
    lengths,
    w_query,
    branch_proj,
    depth_kernel,
    kernel_gen,
    w_out,
    gain_one,
    bias_one,
    w_inner,
    w_outer,
    gain_two,
    bias_two,
    cotangent,
):
    me = links.number()
    core_bit = (me >> 1) & 1
    side = lax.axis_index("branch")
    rows = lengths.shape[0] // 2
    seq = tokens.shape[0] // lengths.shape[0]
    count = rows * seq
    width = tokens.shape[1]
    half = w_query.shape[1]
    groups = w_inner.shape[0]
    units = w_inner.shape[2] * links.count // SLOTS
    hidden = groups * units * SLOTS
    wide = width // groups

    own_w = branch_proj[0]
    far_w = links.send(lax.dynamic_index_in_dim(own_w, core_bit, 0, True), lambda d: d ^ 1)
    other = jnp.stack([2 + core_bit, 3 - core_bit])
    own = jnp.arange(2)
    place = jnp.concatenate(
        [
            side[None],
            jnp.where(side == 0, own, other),
            jnp.where(side == 0, other, own),
            jnp.array(links.slots())[me] & (SLOTS - 1),
        ]
    ).astype(jnp.int32)

    weights = jnp.stack([w_inner, w_outer]).swapaxes(2, 3).reshape((2 * groups, -1, wide))
    weights = links.gather_more(weights).reshape(1, 2 * groups * units, wide)
    weights = links.gather(weights, links.far)
    far_w, weights = tie(far_w, weights)
    near_w = links.core(far_w)

    proj = jnp.concatenate([own_w, far_w, near_w])
    depth_f = jnp.pad(depth_kernel.astype(F32), ((0, 16 - KERN), (0, 0)))
    gen = kernel_gen.reshape(half, HEADS, KERN).swapaxes(1, 2)
    gen = jnp.pad(gen, ((0, 0), (0, 16 - KERN), (0, 8 - HEADS))).reshape(half, LANE)
    columns = jnp.asarray(tap_columns())

    def weight(index):
        return pl.BlockSpec(
            (None, width, half),
            lambda row, where, length: (where[index], 0, 0),
            pipeline_mode=pl.Buffered(1),
        )

    wk, wv, ws, wc = (weight(i) for i in (1, 2, 3, 4))
    wq = fixed((width, half))
    mine = pl.BlockSpec((seq, width), lambda row, where, length: (where[0] * rows + row, 0))
    row_w, row_h, row_l = by_row(seq, width), by_row(seq, half), by_row(seq, LANE)
    row_f = by_row(FEED, width)
    vector, square_w = fixed((1, width)), fixed((width, width))
    tables = [fixed((16, width)), fixed((half, LANE)), fixed(columns.shape)]
    pad_w, pad_h = (pltpu.VMEM((w // LANE, seq + 2 * PAD, LANE), F32) for w in (width, half))
    square = count * seq * half * 2
    project = count * width * half * 2
    norm_one = [gain_one[None], bias_one[None]]
    norm_two = [gain_two[None], bias_two[None]]

    def two_halves(rows_of):
        shape = (KEPT, rows_of, half)
        return [array(shape, F32), array(shape, BF)], [fixed(shape)] * 2, pltpu.VMEM(shape, F32)

    weights = links.gather(weights, links.near)

    x_in, query, key, value, conv_value, spread, span, kern, lse, mixed = call(
        mix_kernel,
        "mix",
        rows,
        [place, lengths, tokens, w_query, proj, proj, proj, proj, depth_f, gen, columns],
        [mine, wq, wk, wv, ws, wc] + tables,
        [
            array((count, width), BF),
            array((count, half), BF),
            array((count, half), BF),
            array((count, half), BF),
            array((count, half), BF),
            array((count, width), BF),
            array((count, half), F32),
            array((count, LANE), F32),
            array((count, LANE), F32),
            array((count, width), BF),
        ],
        [row_w, row_h, row_h, row_h, row_h, row_w, row_h, row_l, row_l, row_w],
        [pad_w, pad_h],
        5 * project + 8 * square,
        16 << 20,
    )
    mixed, weights = tie(mixed, weights)
    other_weights = links.core(weights)
    ffn_rows = 2 * groups * units
    outs, specs, _ = two_halves(ffn_rows)
    out_outs, out_specs, spare = two_halves(width * 2 // SLOTS)
    layer_out, pre_grad, grad_mixed, ffn_keep, ffn_give, out_keep, out_give, vectors = call(
        feed_kernel,
        "feed",
        count // FEED,
        [place, lengths, mixed, x_in, cotangent, w_out, weights, other_weights]
        + norm_one
        + norm_two,
        [row_f, row_f, row_f, square_w] + [fixed((KEPT, ffn_rows, wide))] * 2 + [vector] * 4,
        [array((count, width), BF), array((count, width), F32), array((count, width), BF)]
        + outs
        + out_outs
        + [array((8, width), F32)],
        [row_f, row_f, row_f] + specs + out_specs + [fixed((8, width))],
        [
            pltpu.VMEM((width, width), F32),
            spare,
            pltpu.VMEM((count, hidden), BF),
            pltpu.VMEM((count, hidden), BF),
            pltpu.VMEM((FEED, hidden), BF),
            pltpu.VMEM((FEED, width), F32),
            pltpu.VMEM((FEED, width), F32),
            pltpu.VMEM((count, width), BF),
            pltpu.VMEM((count, width), BF),
        ],
        30 * project,
        32 << 20,
    )
    ffn_more = links.core(ffn_give)
    out_more = links.core(out_give)

    outs, specs, spare = two_halves(width * 2 // SLOTS)
    conv_keep, conv_give, grad_cv, q_conv, x_conv, grad_gen, grad_depth = call(
        conv_kernel,
        "conv",
        rows,
        [place, lengths, x_in, query, conv_value, spread, span, kern, grad_mixed, proj, depth_f]
        + [gen, columns],
        [row_w, row_h, row_h, row_w, row_h, row_l]
        + [pl.BlockSpec((seq, half), lambda row, *_: (row, 1)), ws]
        + tables,
        outs
        + [
            array((count, half), BF),
            array((count, half), F32),
            array((count, width), F32),
            array((half, LANE), F32),
            array((KERN, 8, width), F32),
        ],
        specs + [row_h, row_h, row_w, fixed((half, LANE)), fixed((KERN, 8, width))],
        [
            pad_h,
            pad_h,
            pad_w,
            pltpu.VMEM((1, seq + 2 * PAD, LANE), F32),
            pltpu.VMEM((seq, TILES * KERN * LANE), BF),
            pltpu.VMEM((width, width), F32),
            spare,
        ],
        8 * project,
        16 << 20,
    )
    conv_more = links.core(conv_give)
    ffn_more, out_more, q_conv = tie(ffn_more, out_more, q_conv)
    ffn_terms = [ffn_keep, ffn_more]
    ffn_give = total_of(ffn_terms, KEPT // 2, KEPT).astype(BF)
    out_keep, *out_gives = links.quarters(out_keep + out_more.astype(F32))
    q_conv, ffn_give, out_gives = tie(q_conv, ffn_give, out_gives)
    ffn_terms = [*ffn_terms, links.near(ffn_give, 2)]
    out_mores = [links.near(give, i) for i, give in enumerate(out_gives, 1)]
    outs, specs, spare = two_halves(width * 3 // SLOTS + 8)
    att_keep, att_give, grads = call(
        att_kernel,
        "att",
        rows,
        [place, lengths, x_in, query, key, value, lse, mixed, grad_mixed, q_conv]
        + [vectors, grad_depth, grad_gen],
        [row_w, row_h, row_h, row_h, row_l, row_h, row_h, row_h]
        + [fixed((8, width)), fixed((KERN, 8, width)), fixed((half, LANE))],
        outs + [array((count, 3 * half), BF)],
        specs + [by_row(seq, 3 * half)],
        [
            pltpu.VMEM((width, seq), BF),
            pltpu.VMEM((3, width, half), F32),
            pltpu.VMEM((SLOTS * 8, half), F32),
            spare,
        ],
        3 * project + 20 * square,
        16 << 20,
    )
    att_give, conv_more, ffn_terms, out_mores = tie(att_give, conv_more, ffn_terms, out_mores)
    att_more = links.core(att_give)
    out_sum = out_keep + sum(more.astype(F32) for more in out_mores)
    both_sum = jnp.concatenate(
        [conv_keep + conv_more.astype(F32), att_keep + att_more.astype(F32)], 1
    )
    both_keep, *both_gives = links.quarters(both_sum)
    out_keep, *out_gives = links.quarters(out_sum)
    grads, both_gives, out_gives = tie(grads, both_gives, out_gives)
    both_mores = [links.near(give, i) for i, give in enumerate(both_gives, 1)]
    out_mores = [links.far(give, i) for i, give in enumerate(out_gives, 1)]

    input_grad = call(
        dx_kernel,
        "dx",
        rows,
        [place, lengths, grads, grad_cv, pre_grad, x_conv, w_query, proj, proj, proj],
        [by_row(seq, 3 * half), row_h, row_w, row_w, wq, wk, wv, wc],
        array((count, width), F32),
        row_w,
        [],
        4 * project,
        16 << 20,
    )
    input_grad, both_mores, out_mores = tie(input_grad, both_mores, out_mores)
    out_sum = out_keep + sum(more.astype(F32) for more in out_mores)
    both_sum = both_keep + sum(more.astype(F32) for more in both_mores)
    both_keep, *both_gives = links.quarters(both_sum)
    ffn_give = total_of(ffn_terms, KEPT // 4, KEPT // 2).astype(BF)
    out_piece = links.sum_more(out_sum[0])[None]
    joined = [jnp.concatenate([give, out_piece], 1) for give in both_gives]
    joined, ffn_give = tie(joined, ffn_give)
    joined = [links.far(give, i) for i, give in enumerate(joined, 1)]
    ffn_terms = [*ffn_terms, links.near(ffn_give, 1)]
    joined, ffn_terms = tie(joined, ffn_terms)
    cut = both_keep.shape[1]
    out_own = jnp.concatenate([out_piece] + [more[:, cut:] for more in joined])
    both_sum = both_keep + sum(more[:, :cut].astype(F32) for more in joined)
    both_own = links.gather(links.sum_more(both_sum[0])[None], links.far)
    out_own = links.gather(out_own, links.near)
    both_own, out_own = tie(both_own, out_own)
    chosen = links.send_chosen(both_own, side, core_bit, width * 3 // SLOTS + 8)
    out_other = links.core(out_own)
    chosen[1], ffn_terms = tie(chosen[1], ffn_terms)
    ffn_keep, *ffn_gives = links.quarters(total_of(ffn_terms, 0, KEPT // 4))
    ffn_mores = [links.far(give, i) for i, give in enumerate(ffn_gives, 1)]
    both_own = jnp.concatenate(chosen)
    both_own, out_other, ffn_gives = tie(both_own, out_other, ffn_gives)
    both_other = links.core(both_own)
    out_grad = call(
        out_kernel,
        "place_out",
        1,
        [place, lengths, out_own, out_other],
        [fixed(out_own.shape)] * 2,
        array((width, width), F32),
        square_w,
        [pltpu.VMEM(out_own.shape, F32)],
        0,
        4 << 20,
    )
    grad_query, branch_sum, grad_depth, grad_gen, *vectors = call(
        last_kernel,
        "place",
        1,
        [place, lengths, both_own, both_other],
        [fixed(both_own.shape)] * 2,
        [
            array((width, half), F32),
            array((2, width, half), F32),
            array((KERN, width), F32),
            array(kernel_gen.shape[::-1], F32),
        ]
        + [array((width,), F32)] * 4,
        [wq, fixed((2, width, half)), fixed((KERN, width)), fixed(kernel_gen.shape[::-1])]
        + [fixed((width,))] * 4,
        [pltpu.VMEM((SLOTS * 8, half), F32), pltpu.VMEM(both_own.shape, F32)],
        0,
        8 << 20,
    )
    grad_query, ffn_mores = tie(grad_query, ffn_mores)
    ffn_sum = (ffn_keep + sum(more.astype(F32) for more in ffn_mores))[0]
    ffn_grads = links.scatter_more(ffn_sum.reshape(2 * groups, units, wide))
    ffn_grads = ffn_grads.swapaxes(1, 2).reshape((2,) + w_inner.shape)
    grad_gain_one, grad_bias_one, grad_gain_two, grad_bias_two = vectors
    return (
        layer_out,
        input_grad,
        grad_query,
        branch_sum[None],
        grad_depth,
        grad_gen.T,
        out_grad,
        grad_gain_one,
        grad_bias_one,
        ffn_grads[0],
        ffn_grads[1],
        grad_gain_two,
        grad_bias_two,
    )


def solution(mesh):
    rows = P(AXES, None)
    hidden = P(None, None, AXES)
    weights = P("branch", None, None, None)
    return jax.shard_map(
        partial(per_device, Links(mesh)),
        mesh=mesh,
        in_specs=(
            P("dp", None), P("dp"), P(), weights, P(), P(), P(), P(), P(), hidden, hidden,
            P(), P(), rows,
        ),
        out_specs=(
            rows, rows, P(), weights, P(), P(), P(), P(), P(), hidden, hidden, P(), P(),
        ),
        check_vma=False,
    )
```
